32 devices in a mesh: groups: 1, seq: 32 (over z, y, x, core).
Axes of the slice: x: 2, y: 2, z: 4, core: 2. Of those that a mesh axis runs over, the one named last changes fastest.
Arguments:
- features: bfloat16 [2, 4096, 1536], P('groups', 'seq'), may hold values from -6 to 6
- cotangent: bfloat16 [2, 4096, 1536], P('groups', 'seq'), may hold values from -6 to 6
- dilated_kernel_weight: bfloat16 [1536, 3, 768], P('seq'), may hold values from -0.09375 to 0.09375
- project_weight: bfloat16 [1536, 768], P('seq'), may hold values from -0.21875 to 0.21875
- outer_gain: float32 [1536], replicated, may hold values from 0.1 to 1.9
- inner_gain: float32 [768], replicated, may hold values from 0.1 to 1.9
Outputs:
- block_out: bfloat16 [2, 4096, 1536], P('groups', 'seq')
- grad_features: bfloat16 [2, 4096, 1536], P('groups', 'seq')
- grad_dilated: float32 [1536, 3, 768], P(('groups', 'seq'))
- grad_project: float32 [1536, 768], P(('groups', 'seq'))
- grad_outer_gain: float32 [1536], P(('groups', 'seq'))
- grad_inner_gain: float32 [768], P(('groups', 'seq'))
The draws below stay inside these ranges and needn't reach their ends.
All inputs are finite; a program needn't handle non-finite values.
Results may differ from the reference program's by a relative error of at most 0.0056.
Values may be sent and summed in bfloat16 or wider, within the bound.
No kernel may reach another device: no remote copies, remote signals or barrier semaphores. Data moves between devices by JAX's collectives and lax.ppermute only.
A program may use at most 128 MiB of HBM per device.

```python
import math
import jax
import jax.numpy as jnp
from jax import lax

C = 1536
INNER = 768
KERNEL_TAPS = 3
DILATION_STEP = 32
MB = 2
BINS = 4096


def with_spikes(values, own_key, source, target, blocks, factor):
    owner, partner = [(jnp.arange(values.shape[axis_at]) // (values.shape[axis_at] // blocks)).reshape([-1 if axis == axis_at else 1 for axis in range(values.ndim)]) for axis_at in (source, target)]
    chosen = jax.random.permutation(own_key, blocks)[partner]
    strong = (owner == chosen) | (owner == (partner + blocks // 2) % blocks)
    return jnp.where(strong, factor * values, values)


def shard_levels(rng, dims, split, smallest, largest):
    level = 1.0
    for axis_at, parts in split:
        draws = jax.random.uniform(jax.random.fold_in(jax.random.fold_in(rng, 6), axis_at), (parts,), jnp.float32, smallest / len(split), largest / len(split))
        level = level * jnp.repeat(jnp.exp(draws), dims[axis_at] // parts).reshape((-1,) + (1,) * (len(dims) - 1 - axis_at))
    return level


def gaussian(stream_key, extent, deviation, most, split=(), kind=jnp.bfloat16):
    level = shard_levels(stream_key, extent, split, -0.22, 0.18) if split else 1.0
    array = jax.random.normal(stream_key, extent, jnp.float32) * deviation * level
    return jnp.minimum(jnp.maximum(array, -most), most).astype(kind)


def bell_draw_with(key, shape, scale, most, cuts, heavy, held_as=jnp.bfloat16):
    drawn = scale * jax.random.normal(key, shape, jnp.float32)
    if cuts:
        drawn = drawn * shard_levels(key, shape, cuts, -0.22, 0.18)
    return jnp.clip(with_spikes(drawn, jax.random.fold_in(key, 3), *heavy), -most, most).astype(held_as)


def setup_inputs(seed: int = 0, part: int = 0) -> dict:
    key_of = jax.random.split(jax.random.key(seed), 7)
    part_keys = jax.random.split(jax.random.fold_in(key_of[6], part), 7)
    features = gaussian(part_keys[0], (MB, BINS, C), 1.0, 6.0, ((1, 32),))
    cotangent = bell_draw_with(part_keys[1], (MB, BINS, C), 1.0, 6.0, ((1, 32),), (1, 2, 32, 2.75))
    dilated_kernel_weight = gaussian(key_of[2], (C, KERNEL_TAPS, INNER), (KERNEL_TAPS * C) ** -0.5, 0.09375, ((0, 32),))
    project_weight = gaussian(key_of[3], (C, INNER), INNER ** -0.5, 0.21875, ((0, 32),))
    outer_gain = jnp.clip(1.0 + 0.18 * jax.random.normal(key_of[4], (C,), jnp.float32), 0.1, 1.9)
    inner_gain = jnp.clip(1.0 + 0.18 * jax.random.normal(key_of[5], (INNER,), jnp.float32), 0.1, 1.9)
    return dict(features=features, cotangent=cotangent, dilated_kernel_weight=dilated_kernel_weight, project_weight=project_weight, outer_gain=outer_gain, inner_gain=inner_gain)


eps = 1e-06

def act_norm(values, gain):
    meansq = lax.optimization_barrier(jnp.mean(values * values, axis=-1, keepdims=True))
    return jax.nn.gelu(values * lax.rsqrt(meansq + eps) * gain, approximate=True)

def reference(features, cotangent, dilated_kernel_weight, project_weight, outer_gain, inner_gain):
    bin_count = features.shape[1]
    border_rows = DILATION_STEP * (KERNEL_TAPS // 2)
    factor = 1.0 / math.sqrt(MB * BINS)

    def one_seq(loop_carry, pair):
        dilated_accumulator, projection_accumulator, outer_accumulator, inner_accumulator = loop_carry
        seq_in, seq_cot = pair
        as_float = seq_in.astype(jnp.float32)
        active_features = act_norm(as_float, outer_gain).astype(jnp.bfloat16)
        zero_rows = jnp.zeros((border_rows, C), jnp.bfloat16)
        padded_input = jnp.concatenate([zero_rows, active_features, zero_rows], 0)
        conv_output = jnp.zeros((bin_count, INNER), jnp.float32)
        for tap_index in range(KERNEL_TAPS):
            conv_output = conv_output + jnp.dot(padded_input[tap_index * DILATION_STEP:tap_index * DILATION_STEP + bin_count], dilated_kernel_weight[:, tap_index, :], preferred_element_type=jnp.float32)
        hidden = act_norm(conv_output, inner_gain).astype(jnp.bfloat16)
        sequence_output = (as_float + jnp.dot(hidden, project_weight.T, preferred_element_type=jnp.float32)).astype(jnp.bfloat16)
        grad_hidden = jnp.dot(seq_cot, project_weight, preferred_element_type=jnp.float32)
        unused, pull_inner = jax.vjp(act_norm, conv_output, inner_gain)
        conv_output_gradient, grad_gain_inner = pull_inner(grad_hidden)
        conv_output_gradient = conv_output_gradient.astype(jnp.bfloat16)
        zero_inner = jnp.zeros((border_rows, INNER), jnp.bfloat16)
        padded_input_gradient = jnp.concatenate([zero_inner, conv_output_gradient, zero_inner], 0)
        grad_active = jnp.zeros((bin_count, C), jnp.float32)
        for tap_index in range(KERNEL_TAPS):
            tap_shift = (KERNEL_TAPS - 1 - tap_index) * DILATION_STEP
            grad_active = grad_active + jnp.dot(padded_input_gradient[tap_shift:tap_shift + bin_count], dilated_kernel_weight[:, tap_index, :].T, preferred_element_type=jnp.float32)
        unused_two, pull_outer = jax.vjp(act_norm, as_float, outer_gain)
        grad_branch, grad_gain_outer = pull_outer(grad_active)
        sequence_input_gradient = (seq_cot.astype(jnp.float32) + grad_branch).astype(jnp.bfloat16)
        tap_slices = [jnp.dot(padded_input[tap_index * DILATION_STEP:tap_index * DILATION_STEP + bin_count].T, conv_output_gradient, preferred_element_type=jnp.float32) for tap_index in range(KERNEL_TAPS)]
        dilated_accumulator = dilated_accumulator + jnp.stack(tap_slices, axis=1)
        projection_accumulator = projection_accumulator + jnp.dot(seq_cot.T, hidden, preferred_element_type=jnp.float32)
        outer_accumulator = outer_accumulator + grad_gain_outer
        inner_accumulator = inner_accumulator + grad_gain_inner
        return ((dilated_accumulator, projection_accumulator, outer_accumulator, inner_accumulator), (sequence_output, sequence_input_gradient))
    start = (jnp.zeros((C, KERNEL_TAPS, INNER), jnp.float32), jnp.zeros((C, INNER), jnp.float32), jnp.zeros((C,), jnp.float32), jnp.zeros((INNER,), jnp.float32))
    totals, stacked = lax.scan(one_seq, start, (features, cotangent))
    block_out, grad_features = stacked
    return (block_out, grad_features, totals[0] * factor, totals[1] * factor, totals[2] * factor, totals[3] * factor)
```

```python
import math

import jax
import jax.numpy as jnp
from jax import lax
from jax.experimental import pallas as pl
from jax.experimental.pallas import tpu as pltpu
from jax.sharding import PartitionSpec as P

KERNEL_TAPS = 3
DILATION_STEP = 32
TORUS_DEVICES = 32


eps = 1e-06


def padded(block, sides, width):
    for axis, dim in sides:
        count = lax.axis_size(axis)
        forward = [(i, i + 1) for i in range(count - 1)]
        backward = [(target, source) for source, target in forward]
        low = lax.ppermute(
            lax.slice_in_dim(block, block.shape[dim] - width, None, axis=dim), axis, forward
        )
        high = lax.ppermute(lax.slice_in_dim(block, 0, width, axis=dim), axis, backward)
        block = jnp.concatenate([low, block, high], axis=dim)
    return block


def act_norm(values, gain):
    meansq = jnp.mean(values * values, axis=-1, keepdims=True)
    return jax.nn.gelu(values * lax.rsqrt(meansq + eps) * gain, approximate=True)


def reduce_dilated(padded_input, conv_output_gradient, factor):
    bin_count = conv_output_gradient.shape[1]
    tap_slices = [
        jnp.einsum(
            "btc,bti->ci",
            padded_input[:, tap_index * DILATION_STEP : tap_index * DILATION_STEP + bin_count],
            conv_output_gradient,
            preferred_element_type=jnp.float32,
        )
        for tap_index in range(KERNEL_TAPS)
    ]
    return lax.psum_scatter(
        jnp.stack(tap_slices, axis=1) * factor, "seq", scatter_dimension=0, tiled=True
    )


def body_any(features, cotangent, dilated_kernel_weight, project_weight, outer_gain, inner_gain):
    bin_count = features.shape[1]
    factor = 1.0 / math.sqrt(features.shape[0] * bin_count * lax.axis_size("seq"))
    full_dilated = lax.all_gather(dilated_kernel_weight, "seq", axis=0, tiled=True)
    full_project = lax.all_gather(project_weight, "seq", axis=0, tiled=True)
    as_float = features.astype(jnp.float32)
    active_features = act_norm(as_float, outer_gain).astype(jnp.bfloat16)
    padded_input = padded(active_features, (("seq", 1),), DILATION_STEP)
    conv_output = jnp.einsum(
        "btc,ci->bti",
        padded_input[:, 0:bin_count],
        full_dilated[:, 0, :],
        preferred_element_type=jnp.float32,
    )
    for tap_index in range(1, KERNEL_TAPS):
        conv_output = conv_output + jnp.einsum(
            "btc,ci->bti",
            padded_input[:, tap_index * DILATION_STEP : tap_index * DILATION_STEP + bin_count],
            full_dilated[:, tap_index, :],
            preferred_element_type=jnp.float32,
        )
    hidden = act_norm(conv_output, inner_gain).astype(jnp.bfloat16)
    block_out = (
        as_float
        + jnp.einsum("bti,ci->btc", hidden, full_project, preferred_element_type=jnp.float32)
    ).astype(jnp.bfloat16)
    grad_hidden = jnp.einsum(
        "btc,ci->bti", cotangent, full_project, preferred_element_type=jnp.float32
    )
    unused, pull_inner = jax.vjp(act_norm, conv_output, inner_gain)
    conv_output_gradient, grad_gain_inner = pull_inner(grad_hidden)
    conv_output_gradient = conv_output_gradient.astype(jnp.bfloat16)
    padded_input_gradient = padded(conv_output_gradient, (("seq", 1),), DILATION_STEP)
    grad_active = jnp.zeros(features.shape, jnp.float32)
    for tap_index in range(KERNEL_TAPS):
        tap_shift = (KERNEL_TAPS - 1 - tap_index) * DILATION_STEP
        grad_active = grad_active + jnp.einsum(
            "bti,ci->btc",
            padded_input_gradient[:, tap_shift : tap_shift + bin_count],
            full_dilated[:, tap_index, :],
            preferred_element_type=jnp.float32,
        )
    unused_two, pull_outer = jax.vjp(act_norm, as_float, outer_gain)
    grad_branch, grad_gain_outer = pull_outer(grad_active)
    grad_features = (cotangent.astype(jnp.float32) + grad_branch).astype(jnp.bfloat16)
    grad_dilated = reduce_dilated(padded_input, conv_output_gradient, factor)
    grad_project = lax.psum_scatter(
        jnp.einsum("btc,bti->ci", cotangent, hidden, preferred_element_type=jnp.float32) * factor,
        "seq",
        scatter_dimension=0,
        tiled=True,
    )
    grad_outer_gain, grad_inner_gain = (
        lax.psum_scatter(grad_gain_outer * factor, "seq", scatter_dimension=0, tiled=True),
        lax.psum_scatter(grad_gain_inner * factor, "seq", scatter_dimension=0, tiled=True),
    )
    return (block_out, grad_features, grad_dilated, grad_project, grad_outer_gain, grad_inner_gain)


def links(move):
    return [(i, move(i)) for i in range(TORUS_DEVICES)]


CORE = links(lambda i: i ^ 1)
FIRST = links(lambda i: i ^ (4 if i & 1 else 2))
SECOND = links(lambda i: i ^ (2 if i & 1 else 4))
UP = links(lambda i: (i + 8) % TORUS_DEVICES)
DOWN = links(lambda i: (i - 8) % TORUS_DEVICES)


def send(block, pairs):
    return lax.ppermute(block, "seq", pairs)


def cat(*parts):
    return jnp.concatenate(parts, axis=0)


def gather_z(block):
    half = block.shape[0] // 2
    below = send(block, UP)
    above = send(block, DOWN)
    far_low = send(below[:half], UP)
    far_high = send(above[half:], DOWN)
    return cat(block, above, far_low, far_high, below)


def scatter_z(total):
    n = total.shape[0] // 4
    half = n // 2
    message = total[2 * n : 3 * n].astype(jnp.bfloat16)
    low = send(message[:half], UP).astype(jnp.float32)
    high = send(message[half:], DOWN).astype(jnp.float32)
    to_up = cat(total[n : n + half] + low, total[n + half : 2 * n]).astype(jnp.bfloat16)
    to_down = cat(total[3 * n : 3 * n + half], total[3 * n + half :] + high).astype(jnp.bfloat16)
    from_below = send(to_up, UP).astype(jnp.float32)
    from_above = send(to_down, DOWN).astype(jnp.float32)
    return total[:n] + from_below + from_above


def scatter_pair(total, pairs):
    n = total.shape[0] // 2
    return total[:n] + send(total[n:].astype(jnp.bfloat16), pairs).astype(jnp.float32)


def block_orders():
    both = [(m, r2, r1, k) for r2 in (0, 1) for r1 in (0, 1) for k in range(4) for m in (0, 1)]
    last = [(2, r2, r1, k) for r2 in (0, 1) for k in range(4) for r1 in (0, 1)]
    proj = [(3, r2, r1, k) for k in range(4) for r2 in (0, 1) for r1 in (0, 1)]
    return both + last + proj


def order_kernel(index_ref, source_ref, own_ref, other_ref):
    device = index_ref[0]
    core = device & 1
    x = (device >> 1) & 1
    y = (device >> 2) & 1
    z = device >> 3
    for at, (matrix, r2, r1, k) in enumerate(block_orders()):
        zk = (z + k) & 3
        for target, parity in ((own_ref, core), (other_ref, 1 - core)):
            dx = r1 + parity * (r2 - r1)
            dy = r2 + parity * (r1 - r2)
            block = zk * 8 + (y ^ dy) * 4 + (x ^ dx) * 2 + parity
            target[at] = source_ref[matrix, block]


def in_arrival_order(source):
    shape = jax.ShapeDtypeStruct((64,) + source.shape[2:], source.dtype)
    index = lax.axis_index("seq").astype(jnp.int32).reshape(1)
    return pl.pallas_call(
        order_kernel,
        out_shape=(shape, shape),
        in_specs=[
            pl.BlockSpec(memory_space=pltpu.SMEM),
            pl.BlockSpec(memory_space=pltpu.VMEM),
        ],
        out_specs=[
            pl.BlockSpec(memory_space=pltpu.VMEM),
            pl.BlockSpec(memory_space=pltpu.VMEM),
        ],
        compiler_params=pltpu.CompilerParams(vmem_limit_bytes=32 << 20),
        name="order",
    )(index, source)


def natural_kernel(index_ref, own0, other0, own2, other2, own3, other3, *rest):
    targets, sems = rest[:4], rest[4]
    device = index_ref[0]
    core = device & 1
    x = (device >> 1) & 1
    y = (device >> 2) & 1
    z = device >> 3
    copies = []
    for at, (matrix, r2, r1, k) in enumerate(block_orders()):
        zk = (z + k) & 3
        if at < 32:
            pair, local = (own0, other0), at
        elif at < 48:
            pair, local = (own2, other2), at - 32
        else:
            pair, local = (own3, other3), at - 48
        for side, (source, parity) in enumerate(zip(pair, (core, 1 - core))):
            dx = r1 + parity * (r2 - r1)
            dy = r2 + parity * (r1 - r2)
            block = zk * 8 + (y ^ dy) * 4 + (x ^ dx) * 2 + parity
            copies.append(
                pltpu.make_async_copy(
                    source.at[local], targets[matrix].at[block], sems.at[2 * at + side]
                )
            )
    for copy in copies:
        copy.start()
    for copy in copies:
        copy.wait()


def in_natural_order(own0, other0, own2, other2, own3, other3):
    rows, inner = own0.shape[1:]
    shape = jax.ShapeDtypeStruct((32, rows, inner), own0.dtype)
    index = lax.axis_index("seq").astype(jnp.int32).reshape(1)
    whole = pl.pallas_call(
        natural_kernel,
        out_shape=(shape,) * 4,
        in_specs=[pl.BlockSpec(memory_space=pltpu.SMEM)]
        + [pl.BlockSpec(memory_space=pl.ANY)] * 6,
        out_specs=[pl.BlockSpec(memory_space=pl.ANY)] * 4,
        scratch_shapes=[pltpu.SemaphoreType.DMA((128,))],
        name="natural",
    )(index, own0, other0, own2, other2, own3, other3)
    return [array.reshape(32 * rows, inner) for array in whole]


def rows_dot(left, right):
    return jnp.einsum("nrt,ti->nri", left, right, preferred_element_type=jnp.float32)


def contract(left, right):
    n, rows, tokens = left.shape
    return jnp.einsum(
        "ct,ci->ti",
        left.reshape(n * rows, tokens),
        right.reshape(n * rows, right.shape[2]),
        preferred_element_type=jnp.float32,
    )


def body_torus(features, cotangent, dilated_kernel_weight, project_weight, outer_gain, inner_gain):
    batch, bin_count, channels = features.shape
    inner = project_weight.shape[1]
    rows = project_weight.shape[0]
    tokens = batch * bin_count
    factor = 1.0 / math.sqrt(tokens * TORUS_DEVICES)

    taps01 = jnp.stack([dilated_kernel_weight[:, 0, :], dilated_kernel_weight[:, 1, :]])
    tail = jnp.stack([dilated_kernel_weight[:, 2, :], project_weight])
    tail_first = send(tail, FIRST)
    plane0 = gather_z(taps01)
    tap2 = cat(tail[:1], tail_first[:1])
    proj = cat(tail[1:], tail_first[1:])
    proj = cat(proj, send(proj, SECOND))
    near2 = gather_z(tap2)
    near0 = cat(plane0, send(plane0, FIRST))
    far0 = send(near0, SECOND)
    far2 = send(near2, SECOND)
    own3 = gather_z(proj)
    own0 = cat(near0, far0)
    own2 = cat(near2, far2)
    other0 = cat(send(near0, CORE), send(far0, CORE))
    other2 = cat(send(near2, CORE), send(far2, CORE))
    other3 = send(own3, CORE)

    features_padded = padded(features, (("seq", 1),), DILATION_STEP)
    active = act_norm(features_padded.astype(jnp.float32), outer_gain).astype(jnp.bfloat16)
    turned = [
        active[:, tap * DILATION_STEP : tap * DILATION_STEP + bin_count]
        .reshape(tokens, channels)
        .T.reshape(32, rows, tokens)
        for tap in range(KERNEL_TAPS)
    ]
    turned.append(cotangent.reshape(tokens, channels).T.reshape(32, rows, tokens))
    act_own, act_other = in_arrival_order(jnp.stack(turned))

    conv_output = (
        contract(act_own[:32], own0)
        + contract(act_other[:32], other0)
        + contract(act_own[32:48], own2)
        + contract(act_other[32:48], other2)
    )
    hidden32, pull_inner = jax.vjp(act_norm, conv_output, inner_gain)
    hidden = hidden32.astype(jnp.bfloat16)

    keep3 = rows_dot(act_own[48:], hidden)
    give3 = rows_dot(act_other[48:], hidden).astype(jnp.bfloat16)
    sum3 = keep3 + send(give3, CORE).astype(jnp.float32)
    sum3 = scatter_z(sum3)
    sum3 = scatter_pair(sum3, SECOND)
    sum3 = scatter_pair(sum3, FIRST)
    grad_project = sum3[0] * factor

    grad_hidden = contract(act_own[48:], own3) + contract(act_other[48:], other3)
    grad_conv, grad_gain_inner = pull_inner(grad_hidden)
    grad_conv = grad_conv.astype(jnp.bfloat16)

    keep0 = rows_dot(act_own[:32], grad_conv)
    give0 = rows_dot(act_other[:32], grad_conv).astype(jnp.bfloat16)
    keep2 = rows_dot(act_own[32:48], grad_conv)
    give2 = rows_dot(act_other[32:48], grad_conv).astype(jnp.bfloat16)
    sum0 = keep0 + send(give0, CORE).astype(jnp.float32)
    sum2 = keep2 + send(give2, CORE).astype(jnp.float32)
    sum2 = scatter_pair(sum2, SECOND)
    sum0 = scatter_pair(sum0, SECOND)
    sum2 = scatter_z(sum2)
    sum0 = scatter_pair(sum0, FIRST)
    sum2 = scatter_pair(sum2, FIRST)
    sum0 = scatter_z(sum0)
    grad_dilated = jnp.stack([sum0[0], sum0[1], sum2[0]], axis=1) * factor

    weights = in_natural_order(own0, other0, own2, other2, own3, other3)
    block_out = (
        features.astype(jnp.float32)
        + jnp.einsum(
            "bti,ci->btc",
            hidden.reshape(batch, bin_count, inner),
            weights[3],
            preferred_element_type=jnp.float32,
        )
    ).astype(jnp.bfloat16)
    grad_padded = padded(
        grad_conv.reshape(batch, bin_count, inner), (("seq", 1),), DILATION_STEP
    )
    grad_active = jnp.zeros(features.shape, jnp.float32)
    for tap in range(KERNEL_TAPS):
        shift = (KERNEL_TAPS - 1 - tap) * DILATION_STEP
        grad_active = grad_active + jnp.einsum(
            "bti,ci->btc",
            grad_padded[:, shift : shift + bin_count],
            weights[tap],
            preferred_element_type=jnp.float32,
        )
    unused, pull_outer = jax.vjp(act_norm, features.astype(jnp.float32), outer_gain)
    grad_branch, grad_gain_outer = pull_outer(grad_active)
    grad_features = (cotangent.astype(jnp.float32) + grad_branch).astype(jnp.bfloat16)

    gains = jnp.concatenate([grad_gain_outer, grad_gain_inner]) * factor
    for distance in (1, 2, 4, 8, 16):
        gains = gains + send(gains, links(lambda i: i ^ distance))
    device = lax.axis_index("seq")
    grad_outer_gain = lax.dynamic_slice(gains, (device * rows,), (rows,))
    part = inner // TORUS_DEVICES
    grad_inner_gain = lax.dynamic_slice(gains, (channels + device * part,), (part,))
    return (block_out, grad_features, grad_dilated, grad_project, grad_outer_gain, grad_inner_gain)


def body(*operands):
    if lax.axis_size("seq") == TORUS_DEVICES:
        return body_torus(*operands)
    return body_any(*operands)


def solution(mesh):
    return jax.shard_map(
        body,
        mesh=mesh,
        in_specs=(
            P("groups", "seq", None),
            P("groups", "seq", None),
            P("seq", None, None),
            P("seq", None),
            P(),
            P(),
        ),
        out_specs=(
            P("groups", "seq", None),
            P("groups", "seq", None),
            P(("groups", "seq"), None, None),
            P(("groups", "seq"), None),
            P(("groups", "seq")),
            P(("groups", "seq")),
        ),
        check_vma=False,
    )
```

```python
import math

import jax
import jax.numpy as jnp
from jax import lax
from jax.experimental import pallas as pl
from jax.experimental.pallas import tpu as pltpu
from jax.sharding import PartitionSpec as P

KERNEL_TAPS = 3
DILATION_STEP = 32
TORUS_DEVICES = 32


eps = 1e-06


def padded(block, sides, width):
    for axis, dim in sides:
        count = lax.axis_size(axis)
        forward = [(i, i + 1) for i in range(count - 1)]
        backward = [(target, source) for source, target in forward]
        low = lax.ppermute(
            lax.slice_in_dim(block, block.shape[dim] - width, None, axis=dim), axis, forward
        )
        high = lax.ppermute(lax.slice_in_dim(block, 0, width, axis=dim), axis, backward)
        block = jnp.concatenate([low, block, high], axis=dim)
    return block


def act_norm(values, gain):
    meansq = jnp.mean(values * values, axis=-1, keepdims=True)
    return jax.nn.gelu(values * lax.rsqrt(meansq + eps) * gain, approximate=True)


def reduce_dilated(padded_input, conv_output_gradient, factor):
    bin_count = conv_output_gradient.shape[1]
    tap_slices = [
        jnp.einsum(
            "btc,bti->ci",
            padded_input[:, tap_index * DILATION_STEP : tap_index * DILATION_STEP + bin_count],
            conv_output_gradient,
            preferred_element_type=jnp.float32,
        )
        for tap_index in range(KERNEL_TAPS)
    ]
    return lax.psum_scatter(
        jnp.stack(tap_slices, axis=1) * factor, "seq", scatter_dimension=0, tiled=True
    )


def body_any(features, cotangent, dilated_kernel_weight, project_weight, outer_gain, inner_gain):
    bin_count = features.shape[1]
    factor = 1.0 / math.sqrt(features.shape[0] * bin_count * lax.axis_size("seq"))
    full_dilated = lax.all_gather(dilated_kernel_weight, "seq", axis=0, tiled=True)
    full_project = lax.all_gather(project_weight, "seq", axis=0, tiled=True)
    as_float = features.astype(jnp.float32)
    active_features = act_norm(as_float, outer_gain).astype(jnp.bfloat16)
    padded_input = padded(active_features, (("seq", 1),), DILATION_STEP)
    conv_output = jnp.einsum(
        "btc,ci->bti",
        padded_input[:, 0:bin_count],
        full_dilated[:, 0, :],
        preferred_element_type=jnp.float32,
    )
    for tap_index in range(1, KERNEL_TAPS):
        conv_output = conv_output + jnp.einsum(
            "btc,ci->bti",
            padded_input[:, tap_index * DILATION_STEP : tap_index * DILATION_STEP + bin_count],
            full_dilated[:, tap_index, :],
            preferred_element_type=jnp.float32,
        )
    hidden = act_norm(conv_output, inner_gain).astype(jnp.bfloat16)
    block_out = (
        as_float
        + jnp.einsum("bti,ci->btc", hidden, full_project, preferred_element_type=jnp.float32)
    ).astype(jnp.bfloat16)
    grad_hidden = jnp.einsum(
        "btc,ci->bti", cotangent, full_project, preferred_element_type=jnp.float32
    )
    unused, pull_inner = jax.vjp(act_norm, conv_output, inner_gain)
    conv_output_gradient, grad_gain_inner = pull_inner(grad_hidden)
    conv_output_gradient = conv_output_gradient.astype(jnp.bfloat16)
    padded_input_gradient = padded(conv_output_gradient, (("seq", 1),), DILATION_STEP)
    grad_active = jnp.zeros(features.shape, jnp.float32)
    for tap_index in range(KERNEL_TAPS):
        tap_shift = (KERNEL_TAPS - 1 - tap_index) * DILATION_STEP
        grad_active = grad_active + jnp.einsum(
            "bti,ci->btc",
            padded_input_gradient[:, tap_shift : tap_shift + bin_count],
            full_dilated[:, tap_index, :],
            preferred_element_type=jnp.float32,
        )
    unused_two, pull_outer = jax.vjp(act_norm, as_float, outer_gain)
    grad_branch, grad_gain_outer = pull_outer(grad_active)
    grad_features = (cotangent.astype(jnp.float32) + grad_branch).astype(jnp.bfloat16)
    grad_dilated = reduce_dilated(padded_input, conv_output_gradient, factor)
    grad_project = lax.psum_scatter(
        jnp.einsum("btc,bti->ci", cotangent, hidden, preferred_element_type=jnp.float32) * factor,
        "seq",
        scatter_dimension=0,
        tiled=True,
    )
    grad_outer_gain, grad_inner_gain = (
        lax.psum_scatter(grad_gain_outer * factor, "seq", scatter_dimension=0, tiled=True),
        lax.psum_scatter(grad_gain_inner * factor, "seq", scatter_dimension=0, tiled=True),
    )
    return (block_out, grad_features, grad_dilated, grad_project, grad_outer_gain, grad_inner_gain)


def links(move):
    return [(i, move(i)) for i in range(TORUS_DEVICES)]


CORE = links(lambda i: i ^ 1)
FIRST = links(lambda i: i ^ (4 if i & 1 else 2))
SECOND = links(lambda i: i ^ (2 if i & 1 else 4))
UP = links(lambda i: (i + 8) % TORUS_DEVICES)
DOWN = links(lambda i: (i - 8) % TORUS_DEVICES)
ACROSS = links(lambda i: (i + 16) % TORUS_DEVICES)


def send(block, pairs):
    return lax.ppermute(block, "seq", pairs)


def cat(*parts):
    return jnp.concatenate(parts, axis=0)


def gather_z(block):
    return cat(block, send(block, DOWN), send(block, ACROSS), send(block, UP))


def scatter_z(total):
    n = total.shape[0] // 4
    message = total[n:].astype(jnp.bfloat16)
    up = send(message[:n], UP).astype(jnp.float32)
    across = send(message[n : 2 * n], ACROSS).astype(jnp.float32)
    down = send(message[2 * n :], DOWN).astype(jnp.float32)
    return total[:n] + up + across + down


def scatter_pair(total, pairs):
    n = total.shape[0] // 2
    return total[:n] + send(total[n:].astype(jnp.bfloat16), pairs).astype(jnp.float32)


TAP_ORDER = [
    (tap, r2, r1, k) for r2 in (0, 1) for r1 in (0, 1) for k in range(4) for tap in range(3)
]
PROJECT_ORDER = [(3, r2, r1, k) for k in range(4) for r2 in (0, 1) for r1 in (0, 1)]


def placing(device):
    core = device & 1
    x = (device >> 1) & 1
    y = (device >> 2) & 1
    z = device >> 3

    def block_of(r2, r1, k, other):
        parity = 1 - core if other else core
        dx = r1 + parity * (r2 - r1)
        dy = r2 + parity * (r1 - r2)
        return ((z + k) & 3) * 8 + (y ^ dy) * 4 + (x ^ dx) * 2 + parity

    return block_of


def device_index():
    return lax.axis_index("seq").astype(jnp.int32).reshape(1)


def order_kernel(index_ref, source_ref, own_ref, other_ref):
    block_of = placing(index_ref[0])
    for at, (matrix, r2, r1, k) in enumerate(TAP_ORDER + PROJECT_ORDER):
        own_ref[at] = source_ref[matrix, block_of(r2, r1, k, False)]
        other_ref[at] = source_ref[matrix, block_of(r2, r1, k, True)]


def in_arrival_order(source):
    shape = jax.ShapeDtypeStruct((64,) + source.shape[2:], source.dtype)
    return pl.pallas_call(
        order_kernel,
        out_shape=(shape, shape),
        in_specs=[
            pl.BlockSpec(memory_space=pltpu.SMEM),
            pl.BlockSpec(memory_space=pltpu.VMEM),
        ],
        out_specs=[pl.BlockSpec(memory_space=pltpu.VMEM)] * 2,
        compiler_params=pltpu.CompilerParams(vmem_limit_bytes=32 << 20),
        name="order",
    )(device_index(), source)


def fetch_blocks(order, block_of, own_ref, other_ref, target_of, sems):
    copies = []
    for at, (matrix, r2, r1, k) in enumerate(order):
        for side, source in enumerate((own_ref, other_ref)):
            copies.append(
                pltpu.make_async_copy(
                    source.at[at],
                    target_of(matrix).at[block_of(r2, r1, k, bool(side))],
                    sems.at[2 * at + side],
                )
            )
    for copy in copies:
        copy.start()
    for copy in copies:
        copy.wait()


def block_out_kernel(index_ref, features_ref, hidden_ref, own_ref, other_ref, out_ref, weight, sems):
    block_of = placing(index_ref[0])
    fetch_blocks(PROJECT_ORDER, block_of, own_ref, other_ref, lambda m: weight, sems)
    count, rows, inner = weight.shape
    product = lax.dot_general(
        hidden_ref[...],
        weight[...].reshape(count * rows, inner),
        (((1,), (1,)), ((), ())),
        preferred_element_type=jnp.float32,
    )
    out_ref[...] = (features_ref[...].astype(jnp.float32) + product).astype(jnp.bfloat16)


def project_back(features, hidden, own, other):
    rows, inner = own.shape[1:]
    vmem = pl.BlockSpec(memory_space=pltpu.VMEM)
    hbm = pl.BlockSpec(memory_space=pl.ANY)
    return pl.pallas_call(
        block_out_kernel,
        out_shape=jax.ShapeDtypeStruct(features.shape, features.dtype),
        in_specs=[pl.BlockSpec(memory_space=pltpu.SMEM), vmem, vmem, hbm, hbm],
        out_specs=vmem,
        scratch_shapes=[
            pltpu.VMEM((32, rows, inner), own.dtype),
            pltpu.SemaphoreType.DMA((2 * len(PROJECT_ORDER),)),
        ],
        compiler_params=pltpu.CompilerParams(vmem_limit_bytes=32 << 20),
        name="project_back",
    )(device_index(), features, hidden, own, other)


GELU_SCALE = math.sqrt(2.0 / math.pi)
GELU_CUBE = 0.044715


def stream_grad_kernel(
    index_ref,
    features_ref,
    cotangent_ref,
    grad_ref,
    gain_ref,
    own_ref,
    other_ref,
    out_ref,
    gain_grad_ref,
    weight,
    total,
    sems,
):
    block_of = placing(index_ref[0])
    fetch_blocks(TAP_ORDER, block_of, own_ref, other_ref, lambda m: weight.at[m], sems)
    taps, count, rows, inner = weight.shape
    batch, padded_bins, _ = grad_ref.shape
    bins = padded_bins - 2 * DILATION_STEP
    for b in range(batch):
        rows_sum = None
        for tap in range(taps):
            shift = (taps - 1 - tap) * DILATION_STEP
            part = lax.dot_general(
                grad_ref[b, shift : shift + bins, :],
                weight[tap].reshape(count * rows, inner),
                (((1,), (1,)), ((), ())),
                preferred_element_type=jnp.float32,
            )
            rows_sum = part if rows_sum is None else rows_sum + part
        total[b * bins : (b + 1) * bins, :] = rows_sum
    channels = count * rows
    step = 32
    gain = gain_ref[...]

    def some_rows(i, gain_sum):
        at = pl.ds(pl.multiple_of(i * step, step), step)
        x = features_ref[at, :].astype(jnp.float32)
        inverse = lax.rsqrt(jnp.sum(x * x, axis=-1, keepdims=True) * (1.0 / channels) + eps)
        scaled = x * inverse
        v = scaled * gain
        square = v * v
        t = jnp.tanh(GELU_SCALE * (v + GELU_CUBE * (v * square)))
        slope = 0.5 * (1.0 + t) + 0.5 * v * (1.0 - t * t) * (
            GELU_SCALE * (1.0 + (3.0 * GELU_CUBE) * square)
        )
        dv = total[at, :] * slope
        dn = dv * gain
        mean = jnp.sum(dn * scaled, axis=-1, keepdims=True) * (1.0 / channels)
        dx = inverse * (dn - scaled * mean)
        out_ref[at, :] = (cotangent_ref[at, :].astype(jnp.float32) + dx).astype(jnp.bfloat16)
        return gain_sum + jnp.sum(dv * scaled, axis=0, keepdims=True)

    gain_grad_ref[...] = lax.fori_loop(
        0, batch * bins // step, some_rows, jnp.zeros((1, channels), jnp.float32)
    )


def stream_grad(features, cotangent, grad_padded, gain, own, other):
    rows, inner = own.shape[1:]
    tokens, channels = features.shape
    vmem = pl.BlockSpec(memory_space=pltpu.VMEM)
    hbm = pl.BlockSpec(memory_space=pl.ANY)
    return pl.pallas_call(
        stream_grad_kernel,
        out_shape=(
            jax.ShapeDtypeStruct(features.shape, features.dtype),
            jax.ShapeDtypeStruct((1, channels), jnp.float32),
        ),
        in_specs=[pl.BlockSpec(memory_space=pltpu.SMEM), vmem, vmem, vmem, vmem, hbm, hbm],
        out_specs=[vmem, vmem],
        scratch_shapes=[
            pltpu.VMEM((KERNEL_TAPS, 32, rows, inner), own.dtype),
            pltpu.VMEM((tokens, channels), jnp.float32),
            pltpu.SemaphoreType.DMA((2 * len(TAP_ORDER),)),
        ],
        compiler_params=pltpu.CompilerParams(vmem_limit_bytes=40 << 20),
        name="stream_grad",
    )(device_index(), features, cotangent, grad_padded, gain.reshape(1, channels), own, other)


def rows_dot(left, right):
    return jnp.einsum("nrt,ti->nri", left, right, preferred_element_type=jnp.float32)


def contract(left, right):
    n, rows, tokens = left.shape
    return jnp.einsum(
        "ct,ci->ti",
        left.reshape(n * rows, tokens),
        right.reshape(n * rows, right.shape[2]),
        preferred_element_type=jnp.float32,
    )


def body_torus(features, cotangent, dilated_kernel_weight, project_weight, outer_gain, inner_gain):
    batch, bin_count, channels = features.shape
    inner = project_weight.shape[1]
    rows = project_weight.shape[0]
    tokens = batch * bin_count
    factor = 1.0 / math.sqrt(tokens * TORUS_DEVICES)

    taps = jnp.moveaxis(dilated_kernel_weight, 1, 0)
    plane = gather_z(taps)
    proj = project_weight[None]
    proj = cat(proj, send(proj, FIRST))
    proj = cat(proj, send(proj, SECOND))
    near = cat(plane, send(plane, FIRST))
    far = send(near, SECOND)
    own_project = gather_z(proj)
    own_taps = cat(near, far)
    near_other = send(near, CORE)
    far_other = send(far, CORE)
    other_project = send(own_project, CORE)
    other_taps = cat(near_other, far_other)

    features_padded = padded(features, (("seq", 1),), DILATION_STEP)
    active = act_norm(features_padded.astype(jnp.float32), outer_gain).astype(jnp.bfloat16)
    turned = [
        active[:, tap * DILATION_STEP : tap * DILATION_STEP + bin_count]
        .reshape(tokens, channels)
        .T.reshape(32, rows, tokens)
        for tap in range(KERNEL_TAPS)
    ]
    turned.append(cotangent.reshape(tokens, channels).T.reshape(32, rows, tokens))
    act_own, act_other = in_arrival_order(jnp.stack(turned))

    conv_output = (
        contract(act_own[:24], near)
        + contract(act_other[:24], near_other)
        + contract(act_own[24:48], far)
        + contract(act_other[24:48], far_other)
    )
    hidden32, pull_inner = jax.vjp(act_norm, conv_output, inner_gain)
    hidden = hidden32.astype(jnp.bfloat16)

    keep3 = rows_dot(act_own[48:], hidden)
    give3 = rows_dot(act_other[48:], hidden).astype(jnp.bfloat16)
    sum3 = keep3 + send(give3, CORE).astype(jnp.float32)
    sum3 = scatter_z(sum3)
    sum3 = scatter_pair(sum3, SECOND)
    sum3 = scatter_pair(sum3, FIRST)
    grad_project = sum3[0] * factor

    grad_hidden = contract(act_own[48:], own_project) + contract(act_other[48:], other_project)
    grad_conv, grad_gain_inner = pull_inner(grad_hidden)
    grad_conv = grad_conv.astype(jnp.bfloat16)

    keep = rows_dot(act_own[:48], grad_conv)
    give = rows_dot(act_other[:48], grad_conv).astype(jnp.bfloat16)
    sums = keep + send(give, CORE).astype(jnp.float32)
    sums = scatter_pair(sums, SECOND)
    sums = scatter_pair(sums, FIRST)
    sums = scatter_z(sums)
    grad_dilated = jnp.moveaxis(sums, 0, 1) * factor

    flat = features.reshape(tokens, channels)
    block_out = project_back(flat, hidden, own_project, other_project).reshape(features.shape)
    grad_padded = padded(
        grad_conv.reshape(batch, bin_count, inner), (("seq", 1),), DILATION_STEP
    )
    grad_features, grad_gain_outer = stream_grad(
        flat, cotangent.reshape(tokens, channels), grad_padded, outer_gain, own_taps, other_taps
    )
    grad_features = grad_features.reshape(features.shape)

    gains = jnp.concatenate([grad_gain_outer[0], grad_gain_inner]) * factor
    for distance in (1, 2, 4, 8, 16):
        gains = gains + send(gains, links(lambda i: i ^ distance))
    device = lax.axis_index("seq")
    grad_outer_gain = lax.dynamic_slice(gains, (device * rows,), (rows,))
    part = inner // TORUS_DEVICES
    grad_inner_gain = lax.dynamic_slice(gains, (channels + device * part,), (part,))
    return (block_out, grad_features, grad_dilated, grad_project, grad_outer_gain, grad_inner_gain)


def body(*operands):
    if lax.axis_size("seq") == TORUS_DEVICES:
        return body_torus(*operands)
    return body_any(*operands)


def solution(mesh):
    return jax.shard_map(
        body,
        mesh=mesh,
        in_specs=(
            P("groups", "seq", None),
            P("groups", "seq", None),
            P("seq", None, None),
            P("seq", None),
            P(),
            P(),
        ),
        out_specs=(
            P("groups", "seq", None),
            P("groups", "seq", None),
            P(("groups", "seq"), None, None),
            P(("groups", "seq"), None),
            P(("groups", "seq")),
            P(("groups", "seq")),
        ),
        check_vma=False,
    )
```

```python
import functools
import math

import jax
import jax.numpy as jnp
from jax import lax
from jax.experimental import pallas as pl
from jax.experimental.pallas import tpu as pltpu
from jax.sharding import PartitionSpec as P

KERNEL_TAPS = 3
DILATION_STEP = 32
TORUS_DEVICES = 32


eps = 1e-06


def padded(block, sides, width):
    for axis, dim in sides:
        count = lax.axis_size(axis)
        forward = [(i, i + 1) for i in range(count - 1)]
        backward = [(target, source) for source, target in forward]
        low = lax.ppermute(
            lax.slice_in_dim(block, block.shape[dim] - width, None, axis=dim), axis, forward
        )
        high = lax.ppermute(lax.slice_in_dim(block, 0, width, axis=dim), axis, backward)
        block = jnp.concatenate([low, block, high], axis=dim)
    return block


def act_norm(values, gain):
    meansq = jnp.mean(values * values, axis=-1, keepdims=True)
    return jax.nn.gelu(values * lax.rsqrt(meansq + eps) * gain, approximate=True)


def reduce_dilated(padded_input, conv_output_gradient, factor):
    bin_count = conv_output_gradient.shape[1]
    tap_slices = [
        jnp.einsum(
            "btc,bti->ci",
            padded_input[:, tap_index * DILATION_STEP : tap_index * DILATION_STEP + bin_count],
            conv_output_gradient,
            preferred_element_type=jnp.float32,
        )
        for tap_index in range(KERNEL_TAPS)
    ]
    return lax.psum_scatter(
        jnp.stack(tap_slices, axis=1) * factor, "seq", scatter_dimension=0, tiled=True
    )


def body_any(features, cotangent, dilated_kernel_weight, project_weight, outer_gain, inner_gain):
    bin_count = features.shape[1]
    factor = 1.0 / math.sqrt(features.shape[0] * bin_count * lax.axis_size("seq"))
    full_dilated = lax.all_gather(dilated_kernel_weight, "seq", axis=0, tiled=True)
    full_project = lax.all_gather(project_weight, "seq", axis=0, tiled=True)
    as_float = features.astype(jnp.float32)
    active_features = act_norm(as_float, outer_gain).astype(jnp.bfloat16)
    padded_input = padded(active_features, (("seq", 1),), DILATION_STEP)
    conv_output = jnp.einsum(
        "btc,ci->bti",
        padded_input[:, 0:bin_count],
        full_dilated[:, 0, :],
        preferred_element_type=jnp.float32,
    )
    for tap_index in range(1, KERNEL_TAPS):
        conv_output = conv_output + jnp.einsum(
            "btc,ci->bti",
            padded_input[:, tap_index * DILATION_STEP : tap_index * DILATION_STEP + bin_count],
            full_dilated[:, tap_index, :],
            preferred_element_type=jnp.float32,
        )
    hidden = act_norm(conv_output, inner_gain).astype(jnp.bfloat16)
    block_out = (
        as_float
        + jnp.einsum("bti,ci->btc", hidden, full_project, preferred_element_type=jnp.float32)
    ).astype(jnp.bfloat16)
    grad_hidden = jnp.einsum(
        "btc,ci->bti", cotangent, full_project, preferred_element_type=jnp.float32
    )
    unused, pull_inner = jax.vjp(act_norm, conv_output, inner_gain)
    conv_output_gradient, grad_gain_inner = pull_inner(grad_hidden)
    conv_output_gradient = conv_output_gradient.astype(jnp.bfloat16)
    padded_input_gradient = padded(conv_output_gradient, (("seq", 1),), DILATION_STEP)
    grad_active = jnp.zeros(features.shape, jnp.float32)
    for tap_index in range(KERNEL_TAPS):
        tap_shift = (KERNEL_TAPS - 1 - tap_index) * DILATION_STEP
        grad_active = grad_active + jnp.einsum(
            "bti,ci->btc",
            padded_input_gradient[:, tap_shift : tap_shift + bin_count],
            full_dilated[:, tap_index, :],
            preferred_element_type=jnp.float32,
        )
    unused_two, pull_outer = jax.vjp(act_norm, as_float, outer_gain)
    grad_branch, grad_gain_outer = pull_outer(grad_active)
    grad_features = (cotangent.astype(jnp.float32) + grad_branch).astype(jnp.bfloat16)
    grad_dilated = reduce_dilated(padded_input, conv_output_gradient, factor)
    grad_project = lax.psum_scatter(
        jnp.einsum("btc,bti->ci", cotangent, hidden, preferred_element_type=jnp.float32) * factor,
        "seq",
        scatter_dimension=0,
        tiled=True,
    )
    grad_outer_gain, grad_inner_gain = (
        lax.psum_scatter(grad_gain_outer * factor, "seq", scatter_dimension=0, tiled=True),
        lax.psum_scatter(grad_gain_inner * factor, "seq", scatter_dimension=0, tiled=True),
    )
    return (block_out, grad_features, grad_dilated, grad_project, grad_outer_gain, grad_inner_gain)


def links(move):
    return [(i, move(i)) for i in range(TORUS_DEVICES)]


CORE = links(lambda i: i ^ 1)
FIRST = links(lambda i: i ^ (4 if i & 1 else 2))
SECOND = links(lambda i: i ^ (2 if i & 1 else 4))
Z_NEAR = links(lambda i: i ^ 8)
Z_FAR = links(lambda i: i ^ 16)

BITS = (0, 1)
PAIR_ORDER = [(r2, r1, low, high) for r2 in BITS for r1 in BITS for low in BITS for high in BITS]
LAST_ORDER = [(r2, r1, low, high) for r2 in BITS for low in BITS for high in BITS for r1 in BITS]
TAP_ORDERS = [PAIR_ORDER, PAIR_ORDER, LAST_ORDER]
PROJECT_ORDER = [(r2, r1, low, high) for low in BITS for high in BITS for r2 in BITS for r1 in BITS]
BLOCKS = 16
HALF = 8

VMEM = pl.BlockSpec(memory_space=pltpu.VMEM)
SMEM = pl.BlockSpec(memory_space=pltpu.SMEM)


def send(block, pairs):
    return lax.ppermute(block, "seq", pairs)


def after(value, *events):
    return lax.optimization_barrier((value,) + events)[0]


def device_index():
    return lax.axis_index("seq").astype(jnp.int32).reshape(1)


def block_of(device, place, other):
    r2, r1, low, high = place
    owner = device ^ other
    parity = owner & 1
    dx = r1 + parity * (r2 - r1)
    dy = r2 + parity * (r1 - r2)
    return owner ^ (16 * high + 8 * low + 4 * dy + 2 * dx)


def assemble(inputs, outputs):
    def kernel(*refs):
        sources, targets = refs[: len(inputs)], refs[len(inputs) :]
        for target, (_, _, pieces) in zip(targets, outputs):
            for source, start, count, to_m, to_n in pieces:
                n = sources[source].shape[1]
                target[to_m : to_m + count, to_n : to_n + n] = sources[source][
                    start : start + count
                ]

    tail = inputs[0].shape[2:]
    return pl.pallas_call(
        kernel,
        out_shape=[
            jax.ShapeDtypeStruct((m, n) + tail, inputs[0].dtype) for m, n, pieces in outputs
        ],
        in_specs=[VMEM] * len(inputs),
        out_specs=[VMEM] * len(outputs),
        compiler_params=pltpu.CompilerParams(vmem_limit_bytes=24 << 20),
        name="assemble",
    )(*inputs)


def upper(kept, received, pick=slice(None)):
    n = kept.shape[1] // 2
    total = kept[pick, n:] + received[pick, n:].astype(jnp.float32)
    return total.astype(jnp.bfloat16)


def lower(kept, received, pick=slice(None)):
    n = kept.shape[1] // 2
    return kept[pick, :n] + received[pick, :n].astype(jnp.float32)


GELU_SCALE = math.sqrt(2.0 / math.pi)
GELU_CUBE = 0.044715


def prepare_kernel(
    index_ref, features_ref, cotangent_ref, gain_ref, taps_ref, project_ref, active, turned
):
    device = index_ref[0]
    batch, padded_bins, channels = features_ref.shape
    bins = padded_bins - 2 * DILATION_STEP
    rows = taps_ref.shape[4]
    step = 32
    gain = gain_ref[...]
    for b in range(batch):

        def some_rows(i, carry):
            at = pl.multiple_of(i * step, step)
            x = features_ref[b, pl.ds(at, step), :].astype(jnp.float32)
            inverse = lax.rsqrt(jnp.sum(x * x, axis=-1, keepdims=True) * (1.0 / channels) + eps)
            v = x * inverse * gain
            t = jnp.tanh(GELU_SCALE * (v + GELU_CUBE * (v * v * v)))
            active[b, pl.ds(at, step), :] = (0.5 * v * (1.0 + t)).astype(jnp.bfloat16)
            return carry

        lax.fori_loop(0, padded_bins // step, some_rows, 0)

    def blocks(order):
        for other in BITS:
            for at, where in enumerate(order):
                start = pl.multiple_of(block_of(device, where, other) * rows, 16)
                yield other, at, turned[pl.ds(start, rows), :]

    for tap in range(KERNEL_TAPS):
        for b in range(batch):
            turned[:, b * bins : (b + 1) * bins] = active[
                b, tap * DILATION_STEP : tap * DILATION_STEP + bins, :
            ].T
        for other, at, block in blocks(TAP_ORDERS[tap]):
            taps_ref[other, at // HALF, tap, at % HALF] = block
    turned[...] = cotangent_ref[...].T
    for other, at, block in blocks(PROJECT_ORDER):
        project_ref[other, at // HALF, 0, at % HALF] = block


def prepare(features_padded, cotangent, gain, rows):
    tokens, channels = cotangent.shape
    shape = lambda count: jax.ShapeDtypeStruct((2, 2, count, HALF, rows, tokens), cotangent.dtype)
    return pl.pallas_call(
        prepare_kernel,
        out_shape=[shape(KERNEL_TAPS), shape(1)],
        in_specs=[SMEM, VMEM, VMEM, VMEM],
        out_specs=[VMEM] * 2,
        scratch_shapes=[
            pltpu.VMEM(features_padded.shape, jnp.bfloat16),
            pltpu.VMEM((channels, tokens), jnp.bfloat16),
        ],
        compiler_params=pltpu.CompilerParams(vmem_limit_bytes=32 << 20),
        name="prepare",
    )(device_index(), features_padded, cotangent, gain.reshape(1, channels))


def back_kernel(order_of, index_ref, turned_ref, *refs):
    parts, out_ref, placed = refs[:4], refs[4], refs[5]
    device = index_ref[0]
    matrices, inner, tokens = turned_ref.shape
    rows = parts[0].shape[2]
    for other in BITS:
        for which in BITS:
            part = parts[2 * other + which]
            for matrix in range(matrices):
                product = jnp.dot(
                    part[matrix].reshape(HALF * rows, inner),
                    turned_ref[matrix],
                    preferred_element_type=jnp.float32,
                )
                for at in range(HALF):
                    block = block_of(device, order_of[matrix][which * HALF + at], other)
                    target = pl.ds(pl.multiple_of(block * rows, 16), rows)
                    rows_of = product[at * rows : (at + 1) * rows]
                    if matrix == 0:
                        placed[target, :] = rows_of
                    else:
                        placed[target, :] += rows_of
    out_ref[...] = placed[...].T


def back(turned, parts, order_of):
    rows = parts[0].shape[2]
    tokens = turned.shape[2]
    channels = 2 * BLOCKS * rows
    return pl.pallas_call(
        functools.partial(back_kernel, order_of),
        out_shape=jax.ShapeDtypeStruct((tokens, channels), jnp.float32),
        in_specs=[SMEM] + [VMEM] * 5,
        out_specs=VMEM,
        scratch_shapes=[pltpu.VMEM((channels, tokens), jnp.float32)],
        compiler_params=pltpu.CompilerParams(vmem_limit_bytes=40 << 20),
        name="back",
    )(device_index(), turned, *parts)


def rows_dot(left, right):
    return jnp.einsum("mnrt,ti->mnri", left, right, preferred_element_type=jnp.float32)


def contract(left, right):
    return jnp.einsum(
        "ct,ci->ti",
        left.reshape(-1, left.shape[-1]),
        right.reshape(-1, right.shape[-1]),
        preferred_element_type=jnp.float32,
    )


def body_torus(features, cotangent, dilated_kernel_weight, project_weight, outer_gain, inner_gain):
    batch, bin_count, channels = features.shape
    inner = project_weight.shape[1]
    rows = project_weight.shape[0]
    tokens = batch * bin_count
    factor = 1.0 / math.sqrt(tokens * TORUS_DEVICES)
    as_bf16 = lambda value: value.astype(jnp.bfloat16)
    as_f32 = lambda value: value.astype(jnp.float32)

    taps = jnp.moveaxis(dilated_kernel_weight, 1, 0)[:, None]
    pair = taps[:2]
    rest = jnp.concatenate([taps[2:], project_weight[None, None]])
    pair_in, rest_in = send(pair, Z_FAR), send(rest, FIRST)
    pair, last, proj = assemble(
        (pair, pair_in, rest, rest_in),
        (
            (2, 2, ((0, 0, 2, 0, 0), (1, 0, 2, 0, 1))),
            (1, 2, ((2, 0, 1, 0, 0), (3, 0, 1, 0, 1))),
            (1, 2, ((2, 1, 1, 0, 0), (3, 1, 1, 0, 1))),
        ),
    )
    pair_in, last_in, proj_in = send(pair, Z_NEAR), send(last, Z_FAR), send(proj, SECOND)
    features_padded = padded(after(features, pair), (("seq", 1),), DILATION_STEP)
    grow = lambda m, n, a: (m, 2 * n, ((a, 0, m, 0, 0), (a + 1, 0, m, 0, n)))
    pair, last, proj = assemble(
        (pair, pair_in, last, last_in, proj, proj_in),
        (grow(2, 2, 0), grow(1, 2, 2), grow(1, 2, 4)),
    )
    pair_in, last_in, proj_in = send(pair, FIRST), send(last, Z_NEAR), send(proj, Z_FAR)
    (near,) = assemble(
        after((pair, pair_in, last, last_in), features_padded),
        (
            (
                3,
                8,
                ((0, 0, 2, 0, 0), (1, 0, 2, 0, 4), (2, 0, 1, 2, 0), (3, 0, 1, 2, 4)),
            ),
        ),
    )
    far, near_other = send(near, SECOND), send(near, CORE)
    flat_cotangent = cotangent.reshape(tokens, channels)
    act, act_p = prepare(after(features_padded, near), flat_cotangent, outer_gain, rows)
    (proj,) = assemble((proj, after(proj_in, act)), (grow(1, 4, 0),))
    proj_far, proj_other = send(proj, Z_NEAR), send(proj, CORE)
    conv_output = contract(act[0, 0], after(near, proj)) + contract(act[1, 0], near_other)
    far = after(far, conv_output)
    far_other = send(far, CORE)
    conv_output = conv_output + contract(act[0, 1], far) + contract(act[1, 1], far_other)
    grad_hidden = contract(act_p[0, 0], after(proj, conv_output)) + contract(
        act_p[1, 0], proj_other
    )
    hidden32, pull_inner = jax.vjp(act_norm, conv_output, inner_gain)
    hidden = as_bf16(hidden32)
    give_p = as_bf16(rows_dot(act_p[1].reshape(2, HALF, rows, tokens), hidden))
    recv_p = send(give_p, CORE)
    proj_far = after(proj_far, give_p)
    proj_far_other = send(proj_far, CORE)
    grad_hidden = (
        grad_hidden + contract(act_p[0, 1], proj_far) + contract(act_p[1, 1], proj_far_other)
    )
    grad_conv, grad_gain_inner = pull_inner(grad_hidden)
    grad_conv = as_bf16(grad_conv)
    grad_padded = padded(
        grad_conv.reshape(batch, bin_count, inner), (("seq", 1),), DILATION_STEP
    )

    give = as_bf16(rows_dot(act[1, 1], grad_conv))
    recv_far = send(give, CORE)
    give = as_bf16(rows_dot(act[1, 0], after(grad_conv, give)))
    recv_near = send(give, CORE)
    message_p = as_bf16(rows_dot(act_p[0, 1], after(hidden, give)) + as_f32(recv_p[1:]))
    far_p = send(message_p, Z_NEAR)
    message = as_bf16(
        rows_dot(act[0, 1], after(grad_conv, message_p)) + as_f32(recv_far)
    )
    recv = send(message, SECOND)
    kept = rows_dot(act[0, 0], after(grad_conv, message)) + as_f32(recv_near)
    kept_p = rows_dot(act_p[0, 0], after(hidden, message)) + as_f32(recv_p[:1])

    grad_padded = after(grad_padded, kept, kept_p)
    turned = jnp.stack(
        [
            grad_padded[:, shift : shift + bin_count].reshape(tokens, inner).T
            for shift in (2 * DILATION_STEP, DILATION_STEP, 0)
        ]
    )
    grad_active = back(turned, (near, far, near_other, far_other), TAP_ORDERS)
    far_p = after(far_p, grad_active)
    message_p = upper(kept_p, far_p)
    kept_p, recv_p = lower(kept_p, far_p), send(message_p, Z_FAR)
    unused, pull_outer = jax.vjp(act_norm, as_f32(after(features, message_p)), outer_gain)
    grad_branch, grad_gain_outer = pull_outer(grad_active.reshape(features.shape))
    grad_features = as_bf16(as_f32(cotangent) + grad_branch)
    gains = jnp.concatenate([grad_gain_outer, grad_gain_inner]) * factor
    gains = gains + send(gains, CORE)
    gains = gains + send(gains, links(lambda i: i ^ 2))
    projected = back(
        after(hidden, gains).T[None],
        (proj, proj_far, proj_other, proj_far_other),
        [PROJECT_ORDER],
    )
    block_out = as_bf16(as_f32(features) + projected.reshape(features.shape))

    recv = after(recv, gains, block_out)
    pair, last = slice(0, 2), slice(2, 3)
    message, message_l = upper(kept, recv, pair), upper(kept, recv, last)
    kept, kept_l = lower(kept, recv, pair), lower(kept, recv, last)
    recv, recv_l = send(message, FIRST), send(message_l, Z_NEAR)
    gains = after(gains, message, message_l)
    gains = gains + send(gains, links(lambda i: i ^ 4))

    recv, recv_l, recv_p, _ = lax.optimization_barrier((recv, recv_l, recv_p, gains))
    message, message_l, message_p = upper(kept, recv), upper(kept_l, recv_l), upper(kept_p, recv_p)
    kept, kept_l, kept_p = lower(kept, recv), lower(kept_l, recv_l), lower(kept_p, recv_p)
    recv, recv_l, recv_p = send(message, Z_NEAR), send(message_l, Z_FAR), send(message_p, SECOND)
    gains = after(gains, message, message_l, message_p)
    gains = gains + send(gains, Z_NEAR)

    recv, recv_l, recv_p, _ = lax.optimization_barrier((recv, recv_l, recv_p, gains))
    message = upper(kept, recv)
    message_r = jnp.concatenate([upper(kept_l, recv_l), upper(kept_p, recv_p)])
    kept, kept_l, kept_p = lower(kept, recv), lower(kept_l, recv_l), lower(kept_p, recv_p)
    recv, recv_r = send(message, Z_FAR), send(message_r, FIRST)
    gains = after(gains, message, message_r)
    gains = gains + send(gains, Z_FAR)

    grad_project = (kept_p[0, 0] + as_f32(recv_r[1, 0])) * factor
    sums = kept + as_f32(recv)
    grad_dilated = (
        jnp.stack([sums[0, 0], sums[1, 0], kept_l[0, 0] + as_f32(recv_r[0, 0])], axis=1) * factor
    )

    device = lax.axis_index("seq")
    grad_outer_gain = lax.dynamic_slice(gains, (device * rows,), (rows,))
    part = inner // TORUS_DEVICES
    grad_inner_gain = lax.dynamic_slice(gains, (channels + device * part,), (part,))
    return (block_out, grad_features, grad_dilated, grad_project, grad_outer_gain, grad_inner_gain)


def body(*operands):
    if lax.axis_size("seq") == TORUS_DEVICES:
        return body_torus(*operands)
    return body_any(*operands)


def solution(mesh):
    return jax.shard_map(
        body,
        mesh=mesh,
        in_specs=(
            P("groups", "seq", None),
            P("groups", "seq", None),
            P("seq", None, None),
            P("seq", None),
            P(),
            P(),
        ),
        out_specs=(
            P("groups", "seq", None),
            P("groups", "seq", None),
            P(("groups", "seq"), None, None),
            P(("groups", "seq"), None),
            P(("groups", "seq")),
            P(("groups", "seq")),
        ),
        check_vma=False,
    )
```

```python
import math

import jax
import jax.numpy as jnp
from jax import lax
from jax.experimental import pallas as pl
from jax.experimental.pallas import tpu as pltpu
from jax.sharding import PartitionSpec as P

KERNEL_TAPS = 3
DILATION_STEP = 32
TORUS_DEVICES = 32


eps = 1e-06


def edges(block, axis, dim, width):
    count = lax.axis_size(axis)
    forward = [(i, i + 1) for i in range(count - 1)]
    backward = [(target, source) for source, target in forward]
    low = lax.ppermute(
        lax.slice_in_dim(block, block.shape[dim] - width, None, axis=dim), axis, forward
    )
    high = lax.ppermute(lax.slice_in_dim(block, 0, width, axis=dim), axis, backward)
    return low, high


def padded(block, sides, width):
    for axis, dim in sides:
        low, high = edges(block, axis, dim, width)
        block = jnp.concatenate([low, block, high], axis=dim)
    return block


def act_norm(values, gain):
    meansq = jnp.mean(values * values, axis=-1, keepdims=True)
    return jax.nn.gelu(values * lax.rsqrt(meansq + eps) * gain, approximate=True)


def reduce_dilated(padded_input, conv_output_gradient, factor):
    bin_count = conv_output_gradient.shape[1]
    tap_slices = [
        jnp.einsum(
            "btc,bti->ci",
            padded_input[:, tap_index * DILATION_STEP : tap_index * DILATION_STEP + bin_count],
            conv_output_gradient,
            preferred_element_type=jnp.float32,
        )
        for tap_index in range(KERNEL_TAPS)
    ]
    return lax.psum_scatter(
        jnp.stack(tap_slices, axis=1) * factor, "seq", scatter_dimension=0, tiled=True
    )


def body_any(features, cotangent, dilated_kernel_weight, project_weight, outer_gain, inner_gain):
    bin_count = features.shape[1]
    factor = 1.0 / math.sqrt(features.shape[0] * bin_count * lax.axis_size("seq"))
    full_dilated = lax.all_gather(dilated_kernel_weight, "seq", axis=0, tiled=True)
    full_project = lax.all_gather(project_weight, "seq", axis=0, tiled=True)
    as_float = features.astype(jnp.float32)
    active_features = act_norm(as_float, outer_gain).astype(jnp.bfloat16)
    padded_input = padded(active_features, (("seq", 1),), DILATION_STEP)
    conv_output = jnp.einsum(
        "btc,ci->bti",
        padded_input[:, 0:bin_count],
        full_dilated[:, 0, :],
        preferred_element_type=jnp.float32,
    )
    for tap_index in range(1, KERNEL_TAPS):
        conv_output = conv_output + jnp.einsum(
            "btc,ci->bti",
            padded_input[:, tap_index * DILATION_STEP : tap_index * DILATION_STEP + bin_count],
            full_dilated[:, tap_index, :],
            preferred_element_type=jnp.float32,
        )
    hidden = act_norm(conv_output, inner_gain).astype(jnp.bfloat16)
    block_out = (
        as_float
        + jnp.einsum("bti,ci->btc", hidden, full_project, preferred_element_type=jnp.float32)
    ).astype(jnp.bfloat16)
    grad_hidden = jnp.einsum(
        "btc,ci->bti", cotangent, full_project, preferred_element_type=jnp.float32
    )
    unused, pull_inner = jax.vjp(act_norm, conv_output, inner_gain)
    conv_output_gradient, grad_gain_inner = pull_inner(grad_hidden)
    conv_output_gradient = conv_output_gradient.astype(jnp.bfloat16)
    padded_input_gradient = padded(conv_output_gradient, (("seq", 1),), DILATION_STEP)
    grad_active = jnp.zeros(features.shape, jnp.float32)
    for tap_index in range(KERNEL_TAPS):
        tap_shift = (KERNEL_TAPS - 1 - tap_index) * DILATION_STEP
        grad_active = grad_active + jnp.einsum(
            "bti,ci->btc",
            padded_input_gradient[:, tap_shift : tap_shift + bin_count],
            full_dilated[:, tap_index, :],
            preferred_element_type=jnp.float32,
        )
    unused_two, pull_outer = jax.vjp(act_norm, as_float, outer_gain)
    grad_branch, grad_gain_outer = pull_outer(grad_active)
    grad_features = (cotangent.astype(jnp.float32) + grad_branch).astype(jnp.bfloat16)
    grad_dilated = reduce_dilated(padded_input, conv_output_gradient, factor)
    grad_project = lax.psum_scatter(
        jnp.einsum("btc,bti->ci", cotangent, hidden, preferred_element_type=jnp.float32) * factor,
        "seq",
        scatter_dimension=0,
        tiled=True,
    )
    grad_outer_gain, grad_inner_gain = (
        lax.psum_scatter(grad_gain_outer * factor, "seq", scatter_dimension=0, tiled=True),
        lax.psum_scatter(grad_gain_inner * factor, "seq", scatter_dimension=0, tiled=True),
    )
    return (block_out, grad_features, grad_dilated, grad_project, grad_outer_gain, grad_inner_gain)


def links(move):
    return [(i, move(i)) for i in range(TORUS_DEVICES)]


CORE = links(lambda i: i ^ 1)
FIRST = links(lambda i: i ^ (4 if i & 1 else 2))
SECOND = links(lambda i: i ^ (2 if i & 1 else 4))
Z_NEAR = links(lambda i: i ^ 8)
Z_FAR = links(lambda i: i ^ 16)

BITS = (0, 1)
PAIR_ORDER = [(r2, r1, low, high) for r2 in BITS for r1 in BITS for low in BITS for high in BITS]
LAST_ORDER = [(r2, r1, low, high) for r2 in BITS for low in BITS for high in BITS for r1 in BITS]
TAP_ORDERS = [PAIR_ORDER, PAIR_ORDER, LAST_ORDER]
PROJECT_ORDER = LAST_ORDER
BLOCKS = 16
HALF = 8

VMEM = pl.BlockSpec(memory_space=pltpu.VMEM)
SMEM = pl.BlockSpec(memory_space=pltpu.SMEM)


def send(block, pairs):
    return lax.ppermute(block, "seq", pairs)


def after(value, *events):
    return lax.optimization_barrier((value,) + events)[0]


def device_index():
    return lax.axis_index("seq").astype(jnp.int32).reshape(1)


def block_of(device, place, other):
    r2, r1, low, high = place
    owner = device ^ other
    parity = owner & 1
    dx = r1 + parity * (r2 - r1)
    dy = r2 + parity * (r1 - r2)
    return owner ^ (16 * high + 8 * low + 4 * dy + 2 * dx)


def assemble(inputs, outputs):
    def kernel(*refs):
        sources, targets = refs[: len(inputs)], refs[len(inputs) :]
        for target, (_, _, pieces) in zip(targets, outputs):
            for source, start, count, to_m, to_n in pieces:
                n = sources[source].shape[1]
                target[to_m : to_m + count, to_n : to_n + n] = sources[source][
                    start : start + count
                ]

    tail = inputs[0].shape[2:]
    return pl.pallas_call(
        kernel,
        out_shape=[
            jax.ShapeDtypeStruct((m, n) + tail, inputs[0].dtype) for m, n, pieces in outputs
        ],
        in_specs=[VMEM] * len(inputs),
        out_specs=[VMEM] * len(outputs),
        compiler_params=pltpu.CompilerParams(vmem_limit_bytes=8 << 20),
        name="assemble",
    )(*inputs)


def upper(kept, received, pick=slice(None)):
    n = kept.shape[1] // 2
    total = kept[pick, n:] + received[pick, n:].astype(jnp.float32)
    return total.astype(jnp.bfloat16)


def lower(kept, received, pick=slice(None)):
    n = kept.shape[1] // 2
    return kept[pick, :n] + received[pick, :n].astype(jnp.float32)


GELU_SCALE = math.sqrt(2.0 / math.pi)
GELU_CUBE = 0.044715


def prepare_kernel(
    index_ref, features_ref, cotangent_ref, gain_ref, taps_ref, project_ref, active, turned
):
    device = index_ref[0]
    batch, padded_bins, channels = features_ref.shape
    bins = padded_bins - 2 * DILATION_STEP
    rows = taps_ref.shape[4]
    step = 32
    gain = gain_ref[...]
    for b in range(batch):

        def some_rows(i, carry):
            at = pl.multiple_of(i * step, step)
            x = features_ref[b, pl.ds(at, step), :].astype(jnp.float32)
            inverse = lax.rsqrt(jnp.sum(x * x, axis=-1, keepdims=True) * (1.0 / channels) + eps)
            v = x * inverse * gain
            t = jnp.tanh(GELU_SCALE * (v + GELU_CUBE * (v * v * v)))
            active[b, pl.ds(at, step), :] = (0.5 * v * (1.0 + t)).astype(jnp.bfloat16)
            return carry

        lax.fori_loop(0, padded_bins // step, some_rows, 0)

    def blocks(order):
        for other in BITS:
            for at, where in enumerate(order):
                start = pl.multiple_of(block_of(device, where, other) * rows, 16)
                yield other, at, turned[pl.ds(start, rows), :]

    for tap in range(KERNEL_TAPS):
        for b in range(batch):
            turned[:, b * bins : (b + 1) * bins] = active[
                b, tap * DILATION_STEP : tap * DILATION_STEP + bins, :
            ].T
        for other, at, block in blocks(TAP_ORDERS[tap]):
            taps_ref[other, at // HALF, tap, at % HALF] = block
    turned[...] = cotangent_ref[...].T
    for other, at, block in blocks(PROJECT_ORDER):
        project_ref[other, at // HALF, 0, at % HALF] = block


def prepare(features_padded, cotangent, gain, rows):
    tokens, channels = cotangent.shape
    shape = lambda count: jax.ShapeDtypeStruct((2, 2, count, HALF, rows, tokens), cotangent.dtype)
    return pl.pallas_call(
        prepare_kernel,
        out_shape=[shape(KERNEL_TAPS), shape(1)],
        in_specs=[SMEM, VMEM, VMEM, VMEM],
        out_specs=[VMEM] * 2,
        scratch_shapes=[
            pltpu.VMEM(features_padded.shape, jnp.bfloat16),
            pltpu.VMEM((channels, tokens), jnp.bfloat16),
        ],
        compiler_params=pltpu.CompilerParams(vmem_limit_bytes=16 << 20),
        name="prepare",
    )(device_index(), features_padded, cotangent, gain.reshape(1, channels))


def place_products(device, parts, turned, orders, placed):
    rows, inner = parts[0].shape[2:]
    for other in BITS:
        for which in BITS:
            part = parts[2 * other + which]
            for matrix, right in enumerate(turned):
                product = jnp.dot(
                    part[matrix].reshape(HALF * rows, inner),
                    right,
                    preferred_element_type=jnp.float32,
                )
                for at in range(HALF):
                    block = block_of(device, orders[matrix][which * HALF + at], other)
                    target = pl.ds(pl.multiple_of(block * rows, 16), rows)
                    rows_of = product[at * rows : (at + 1) * rows]
                    if matrix == 0:
                        placed[target, :] = rows_of
                    else:
                        placed[target, :] += rows_of


def project_back_kernel(index_ref, hidden_ref, features_ref, *refs):
    parts, out_ref, placed = refs[:4], refs[4], refs[5]
    place_products(index_ref[0], parts, [hidden_ref[...].T], [PROJECT_ORDER], placed)
    out_ref[...] = (features_ref[...].astype(jnp.float32) + placed[...].T).astype(jnp.bfloat16)


def project_back(hidden, features, parts):
    return pl.pallas_call(
        project_back_kernel,
        out_shape=jax.ShapeDtypeStruct(features.shape, features.dtype),
        in_specs=[SMEM] + [VMEM] * 6,
        out_specs=VMEM,
        scratch_shapes=[pltpu.VMEM(features.shape[::-1], jnp.float32)],
        compiler_params=pltpu.CompilerParams(vmem_limit_bytes=16 << 20),
        name="project_back",
    )(device_index(), hidden, features, *parts)


def grad_active_kernel(index_ref, grad_ref, low_ref, high_ref, *refs):
    parts, (out_ref, padded_ref, placed) = refs[:4], refs[4:]
    batch, padded_bins, _ = padded_ref.shape
    bins = padded_bins - 2 * DILATION_STEP
    for b in range(batch):
        padded_ref[b, :DILATION_STEP] = low_ref[b]
        padded_ref[b, DILATION_STEP : DILATION_STEP + bins] = grad_ref[b * bins : (b + 1) * bins]
        padded_ref[b, DILATION_STEP + bins :] = high_ref[b]
    turned = []
    for tap in range(KERNEL_TAPS):
        shift = (KERNEL_TAPS - 1 - tap) * DILATION_STEP
        turned.append(
            jnp.concatenate([padded_ref[b, shift : shift + bins] for b in range(batch)], axis=0).T
        )
    place_products(index_ref[0], parts, turned, TAP_ORDERS, placed)
    out_ref[...] = placed[...].T


def grad_of_active(grad, low, high, parts):
    tokens, inner = grad.shape
    batch = low.shape[0]
    channels = 2 * BLOCKS * parts[0].shape[2]
    return pl.pallas_call(
        grad_active_kernel,
        out_shape=jax.ShapeDtypeStruct((tokens, channels), jnp.float32),
        in_specs=[SMEM] + [VMEM] * 7,
        out_specs=VMEM,
        scratch_shapes=[
            pltpu.VMEM((batch, tokens // batch + 2 * DILATION_STEP, inner), grad.dtype),
            pltpu.VMEM((channels, tokens), jnp.float32),
        ],
        compiler_params=pltpu.CompilerParams(vmem_limit_bytes=24 << 20),
        name="grad_active",
    )(device_index(), grad, low, high, *parts)


def rows_dot(left, right):
    return jnp.einsum("mnrt,ti->mnri", left, right, preferred_element_type=jnp.float32)


def contract(left, right):
    return jnp.einsum(
        "ct,ci->ti",
        left.reshape(-1, left.shape[-1]),
        right.reshape(-1, right.shape[-1]),
        preferred_element_type=jnp.float32,
    )


def body_torus(features, cotangent, dilated_kernel_weight, project_weight, outer_gain, inner_gain):
    batch, bin_count, channels = features.shape
    inner = project_weight.shape[1]
    rows = project_weight.shape[0]
    tokens = batch * bin_count
    factor = 1.0 / math.sqrt(tokens * TORUS_DEVICES)
    as_bf16 = lambda value: value.astype(jnp.bfloat16)
    as_f32 = lambda value: value.astype(jnp.float32)

    taps = jnp.moveaxis(dilated_kernel_weight, 1, 0)[:, None]
    pair = taps[:2]
    rest = jnp.concatenate([taps[2:], project_weight[None, None]])
    pair_in, rest_in = send(pair, Z_FAR), send(rest, FIRST)
    low, high = edges(features, "seq", 1, DILATION_STEP)
    pair_in = after(pair_in, low, high)
    pair, last, proj = assemble(
        (pair, pair_in, rest, rest_in),
        (
            (2, 2, ((0, 0, 2, 0, 0), (1, 0, 2, 0, 1))),
            (1, 2, ((2, 0, 1, 0, 0), (3, 0, 1, 0, 1))),
            (1, 2, ((2, 1, 1, 0, 0), (3, 1, 1, 0, 1))),
        ),
    )
    pair_in, last_in, proj_b = send(pair, Z_NEAR), send(last, Z_FAR), send(proj, SECOND)
    grow = lambda m, n, a: (m, 2 * n, ((a, 0, m, 0, 0), (a + 1, 0, m, 0, n)))
    pair_in = after(pair_in, proj_b)
    pair, last = assemble((pair, pair_in, last, last_in), (grow(2, 2, 0), grow(1, 2, 2)))
    pair_in, last_in, proj_in = send(pair, FIRST), send(last, Z_NEAR), send(proj, Z_FAR)
    near, proj_a = assemble(
        (pair, pair_in, last, last_in, proj, proj_in),
        (
            (3, 8, ((0, 0, 2, 0, 0), (1, 0, 2, 0, 4), (2, 0, 1, 2, 0), (3, 0, 1, 2, 4))),
            grow(1, 2, 4),
        ),
    )
    far, near_other = send(near, SECOND), send(near, CORE)
    proj_in, proj_b_in = send(proj_a, Z_NEAR), send(proj_b, Z_FAR)
    flat_cotangent = cotangent.reshape(tokens, channels)
    features_padded = jnp.concatenate([low, after(features, near), high], axis=1)
    act, act_p = prepare(features_padded, flat_cotangent, outer_gain, rows)
    proj_a, proj_b = assemble(
        (proj_a, after(proj_in, act), proj_b, proj_b_in), (grow(1, 4, 0), grow(1, 2, 2))
    )
    proj_b_in, proj_a_other = send(proj_b, Z_NEAR), send(proj_a, CORE)
    conv_output = contract(act[0, 0], after(near, proj_b)) + contract(act[1, 0], near_other)
    grad_hidden = contract(act_p[0, 0], after(proj_a, conv_output)) + contract(
        act_p[1, 0], proj_a_other
    )
    (proj_b,) = assemble((proj_b, after(proj_b_in, grad_hidden)), (grow(1, 4, 0),))
    proj_b_other = send(proj_b, CORE)
    far = after(far, proj_b)
    far_other = send(far, CORE)
    conv_output = conv_output + contract(act[0, 1], far) + contract(act[1, 1], far_other)
    grad_hidden = (
        grad_hidden + contract(act_p[0, 1], proj_b) + contract(act_p[1, 1], proj_b_other)
    )
    hidden32, pull_inner = jax.vjp(act_norm, conv_output, inner_gain)
    hidden = as_bf16(hidden32)
    give_p = as_bf16(rows_dot(act_p[1].reshape(2, HALF, rows, tokens), hidden))
    recv_p = send(give_p, CORE)
    grad_conv, grad_gain_inner = pull_inner(after(grad_hidden, give_p))
    grad_conv = as_bf16(grad_conv)

    give = as_bf16(rows_dot(act[1, 1], grad_conv))
    recv_far = send(give, CORE)
    give = as_bf16(rows_dot(act[1, 0], after(grad_conv, give)))
    recv_near = send(give, CORE)
    low, high = edges(
        after(grad_conv, give).reshape(batch, bin_count, inner), "seq", 1, DILATION_STEP
    )
    message = as_bf16(rows_dot(act[0, 1], after(grad_conv, give)) + as_f32(recv_far))
    recv = send(message, SECOND)
    grad_p = after(hidden, message)
    split = lambda which: act_p[0, which].reshape(2, HALF // 2, rows, tokens)
    parts_of = lambda array, which: array[which].reshape(2, HALF // 2, rows, inner)
    message_b = as_bf16(
        rows_dot(split(1)[1:], grad_p) + as_f32(parts_of(recv_p, 1)[1:])
    )
    recv_b = send(message_b, Z_NEAR)
    message_a = as_bf16(
        rows_dot(split(0)[1:], grad_p) + as_f32(parts_of(recv_p, 0)[1:])
    )
    grad_p = after(hidden, message_a, message_b)
    kept_b = rows_dot(split(1)[:1], grad_p) + as_f32(parts_of(recv_p, 1)[:1])
    kept_a = rows_dot(split(0)[:1], grad_p) + as_f32(parts_of(recv_p, 0)[:1])
    kept = rows_dot(act[0, 0], after(grad_conv, kept_a, kept_b)) + as_f32(recv_near)

    flat = features.reshape(tokens, channels)
    grad_active = grad_of_active(
        after(grad_conv, kept), low, high, (near, far, near_other, far_other)
    )
    recv_b = after(recv_b, grad_active)
    message_b = upper(kept_b, recv_b)
    kept_b, recv_b = lower(kept_b, recv_b), send(message_b, Z_FAR)
    recv_a = send(after(message_a, message_b), Z_NEAR)
    unused, pull_outer = jax.vjp(act_norm, as_f32(after(features, message_b)), outer_gain)
    grad_branch, grad_gain_outer = pull_outer(grad_active.reshape(features.shape))
    grad_features = as_bf16(as_f32(cotangent) + grad_branch)
    gains = jnp.concatenate([grad_gain_outer, grad_gain_inner]) * factor
    gains = gains + send(gains, CORE)
    block_out = project_back(
        after(hidden, gains), flat, (proj_a, proj_b, proj_a_other, proj_b_other)
    ).reshape(features.shape)
    gains = after(gains, block_out)
    gains = gains + send(gains, links(lambda i: i ^ 2))
    recv_a, recv_b = after((recv_a, recv_b), gains)
    message_a, kept_a = upper(kept_a, recv_a), lower(kept_a, recv_a)
    kept_b = kept_b + as_f32(recv_b)

    recv = after(recv, message_a, kept_b)
    pair, last = slice(0, 2), slice(2, 3)
    message, message_l = upper(kept, recv, pair), upper(kept, recv, last)
    kept, kept_l = lower(kept, recv, pair), lower(kept, recv, last)
    recv, recv_l, recv_a = send(message, FIRST), send(message_l, Z_NEAR), send(message_a, Z_FAR)
    gains = after(gains, message, message_l)
    gains = gains + send(gains, links(lambda i: i ^ 4))

    recv, recv_l, recv_a, _ = lax.optimization_barrier((recv, recv_l, recv_a, gains))
    message, message_l, message_p = upper(kept, recv), upper(kept_l, recv_l), as_bf16(kept_b)
    kept, kept_l, kept_p = lower(kept, recv), lower(kept_l, recv_l), kept_a + as_f32(recv_a)
    recv, recv_l, recv_p = send(message, Z_NEAR), send(message_l, Z_FAR), send(message_p, SECOND)
    gains = after(gains, message, message_l, message_p)
    gains = gains + send(gains, Z_NEAR)

    recv, recv_l, recv_p, _ = lax.optimization_barrier((recv, recv_l, recv_p, gains))
    message = upper(kept, recv)
    kept_p = kept_p + as_f32(recv_p)
    message_r = jnp.concatenate([upper(kept_l, recv_l), as_bf16(kept_p[:, 1:])])
    kept, kept_l, kept_p = lower(kept, recv), lower(kept_l, recv_l), kept_p[:, :1]
    recv, recv_r = send(message, Z_FAR), send(message_r, FIRST)
    gains = after(gains, message, message_r)
    gains = gains + send(gains, Z_FAR)

    grad_project = (kept_p[0, 0] + as_f32(recv_r[1, 0])) * factor
    sums = kept + as_f32(recv)
    grad_dilated = (
        jnp.stack([sums[0, 0], sums[1, 0], kept_l[0, 0] + as_f32(recv_r[0, 0])], axis=1) * factor
    )

    device = lax.axis_index("seq")
    grad_outer_gain = lax.dynamic_slice(gains, (device * rows,), (rows,))
    part = inner // TORUS_DEVICES
    grad_inner_gain = lax.dynamic_slice(gains, (channels + device * part,), (part,))
    return (block_out, grad_features, grad_dilated, grad_project, grad_outer_gain, grad_inner_gain)


def body(*operands):
    if lax.axis_size("seq") == TORUS_DEVICES:
        return body_torus(*operands)
    return body_any(*operands)


def solution(mesh):
    return jax.shard_map(
        body,
        mesh=mesh,
        in_specs=(
            P("groups", "seq", None),
            P("groups", "seq", None),
            P("seq", None, None),
            P("seq", None),
            P(),
            P(),
        ),
        out_specs=(
            P("groups", "seq", None),
            P("groups", "seq", None),
            P(("groups", "seq"), None, None),
            P(("groups", "seq"), None),
            P(("groups", "seq")),
            P(("groups", "seq")),
        ),
        check_vma=False,
    )
```

```python
import math

import jax
import jax.numpy as jnp
from jax import lax
from jax.experimental import pallas as pl
from jax.experimental.pallas import tpu as pltpu
from jax.sharding import PartitionSpec as P

KERNEL_TAPS = 3
DILATION_STEP = 32
TORUS_DEVICES = 32


eps = 1e-06


def padded(block, sides, width):
    for axis, dim in sides:
        count = lax.axis_size(axis)
        forward = [(i, i + 1) for i in range(count - 1)]
        backward = [(target, source) for source, target in forward]
        low = lax.ppermute(
            lax.slice_in_dim(block, block.shape[dim] - width, None, axis=dim), axis, forward
        )
        high = lax.ppermute(lax.slice_in_dim(block, 0, width, axis=dim), axis, backward)
        block = jnp.concatenate([low, block, high], axis=dim)
    return block


def act_norm(values, gain):
    meansq = jnp.mean(values * values, axis=-1, keepdims=True)
    return jax.nn.gelu(values * lax.rsqrt(meansq + eps) * gain, approximate=True)


def reduce_dilated(padded_input, conv_output_gradient, factor):
    bin_count = conv_output_gradient.shape[1]
    tap_slices = [
        jnp.einsum(
            "btc,bti->ci",
            padded_input[:, tap_index * DILATION_STEP : tap_index * DILATION_STEP + bin_count],
            conv_output_gradient,
            preferred_element_type=jnp.float32,
        )
        for tap_index in range(KERNEL_TAPS)
    ]
    return lax.psum_scatter(
        jnp.stack(tap_slices, axis=1) * factor, "seq", scatter_dimension=0, tiled=True
    )


def body_any(features, cotangent, dilated_kernel_weight, project_weight, outer_gain, inner_gain):
    bin_count = features.shape[1]
    factor = 1.0 / math.sqrt(features.shape[0] * bin_count * lax.axis_size("seq"))
    full_dilated = lax.all_gather(dilated_kernel_weight, "seq", axis=0, tiled=True)
    full_project = lax.all_gather(project_weight, "seq", axis=0, tiled=True)
    as_float = features.astype(jnp.float32)
    active_features = act_norm(as_float, outer_gain).astype(jnp.bfloat16)
    padded_input = padded(active_features, (("seq", 1),), DILATION_STEP)
    conv_output = jnp.einsum(
        "btc,ci->bti",
        padded_input[:, 0:bin_count],
        full_dilated[:, 0, :],
        preferred_element_type=jnp.float32,
    )
    for tap_index in range(1, KERNEL_TAPS):
        conv_output = conv_output + jnp.einsum(
            "btc,ci->bti",
            padded_input[:, tap_index * DILATION_STEP : tap_index * DILATION_STEP + bin_count],
            full_dilated[:, tap_index, :],
            preferred_element_type=jnp.float32,
        )
    hidden = act_norm(conv_output, inner_gain).astype(jnp.bfloat16)
    block_out = (
        as_float
        + jnp.einsum("bti,ci->btc", hidden, full_project, preferred_element_type=jnp.float32)
    ).astype(jnp.bfloat16)
    grad_hidden = jnp.einsum(
        "btc,ci->bti", cotangent, full_project, preferred_element_type=jnp.float32
    )
    unused, pull_inner = jax.vjp(act_norm, conv_output, inner_gain)
    conv_output_gradient, grad_gain_inner = pull_inner(grad_hidden)
    conv_output_gradient = conv_output_gradient.astype(jnp.bfloat16)
    padded_input_gradient = padded(conv_output_gradient, (("seq", 1),), DILATION_STEP)
    grad_active = jnp.zeros(features.shape, jnp.float32)
    for tap_index in range(KERNEL_TAPS):
        tap_shift = (KERNEL_TAPS - 1 - tap_index) * DILATION_STEP
        grad_active = grad_active + jnp.einsum(
            "bti,ci->btc",
            padded_input_gradient[:, tap_shift : tap_shift + bin_count],
            full_dilated[:, tap_index, :],
            preferred_element_type=jnp.float32,
        )
    unused_two, pull_outer = jax.vjp(act_norm, as_float, outer_gain)
    grad_branch, grad_gain_outer = pull_outer(grad_active)
    grad_features = (cotangent.astype(jnp.float32) + grad_branch).astype(jnp.bfloat16)
    grad_dilated = reduce_dilated(padded_input, conv_output_gradient, factor)
    grad_project = lax.psum_scatter(
        jnp.einsum("btc,bti->ci", cotangent, hidden, preferred_element_type=jnp.float32) * factor,
        "seq",
        scatter_dimension=0,
        tiled=True,
    )
    grad_outer_gain, grad_inner_gain = (
        lax.psum_scatter(grad_gain_outer * factor, "seq", scatter_dimension=0, tiled=True),
        lax.psum_scatter(grad_gain_inner * factor, "seq", scatter_dimension=0, tiled=True),
    )
    return (block_out, grad_features, grad_dilated, grad_project, grad_outer_gain, grad_inner_gain)


def links(move):
    return [(i, move(i)) for i in range(TORUS_DEVICES)]


CORE = links(lambda i: i ^ 1)
FIRST = links(lambda i: i ^ (4 if i & 1 else 2))
SECOND = links(lambda i: i ^ (2 if i & 1 else 4))
Z_NEAR = links(lambda i: i ^ 8)
Z_FAR = links(lambda i: i ^ 16)

BITS = (0, 1)
PAIR_ORDER = [(r2, r1, low, high) for r2 in BITS for r1 in BITS for low in BITS for high in BITS]
LAST_ORDER = [(r2, r1, low, high) for r2 in BITS for low in BITS for high in BITS for r1 in BITS]
TAP_ORDERS = [PAIR_ORDER, PAIR_ORDER, LAST_ORDER]
PROJECT_ORDER = LAST_ORDER
BLOCKS = 16
HALF = 8

OUTER = [
    (i, j)
    for odd in range(1, TORUS_DEVICES - 1, 2)
    for i, j in ((odd, odd + 1), (odd + 1, odd))
]

VMEM = pl.BlockSpec(memory_space=pltpu.VMEM)
SMEM = pl.BlockSpec(memory_space=pltpu.SMEM)


def send(block, pairs):
    return lax.ppermute(block, "seq", pairs)


def after(value, *events):
    return lax.optimization_barrier((value,) + events)[0]


def device_index():
    return lax.axis_index("seq").astype(jnp.int32).reshape(1)


def block_of(device, place, other):
    r2, r1, low, high = place
    owner = device ^ other
    parity = owner & 1
    dx = r1 + parity * (r2 - r1)
    dy = r2 + parity * (r1 - r2)
    return owner ^ (16 * high + 8 * low + 4 * dy + 2 * dx)


def edge_swaps(block, parity):
    width = DILATION_STEP
    last = block.shape[1] - width
    inside = lax.dynamic_slice_in_dim(block, (1 - parity) * last, width, axis=1)
    outside = lax.dynamic_slice_in_dim(block, parity * last, width, axis=1)
    return send(inside, CORE), send(outside, OUTER)


def fold(inputs, outputs):
    def kernel(*refs):
        sources, targets = refs[: len(inputs)], refs[len(inputs) :]
        for target, (dtype, _, _, pieces) in zip(targets, outputs):
            for added, (m, m_count), (n, n_count), to_m, to_n in pieces:
                total = None
                for source in added:
                    value = sources[source][m : m + m_count, n : n + n_count]
                    value = value.astype(jnp.float32)
                    total = value if total is None else total + value
                target[to_m : to_m + m_count, to_n : to_n + n_count] = total.astype(dtype)

    tail = inputs[0].shape[2:]
    return pl.pallas_call(
        kernel,
        out_shape=[
            jax.ShapeDtypeStruct((m, n) + tail, dtype) for dtype, m, n, pieces in outputs
        ],
        in_specs=[VMEM] * len(inputs),
        out_specs=[VMEM] * len(outputs),
        compiler_params=pltpu.CompilerParams(vmem_limit_bytes=12 << 20),
        name="fold",
    )(*inputs)


def assemble(inputs, outputs):
    def kernel(*refs):
        sources, targets = refs[: len(inputs)], refs[len(inputs) :]
        for target, (_, _, pieces) in zip(targets, outputs):
            for source, start, count, to_m, to_n in pieces:
                n = sources[source].shape[1]
                target[to_m : to_m + count, to_n : to_n + n] = sources[source][
                    start : start + count
                ]

    tail = inputs[0].shape[2:]
    return pl.pallas_call(
        kernel,
        out_shape=[
            jax.ShapeDtypeStruct((m, n) + tail, inputs[0].dtype) for m, n, pieces in outputs
        ],
        in_specs=[VMEM] * len(inputs),
        out_specs=[VMEM] * len(outputs),
        compiler_params=pltpu.CompilerParams(vmem_limit_bytes=8 << 20),
        name="assemble",
    )(*inputs)


GELU_SCALE = math.sqrt(2.0 / math.pi)
GELU_CUBE = 0.044715


def edge_places(device, bins):
    parity = device & 1
    beyond = bins + DILATION_STEP
    core_at = pl.multiple_of((1 - parity) * beyond, DILATION_STEP)
    outer_at = pl.multiple_of(parity * beyond, DILATION_STEP)
    return core_at, outer_at


def prepare_kernel(
    index_ref,
    features_ref,
    core_ref,
    outer_ref,
    cotangent_ref,
    gain_ref,
    taps_ref,
    project_ref,
    active,
    turned,
):
    device = index_ref[0]
    batch, bins, channels = features_ref.shape
    rows = taps_ref.shape[4]
    width = DILATION_STEP
    gain = gain_ref[...]
    core_at, outer_at = edge_places(device, bins)

    def activate(x):
        x = x.astype(jnp.float32)
        inverse = lax.rsqrt(jnp.sum(x * x, axis=-1, keepdims=True) * (1.0 / channels) + eps)
        v = x * inverse * gain
        t = jnp.tanh(GELU_SCALE * (v + GELU_CUBE * (v * v * v)))
        return (0.5 * v * (1.0 + t)).astype(jnp.bfloat16)

    for b in range(batch):

        def some_rows(i, carry):
            at = pl.multiple_of(i * width, width)
            rows_of = activate(features_ref[b, pl.ds(at, width), :])
            active[b, pl.ds(pl.multiple_of(at + width, width), width), :] = rows_of
            return carry

        lax.fori_loop(0, bins // width, some_rows, 0)
        active[b, pl.ds(core_at, width), :] = activate(core_ref[b])
        active[b, pl.ds(outer_at, width), :] = activate(outer_ref[b])

    def blocks(order):
        for other in BITS:
            for at, where in enumerate(order):
                start = pl.multiple_of(block_of(device, where, other) * rows, 16)
                yield other, at, turned[pl.ds(start, rows), :]

    for tap in range(KERNEL_TAPS):
        for b in range(batch):
            turned[:, b * bins : (b + 1) * bins] = active[
                b, tap * DILATION_STEP : tap * DILATION_STEP + bins, :
            ].T
        for other, at, block in blocks(TAP_ORDERS[tap]):
            taps_ref[other, at // HALF, tap, at % HALF] = block
    turned[...] = cotangent_ref[...].T
    for other, at, block in blocks(PROJECT_ORDER):
        project_ref[other, at // HALF, 0, at % HALF] = block


def prepare(features, edges_of, cotangent, gain, rows):
    tokens, channels = cotangent.shape
    batch, bins, _ = features.shape
    shape = lambda count: jax.ShapeDtypeStruct((2, 2, count, HALF, rows, tokens), cotangent.dtype)
    return pl.pallas_call(
        prepare_kernel,
        out_shape=[shape(KERNEL_TAPS), shape(1)],
        in_specs=[SMEM] + [VMEM] * 5,
        out_specs=[VMEM] * 2,
        scratch_shapes=[
            pltpu.VMEM((batch, bins + 2 * DILATION_STEP, channels), jnp.bfloat16),
            pltpu.VMEM((channels, tokens), jnp.bfloat16),
        ],
        compiler_params=pltpu.CompilerParams(vmem_limit_bytes=16 << 20),
        name="prepare",
    )(device_index(), features, *edges_of, cotangent, gain.reshape(1, channels))


def place_products(device, parts, turned, orders, placed):
    rows, inner = parts[0].shape[2:]
    for other in BITS:
        for which in BITS:
            part = parts[2 * other + which]
            for matrix, right in enumerate(turned):
                product = jnp.dot(
                    part[matrix].reshape(HALF * rows, inner),
                    right,
                    preferred_element_type=jnp.float32,
                )
                for at in range(HALF):
                    block = block_of(device, orders[matrix][which * HALF + at], other)
                    target = pl.ds(pl.multiple_of(block * rows, 16), rows)
                    rows_of = product[at * rows : (at + 1) * rows]
                    if matrix == 0:
                        placed[target, :] = rows_of
                    else:
                        placed[target, :] += rows_of


def project_back_kernel(index_ref, hidden_ref, features_ref, *refs):
    parts, out_ref, placed = refs[:4], refs[4], refs[5]
    place_products(index_ref[0], parts, [hidden_ref[...].T], [PROJECT_ORDER], placed)
    out_ref[...] = (features_ref[...].astype(jnp.float32) + placed[...].T).astype(jnp.bfloat16)


def project_back(hidden, features, parts):
    return pl.pallas_call(
        project_back_kernel,
        out_shape=jax.ShapeDtypeStruct(features.shape, features.dtype),
        in_specs=[SMEM] + [VMEM] * 6,
        out_specs=VMEM,
        scratch_shapes=[pltpu.VMEM(features.shape[::-1], jnp.float32)],
        compiler_params=pltpu.CompilerParams(vmem_limit_bytes=16 << 20),
        name="project_back",
    )(device_index(), hidden, features, *parts)


def grad_active_kernel(index_ref, grad_ref, core_ref, outer_ref, *refs):
    parts, (out_ref, padded_ref, placed) = refs[:4], refs[4:]
    batch, padded_bins, _ = padded_ref.shape
    bins = padded_bins - 2 * DILATION_STEP
    core_at, outer_at = edge_places(index_ref[0], bins)
    for b in range(batch):
        padded_ref[b, DILATION_STEP : DILATION_STEP + bins] = grad_ref[b * bins : (b + 1) * bins]
        padded_ref[b, pl.ds(core_at, DILATION_STEP), :] = core_ref[b]
        padded_ref[b, pl.ds(outer_at, DILATION_STEP), :] = outer_ref[b]
    turned = []
    for tap in range(KERNEL_TAPS):
        shift = (KERNEL_TAPS - 1 - tap) * DILATION_STEP
        turned.append(
            jnp.concatenate([padded_ref[b, shift : shift + bins] for b in range(batch)], axis=0).T
        )
    place_products(index_ref[0], parts, turned, TAP_ORDERS, placed)
    out_ref[...] = placed[...].T


def grad_of_active(grad, edges_of, parts):
    tokens, inner = grad.shape
    batch = edges_of[0].shape[0]
    channels = 2 * BLOCKS * parts[0].shape[2]
    return pl.pallas_call(
        grad_active_kernel,
        out_shape=jax.ShapeDtypeStruct((tokens, channels), jnp.float32),
        in_specs=[SMEM] + [VMEM] * 7,
        out_specs=VMEM,
        scratch_shapes=[
            pltpu.VMEM((batch, tokens // batch + 2 * DILATION_STEP, inner), grad.dtype),
            pltpu.VMEM((channels, tokens), jnp.float32),
        ],
        compiler_params=pltpu.CompilerParams(vmem_limit_bytes=24 << 20),
        name="grad_active",
    )(device_index(), grad, *edges_of, *parts)


def rows_dot(left, right):
    return jnp.einsum("mnrt,ti->mnri", left, right, preferred_element_type=jnp.float32)


def contract(left, right):
    return jnp.einsum(
        "ct,ci->ti",
        left.reshape(-1, left.shape[-1]),
        right.reshape(-1, right.shape[-1]),
        preferred_element_type=jnp.float32,
    )


def body_torus(features, cotangent, dilated_kernel_weight, project_weight, outer_gain, inner_gain):
    batch, bin_count, channels = features.shape
    inner = project_weight.shape[1]
    rows = project_weight.shape[0]
    tokens = batch * bin_count
    factor = 1.0 / math.sqrt(tokens * TORUS_DEVICES)
    as_bf16 = lambda value: value.astype(jnp.bfloat16)
    as_f32 = lambda value: value.astype(jnp.float32)

    taps = jnp.moveaxis(dilated_kernel_weight, 1, 0)[:, None]
    pair = taps[:2]
    rest = jnp.concatenate([taps[2:], project_weight[None, None]])
    pair_in, rest_in = send(pair, Z_FAR), send(rest, FIRST)
    pair, last, proj = assemble(
        (pair, pair_in, rest, rest_in),
        (
            (2, 2, ((0, 0, 2, 0, 0), (1, 0, 2, 0, 1))),
            (1, 2, ((2, 0, 1, 0, 0), (3, 0, 1, 0, 1))),
            (1, 2, ((2, 1, 1, 0, 0), (3, 1, 1, 0, 1))),
        ),
    )
    pair_in, last_in, proj_b = send(pair, Z_NEAR), send(last, Z_FAR), send(proj, SECOND)
    parity = lax.axis_index("seq") & 1
    feature_edges = edge_swaps(after(features, pair), parity)
    grow = lambda m, n, a: (m, 2 * n, ((a, 0, m, 0, 0), (a + 1, 0, m, 0, n)))
    pair_in = after(pair_in, proj_b, *feature_edges)
    pair, last = assemble((pair, pair_in, last, last_in), (grow(2, 2, 0), grow(1, 2, 2)))
    pair_in, last_in, proj_in = send(pair, FIRST), send(last, Z_NEAR), send(proj, Z_FAR)
    near, proj_a = assemble(
        (pair, pair_in, last, last_in, proj, proj_in),
        (
            (3, 8, ((0, 0, 2, 0, 0), (1, 0, 2, 0, 4), (2, 0, 1, 2, 0), (3, 0, 1, 2, 4))),
            grow(1, 2, 4),
        ),
    )
    far, near_other = send(near, SECOND), send(near, CORE)
    proj_in, proj_b_in = send(proj_a, Z_NEAR), send(proj_b, Z_FAR)
    flat_cotangent = cotangent.reshape(tokens, channels)
    act, act_p = prepare(
        after(features, near), feature_edges, flat_cotangent, outer_gain, rows
    )
    proj_a, proj_b = assemble(
        (proj_a, after(proj_in, act), proj_b, proj_b_in), (grow(1, 4, 0), grow(1, 2, 2))
    )
    proj_b_in, proj_a_other = send(proj_b, Z_NEAR), send(proj_a, CORE)
    conv_output = contract(act[0, 0], after(near, proj_b)) + contract(act[1, 0], near_other)
    grad_hidden = contract(act_p[0, 0], after(proj_a, conv_output)) + contract(
        act_p[1, 0], proj_a_other
    )
    (proj_b,) = assemble((proj_b, after(proj_b_in, grad_hidden)), (grow(1, 4, 0),))
    proj_b_other = send(proj_b, CORE)
    far = after(far, proj_b)
    far_other = send(far, CORE)
    conv_output = conv_output + contract(act[0, 1], far) + contract(act[1, 1], far_other)
    grad_hidden = (
        grad_hidden + contract(act_p[0, 1], proj_b) + contract(act_p[1, 1], proj_b_other)
    )
    hidden32, pull_inner = jax.vjp(act_norm, conv_output, inner_gain)
    hidden = as_bf16(hidden32)
    give_p = as_bf16(rows_dot(act_p[1].reshape(2, HALF, rows, tokens), hidden))
    recv_p = send(give_p, CORE)
    grad_conv, grad_gain_inner = pull_inner(after(grad_hidden, give_p))
    grad_conv = as_bf16(grad_conv)

    give = as_bf16(rows_dot(act[1, 1], grad_conv))
    recv_far = send(give, CORE)
    give = as_bf16(rows_dot(act[1, 0], after(grad_conv, give)))
    recv_near = send(give, CORE)
    grad_edges = edge_swaps(after(grad_conv, give).reshape(batch, bin_count, inner), parity)
    message = as_bf16(rows_dot(act[0, 1], after(grad_conv, give)) + as_f32(recv_far))
    recv = send(message, SECOND)
    grad_p = after(hidden, message)
    split = lambda which: act_p[0, which].reshape(2, HALF // 2, rows, tokens)
    parts_of = lambda array, which: array[which].reshape(2, HALF // 2, rows, inner)
    message_b = as_bf16(
        rows_dot(split(1)[1:], grad_p) + as_f32(parts_of(recv_p, 1)[1:])
    )
    recv_b = send(message_b, Z_NEAR)
    message_a = as_bf16(
        rows_dot(split(0)[1:], grad_p) + as_f32(parts_of(recv_p, 0)[1:])
    )
    grad_p = after(hidden, message_a, message_b)
    kept_b = rows_dot(split(1)[:1], grad_p) + as_f32(parts_of(recv_p, 1)[:1])
    kept_a = rows_dot(split(0)[:1], grad_p) + as_f32(parts_of(recv_p, 0)[:1])
    kept = rows_dot(act[0, 0], after(grad_conv, kept_a, kept_b)) + as_f32(recv_near)

    flat = features.reshape(tokens, channels)
    grad_active = grad_of_active(
        after(grad_conv, kept), grad_edges, (near, far, near_other, far_other)
    )
    f32, bf16 = jnp.float32, jnp.bfloat16
    recv_b = after(recv_b, grad_active)
    message_b, kept_b = fold(
        (kept_b, recv_b),
        (
            (bf16, 1, 2, (((0, 1), (0, 1), (2, 2), 0, 0),)),
            (f32, 1, 2, (((0, 1), (0, 1), (0, 2), 0, 0),)),
        ),
    )
    recv_b = send(message_b, Z_FAR)
    recv_a = send(after(message_a, message_b), Z_NEAR)
    unused, pull_outer = jax.vjp(act_norm, as_f32(after(features, message_b)), outer_gain)
    grad_branch, grad_gain_outer = pull_outer(grad_active.reshape(features.shape))
    grad_features = as_bf16(as_f32(cotangent) + grad_branch)
    gains = jnp.concatenate([grad_gain_outer, grad_gain_inner]) * factor
    gains = gains + send(gains, CORE)

    recv_a = after(recv_a, gains)
    message, message_l, message_a, message_p, kept, kept_l, kept_a, kept_b = fold(
        (kept, recv, kept_a, recv_a, kept_b, recv_b),
        (
            (bf16, 2, 4, (((0, 1), (0, 2), (4, 4), 0, 0),)),
            (bf16, 1, 4, (((0, 1), (2, 1), (4, 4), 0, 0),)),
            (bf16, 1, 2, (((2, 3), (0, 1), (2, 2), 0, 0),)),
            (bf16, 1, 2, (((4, 5), (0, 1), (0, 2), 0, 0),)),
            (f32, 2, 4, (((0, 1), (0, 2), (0, 4), 0, 0),)),
            (f32, 1, 4, (((0, 1), (2, 1), (0, 4), 0, 0),)),
            (f32, 1, 2, (((2, 3), (0, 1), (0, 2), 0, 0),)),
            (f32, 1, 2, (((4, 5), (0, 1), (0, 2), 0, 0),)),
        ),
    )
    recv, recv_l, recv_a = send(message, FIRST), send(message_l, Z_NEAR), send(message_a, Z_FAR)
    gains = after(gains, message)
    gains = gains + send(gains, links(lambda i: i ^ 2))
    block_out = project_back(
        after(hidden, message), flat, (proj_a, proj_b, proj_a_other, proj_b_other)
    ).reshape(features.shape)
    gains = after(gains, block_out)

    recv = after(recv, gains)
    message, message_l, kept, kept_l, kept_p = fold(
        (kept, recv, kept_l, recv_l, kept_a, recv_a),
        (
            (bf16, 2, 2, (((0, 1), (0, 2), (2, 2), 0, 0),)),
            (bf16, 1, 2, (((2, 3), (0, 1), (2, 2), 0, 0),)),
            (f32, 2, 2, (((0, 1), (0, 2), (0, 2), 0, 0),)),
            (f32, 1, 2, (((2, 3), (0, 1), (0, 2), 0, 0),)),
            (f32, 1, 2, (((4, 5), (0, 1), (0, 2), 0, 0),)),
        ),
    )
    message_p = after(message_p, message)
    recv, recv_l, recv_p = send(message, Z_NEAR), send(message_l, Z_FAR), send(message_p, SECOND)
    gains = after(gains, message)
    gains = gains + send(gains, links(lambda i: i ^ 4))

    recv = after(recv, gains)
    message, message_r, kept, kept_r = fold(
        (kept, recv, kept_l, recv_l, kept_p, recv_p),
        (
            (bf16, 2, 1, (((0, 1), (0, 2), (1, 1), 0, 0),)),
            (bf16, 2, 1, (((2, 3), (0, 1), (1, 1), 0, 0), ((4, 5), (0, 1), (1, 1), 1, 0))),
            (f32, 2, 1, (((0, 1), (0, 2), (0, 1), 0, 0),)),
            (f32, 2, 1, (((2, 3), (0, 1), (0, 1), 0, 0), ((4, 5), (0, 1), (0, 1), 1, 0))),
        ),
    )
    recv, recv_r = send(message, Z_FAR), send(message_r, FIRST)
    gains = after(gains, message)
    gains = gains + send(gains, Z_NEAR)
    gains = gains + send(gains, Z_FAR)

    sums = kept + as_f32(recv)
    sums_r = kept_r + as_f32(recv_r)
    grad_project = sums_r[1, 0] * factor
    grad_dilated = jnp.stack([sums[0, 0], sums[1, 0], sums_r[0, 0]], axis=1) * factor

    device = lax.axis_index("seq")
    grad_outer_gain = lax.dynamic_slice(gains, (device * rows,), (rows,))
    part = inner // TORUS_DEVICES
    grad_inner_gain = lax.dynamic_slice(gains, (channels + device * part,), (part,))
    return (block_out, grad_features, grad_dilated, grad_project, grad_outer_gain, grad_inner_gain)


def body(*operands):
    if lax.axis_size("seq") == TORUS_DEVICES:
        return body_torus(*operands)
    return body_any(*operands)


def solution(mesh):
    return jax.shard_map(
        body,
        mesh=mesh,
        in_specs=(
            P("groups", "seq", None),
            P("groups", "seq", None),
            P("seq", None, None),
            P("seq", None),
            P(),
            P(),
        ),
        out_specs=(
            P("groups", "seq", None),
            P("groups", "seq", None),
            P(("groups", "seq"), None, None),
            P(("groups", "seq"), None),
            P(("groups", "seq")),
            P(("groups", "seq")),
        ),
        check_vma=False,
    )
```

```python
import math

import jax
import jax.numpy as jnp
from jax import lax
from jax.experimental import pallas as pl
from jax.experimental.pallas import tpu as pltpu
from jax.sharding import PartitionSpec as P

KERNEL_TAPS = 3
DILATION_STEP = 32
TORUS_DEVICES = 32


eps = 1e-06


def padded(block, sides, width):
    for axis, dim in sides:
        count = lax.axis_size(axis)
        forward = [(i, i + 1) for i in range(count - 1)]
        backward = [(target, source) for source, target in forward]
        low = lax.ppermute(
            lax.slice_in_dim(block, block.shape[dim] - width, None, axis=dim), axis, forward
        )
        high = lax.ppermute(lax.slice_in_dim(block, 0, width, axis=dim), axis, backward)
        block = jnp.concatenate([low, block, high], axis=dim)
    return block


def act_norm(values, gain):
    meansq = jnp.mean(values * values, axis=-1, keepdims=True)
    return jax.nn.gelu(values * lax.rsqrt(meansq + eps) * gain, approximate=True)


def reduce_dilated(padded_input, conv_output_gradient, factor):
    bin_count = conv_output_gradient.shape[1]
    tap_slices = [
        jnp.einsum(
            "btc,bti->ci",
            padded_input[:, tap_index * DILATION_STEP : tap_index * DILATION_STEP + bin_count],
            conv_output_gradient,
            preferred_element_type=jnp.float32,
        )
        for tap_index in range(KERNEL_TAPS)
    ]
    return lax.psum_scatter(
        jnp.stack(tap_slices, axis=1) * factor, "seq", scatter_dimension=0, tiled=True
    )


def body_any(features, cotangent, dilated_kernel_weight, project_weight, outer_gain, inner_gain):
    bin_count = features.shape[1]
    factor = 1.0 / math.sqrt(features.shape[0] * bin_count * lax.axis_size("seq"))
    full_dilated = lax.all_gather(dilated_kernel_weight, "seq", axis=0, tiled=True)
    full_project = lax.all_gather(project_weight, "seq", axis=0, tiled=True)
    as_float = features.astype(jnp.float32)
    active_features = act_norm(as_float, outer_gain).astype(jnp.bfloat16)
    padded_input = padded(active_features, (("seq", 1),), DILATION_STEP)
    conv_output = jnp.einsum(
        "btc,ci->bti",
        padded_input[:, 0:bin_count],
        full_dilated[:, 0, :],
        preferred_element_type=jnp.float32,
    )
    for tap_index in range(1, KERNEL_TAPS):
        conv_output = conv_output + jnp.einsum(
            "btc,ci->bti",
            padded_input[:, tap_index * DILATION_STEP : tap_index * DILATION_STEP + bin_count],
            full_dilated[:, tap_index, :],
            preferred_element_type=jnp.float32,
        )
    hidden = act_norm(conv_output, inner_gain).astype(jnp.bfloat16)
    block_out = (
        as_float
        + jnp.einsum("bti,ci->btc", hidden, full_project, preferred_element_type=jnp.float32)
    ).astype(jnp.bfloat16)
    grad_hidden = jnp.einsum(
        "btc,ci->bti", cotangent, full_project, preferred_element_type=jnp.float32
    )
    unused, pull_inner = jax.vjp(act_norm, conv_output, inner_gain)
    conv_output_gradient, grad_gain_inner = pull_inner(grad_hidden)
    conv_output_gradient = conv_output_gradient.astype(jnp.bfloat16)
    padded_input_gradient = padded(conv_output_gradient, (("seq", 1),), DILATION_STEP)
    grad_active = jnp.zeros(features.shape, jnp.float32)
    for tap_index in range(KERNEL_TAPS):
        tap_shift = (KERNEL_TAPS - 1 - tap_index) * DILATION_STEP
        grad_active = grad_active + jnp.einsum(
            "bti,ci->btc",
            padded_input_gradient[:, tap_shift : tap_shift + bin_count],
            full_dilated[:, tap_index, :],
            preferred_element_type=jnp.float32,
        )
    unused_two, pull_outer = jax.vjp(act_norm, as_float, outer_gain)
    grad_branch, grad_gain_outer = pull_outer(grad_active)
    grad_features = (cotangent.astype(jnp.float32) + grad_branch).astype(jnp.bfloat16)
    grad_dilated = reduce_dilated(padded_input, conv_output_gradient, factor)
    grad_project = lax.psum_scatter(
        jnp.einsum("btc,bti->ci", cotangent, hidden, preferred_element_type=jnp.float32) * factor,
        "seq",
        scatter_dimension=0,
        tiled=True,
    )
    grad_outer_gain, grad_inner_gain = (
        lax.psum_scatter(grad_gain_outer * factor, "seq", scatter_dimension=0, tiled=True),
        lax.psum_scatter(grad_gain_inner * factor, "seq", scatter_dimension=0, tiled=True),
    )
    return (block_out, grad_features, grad_dilated, grad_project, grad_outer_gain, grad_inner_gain)


def links(move):
    return [(i, move(i)) for i in range(TORUS_DEVICES)]


CORE = links(lambda i: i ^ 1)
FIRST = links(lambda i: i ^ (4 if i & 1 else 2))
SECOND = links(lambda i: i ^ (2 if i & 1 else 4))
Z_NEAR = links(lambda i: i ^ 8)
Z_FAR = links(lambda i: i ^ 16)

BITS = (0, 1)
PAIR_ORDER = [(r2, r1, low, high) for r2 in BITS for r1 in BITS for low in BITS for high in BITS]
LAST_ORDER = [(r2, r1, low, high) for r2 in BITS for low in BITS for high in BITS for r1 in BITS]
TAP_ORDERS = [PAIR_ORDER, PAIR_ORDER, LAST_ORDER]
PROJECT_ORDER = LAST_ORDER
BLOCKS = 16
HALF = 8

OUTER = [
    (i, j)
    for odd in range(1, TORUS_DEVICES - 1, 2)
    for i, j in ((odd, odd + 1), (odd + 1, odd))
]

VMEM = pl.BlockSpec(memory_space=pltpu.VMEM)
SMEM = pl.BlockSpec(memory_space=pltpu.SMEM)


def send(block, pairs):
    return lax.ppermute(block, "seq", pairs)


def after(value, *events):
    return lax.optimization_barrier((value,) + events)[0]


def device_index():
    return lax.axis_index("seq").astype(jnp.int32).reshape(1)


def block_of(device, place, other):
    r2, r1, low, high = place
    owner = device ^ other
    parity = owner & 1
    dx = r1 + parity * (r2 - r1)
    dy = r2 + parity * (r1 - r2)
    return owner ^ (16 * high + 8 * low + 4 * dy + 2 * dx)


def edge_swaps(block, parity):
    width = DILATION_STEP
    last = block.shape[1] - width
    inside = lax.dynamic_slice_in_dim(block, (1 - parity) * last, width, axis=1)
    outside = lax.dynamic_slice_in_dim(block, parity * last, width, axis=1)
    return send(inside, CORE), send(outside, OUTER)


def fold(inputs, outputs):
    def kernel(*refs):
        sources, targets = refs[: len(inputs)], refs[len(inputs) :]
        for target, (dtype, _, _, pieces) in zip(targets, outputs):
            for added, (m, m_count), (n, n_count), to_m, to_n in pieces:
                total = None
                for source in added:
                    value = sources[source][m : m + m_count, n : n + n_count]
                    value = value.astype(jnp.float32)
                    total = value if total is None else total + value
                target[to_m : to_m + m_count, to_n : to_n + n_count] = total.astype(dtype)

    tail = inputs[0].shape[2:]
    return pl.pallas_call(
        kernel,
        out_shape=[
            jax.ShapeDtypeStruct((m, n) + tail, dtype) for dtype, m, n, pieces in outputs
        ],
        in_specs=[VMEM] * len(inputs),
        out_specs=[VMEM] * len(outputs),
        compiler_params=pltpu.CompilerParams(vmem_limit_bytes=12 << 20),
        name="fold",
    )(*inputs)


def assemble(inputs, outputs):
    def kernel(*refs):
        sources, targets = refs[: len(inputs)], refs[len(inputs) :]
        for target, (_, _, pieces) in zip(targets, outputs):
            for source, start, count, to_m, to_n in pieces:
                n = sources[source].shape[1]
                target[to_m : to_m + count, to_n : to_n + n] = sources[source][
                    start : start + count
                ]

    tail = inputs[0].shape[2:]
    return pl.pallas_call(
        kernel,
        out_shape=[
            jax.ShapeDtypeStruct((m, n) + tail, inputs[0].dtype) for m, n, pieces in outputs
        ],
        in_specs=[VMEM] * len(inputs),
        out_specs=[VMEM] * len(outputs),
        compiler_params=pltpu.CompilerParams(vmem_limit_bytes=8 << 20),
        name="assemble",
    )(*inputs)


GELU_SCALE = math.sqrt(2.0 / math.pi)
GELU_CUBE = 0.044715


def edge_places(device, bins):
    parity = device & 1
    beyond = bins + DILATION_STEP
    core_at = pl.multiple_of((1 - parity) * beyond, DILATION_STEP)
    outer_at = pl.multiple_of(parity * beyond, DILATION_STEP)
    return core_at, outer_at


def prepare_kernel(
    index_ref,
    features_ref,
    cotangent_ref,
    gain_ref,
    *refs,
):
    device = index_ref[0]
    batch, bins, channels = features_ref.shape
    core_refs, outer_refs = refs[:batch], refs[batch : 2 * batch]
    taps_ref, project_ref, active, turned = refs[2 * batch :]
    rows = taps_ref.shape[4]
    width = DILATION_STEP
    gain = gain_ref[...]
    core_at, outer_at = edge_places(device, bins)

    def activate(x):
        x = x.astype(jnp.float32)
        inverse = lax.rsqrt(jnp.sum(x * x, axis=-1, keepdims=True) * (1.0 / channels) + eps)
        v = x * inverse * gain
        t = jnp.tanh(GELU_SCALE * (v + GELU_CUBE * (v * v * v)))
        return (0.5 * v * (1.0 + t)).astype(jnp.bfloat16)

    for b in range(batch):

        def some_rows(i, carry):
            at = pl.multiple_of(i * width, width)
            rows_of = activate(features_ref[b, pl.ds(at, width), :])
            active[b, pl.ds(pl.multiple_of(at + width, width), width), :] = rows_of
            return carry

        lax.fori_loop(0, bins // width, some_rows, 0)
        active[b, pl.ds(core_at, width), :] = activate(core_refs[b][0])
        active[b, pl.ds(outer_at, width), :] = activate(outer_refs[b][0])

    def blocks(order):
        for other in BITS:
            for at, where in enumerate(order):
                start = pl.multiple_of(block_of(device, where, other) * rows, 16)
                yield other, at, turned[pl.ds(start, rows), :]

    for tap in range(KERNEL_TAPS):
        for b in range(batch):
            turned[:, b * bins : (b + 1) * bins] = active[
                b, tap * DILATION_STEP : tap * DILATION_STEP + bins, :
            ].T
        for other, at, block in blocks(TAP_ORDERS[tap]):
            taps_ref[other, at // HALF, tap, at % HALF] = block
    turned[...] = cotangent_ref[...].T
    for other, at, block in blocks(PROJECT_ORDER):
        project_ref[other, at // HALF, 0, at % HALF] = block


def prepare(features, edges_of, cotangent, gain, rows):
    tokens, channels = cotangent.shape
    batch, bins, _ = features.shape
    shape = lambda count: jax.ShapeDtypeStruct((2, 2, count, HALF, rows, tokens), cotangent.dtype)
    return pl.pallas_call(
        prepare_kernel,
        out_shape=[shape(KERNEL_TAPS), shape(1)],
        in_specs=[SMEM] + [VMEM] * (3 + 2 * batch),
        out_specs=[VMEM] * 2,
        scratch_shapes=[
            pltpu.VMEM((batch, bins + 2 * DILATION_STEP, channels), jnp.bfloat16),
            pltpu.VMEM((channels, tokens), jnp.bfloat16),
        ],
        compiler_params=pltpu.CompilerParams(vmem_limit_bytes=16 << 20),
        name="prepare",
    )(device_index(), features, cotangent, gain.reshape(1, channels), *edges_of)


def place_products(device, parts, turned, orders, placed):
    rows, inner = parts[0].shape[2:]
    for other in BITS:
        for which in BITS:
            part = parts[2 * other + which]
            for matrix, right in enumerate(turned):
                product = jnp.dot(
                    part[matrix].reshape(HALF * rows, inner),
                    right,
                    preferred_element_type=jnp.float32,
                )
                for at in range(HALF):
                    block = block_of(device, orders[matrix][which * HALF + at], other)
                    target = pl.ds(pl.multiple_of(block * rows, 16), rows)
                    rows_of = product[at * rows : (at + 1) * rows]
                    if matrix == 0:
                        placed[target, :] = rows_of
                    else:
                        placed[target, :] += rows_of


def project_back_kernel(index_ref, hidden_ref, features_ref, *refs):
    parts, out_ref, placed = refs[:4], refs[4], refs[5]
    place_products(index_ref[0], parts, [hidden_ref[...].T], [PROJECT_ORDER], placed)
    out_ref[...] = (features_ref[...].astype(jnp.float32) + placed[...].T).astype(jnp.bfloat16)


def project_back(hidden, features, parts):
    return pl.pallas_call(
        project_back_kernel,
        out_shape=jax.ShapeDtypeStruct(features.shape, features.dtype),
        in_specs=[SMEM] + [VMEM] * 6,
        out_specs=VMEM,
        scratch_shapes=[pltpu.VMEM(features.shape[::-1], jnp.float32)],
        compiler_params=pltpu.CompilerParams(vmem_limit_bytes=16 << 20),
        name="project_back",
    )(device_index(), hidden, features, *parts)


def grad_active_kernel(index_ref, grad_ref, core_ref, outer_ref, *refs):
    parts, (out_ref, padded_ref, placed) = refs[:4], refs[4:]
    batch, padded_bins, _ = padded_ref.shape
    bins = padded_bins - 2 * DILATION_STEP
    core_at, outer_at = edge_places(index_ref[0], bins)
    for b in range(batch):
        padded_ref[b, DILATION_STEP : DILATION_STEP + bins] = grad_ref[b * bins : (b + 1) * bins]
        padded_ref[b, pl.ds(core_at, DILATION_STEP), :] = core_ref[b]
        padded_ref[b, pl.ds(outer_at, DILATION_STEP), :] = outer_ref[b]
    turned = []
    for tap in range(KERNEL_TAPS):
        shift = (KERNEL_TAPS - 1 - tap) * DILATION_STEP
        turned.append(
            jnp.concatenate([padded_ref[b, shift : shift + bins] for b in range(batch)], axis=0).T
        )
    place_products(index_ref[0], parts, turned, TAP_ORDERS, placed)
    out_ref[...] = placed[...].T


def grad_of_active(grad, edges_of, parts):
    tokens, inner = grad.shape
    batch = edges_of[0].shape[0]
    channels = 2 * BLOCKS * parts[0].shape[2]
    return pl.pallas_call(
        grad_active_kernel,
        out_shape=jax.ShapeDtypeStruct((tokens, channels), jnp.float32),
        in_specs=[SMEM] + [VMEM] * 7,
        out_specs=VMEM,
        scratch_shapes=[
            pltpu.VMEM((batch, tokens // batch + 2 * DILATION_STEP, inner), grad.dtype),
            pltpu.VMEM((channels, tokens), jnp.float32),
        ],
        compiler_params=pltpu.CompilerParams(vmem_limit_bytes=24 << 20),
        name="grad_active",
    )(device_index(), grad, *edges_of, *parts)


def rows_dot(left, right):
    return jnp.einsum("mnrt,ti->mnri", left, right, preferred_element_type=jnp.float32)


def contract(left, right):
    return jnp.einsum(
        "ct,ci->ti",
        left.reshape(-1, left.shape[-1]),
        right.reshape(-1, right.shape[-1]),
        preferred_element_type=jnp.float32,
    )


def body_torus(features, cotangent, dilated_kernel_weight, project_weight, outer_gain, inner_gain):
    batch, bin_count, channels = features.shape
    inner = project_weight.shape[1]
    rows = project_weight.shape[0]
    tokens = batch * bin_count
    factor = 1.0 / math.sqrt(tokens * TORUS_DEVICES)
    as_bf16 = lambda value: value.astype(jnp.bfloat16)
    as_f32 = lambda value: value.astype(jnp.float32)

    taps = jnp.moveaxis(dilated_kernel_weight, 1, 0)[:, None]
    pair = taps[:2]
    rest = jnp.concatenate([taps[2:], project_weight[None, None]])
    pair_in, rest_in = send(pair, Z_FAR), send(rest, FIRST)
    pair, last, proj = assemble(
        (pair, pair_in, rest, rest_in),
        (
            (2, 2, ((0, 0, 2, 0, 0), (1, 0, 2, 0, 1))),
            (1, 2, ((2, 0, 1, 0, 0), (3, 0, 1, 0, 1))),
            (1, 2, ((2, 1, 1, 0, 0), (3, 1, 1, 0, 1))),
        ),
    )
    pair_in, last_in, proj_b = send(pair, Z_NEAR), send(last, Z_FAR), send(proj, SECOND)
    parity = lax.axis_index("seq") & 1
    feature_edges = list(
        zip(*(edge_swaps(after(features, pair)[b : b + 1], parity) for b in range(batch)))
    )
    feature_edges = [array for side in feature_edges for array in side]
    grow = lambda m, n, a: (m, 2 * n, ((a, 0, m, 0, 0), (a + 1, 0, m, 0, n)))
    pair_in = after(pair_in, proj_b, *feature_edges)
    pair, last = assemble((pair, pair_in, last, last_in), (grow(2, 2, 0), grow(1, 2, 2)))
    pair_in, last_in, proj_in = send(pair, FIRST), send(last, Z_NEAR), send(proj, Z_FAR)
    (proj_a,) = assemble((proj, proj_in), (grow(1, 2, 0),))
    (near,) = assemble(
        after((pair, pair_in, last, last_in), proj_a),
        ((3, 8, ((0, 0, 2, 0, 0), (1, 0, 2, 0, 4), (2, 0, 1, 2, 0), (3, 0, 1, 2, 4))),),
    )
    far, near_other = send(near, SECOND), send(near, CORE)
    proj_in, proj_b_in = send(proj_a, Z_NEAR), send(proj_b, Z_FAR)
    flat_cotangent = cotangent.reshape(tokens, channels)
    act, act_p = prepare(
        after(features, near), feature_edges, flat_cotangent, outer_gain, rows
    )
    (proj_b,) = assemble((proj_b, after(proj_b_in, act)), (grow(1, 2, 0),))
    proj_b_in = send(proj_b, Z_NEAR)
    conv_output = contract(act[0, 0], after(near, proj_b))
    (proj_a,) = assemble((proj_a, after(proj_in, conv_output)), (grow(1, 4, 0),))
    proj_a_other = send(proj_a, CORE)
    grad_hidden = contract(act_p[0, 0], proj_a) + contract(act_p[1, 0], proj_a_other)
    (proj_b,) = assemble((proj_b, after(proj_b_in, grad_hidden)), (grow(1, 4, 0),))
    proj_b_other = send(proj_b, CORE)
    far = after(far, conv_output, proj_b)
    conv_output = conv_output + contract(act[1, 0], after(near_other, far))
    far_other = send(far, CORE)
    conv_output = conv_output + contract(act[0, 1], far) + contract(act[1, 1], far_other)
    grad_hidden = (
        grad_hidden + contract(act_p[0, 1], proj_b) + contract(act_p[1, 1], proj_b_other)
    )
    hidden32, pull_inner = jax.vjp(act_norm, conv_output, inner_gain)
    hidden = as_bf16(hidden32)
    grad_conv, grad_gain_inner = pull_inner(grad_hidden)
    grad_conv = as_bf16(grad_conv)

    give = as_bf16(rows_dot(act[1, 1], grad_conv))
    recv_far = send(give, CORE)
    give = as_bf16(rows_dot(act[1, 0], after(grad_conv, give)))
    recv_near = send(give, CORE)
    give = as_bf16(
        rows_dot(act_p[1].reshape(2, HALF, rows, tokens), after(hidden, give))
    )
    recv_p = send(give, CORE)
    grad_edges = edge_swaps(after(grad_conv, give).reshape(batch, bin_count, inner), parity)
    message = as_bf16(rows_dot(act[0, 1], after(grad_conv, give)) + as_f32(recv_far))
    recv = send(message, SECOND)
    grad_p = after(hidden, message)
    split = lambda which: act_p[0, which].reshape(2, HALF // 2, rows, tokens)
    parts_of = lambda array, which: array[which].reshape(2, HALF // 2, rows, inner)
    message_b = as_bf16(
        rows_dot(split(1)[1:], grad_p) + as_f32(parts_of(recv_p, 1)[1:])
    )
    recv_b = send(message_b, Z_NEAR)
    message_a = as_bf16(
        rows_dot(split(0)[1:], grad_p) + as_f32(parts_of(recv_p, 0)[1:])
    )
    grad_p = after(hidden, message_a, message_b)
    kept_b = rows_dot(split(1)[:1], grad_p) + as_f32(parts_of(recv_p, 1)[:1])
    kept_a = rows_dot(split(0)[:1], grad_p) + as_f32(parts_of(recv_p, 0)[:1])
    kept = rows_dot(act[0, 0], after(grad_conv, kept_a, kept_b)) + as_f32(recv_near)

    flat = features.reshape(tokens, channels)
    grad_active = grad_of_active(
        after(grad_conv, kept), grad_edges, (near, far, near_other, far_other)
    )
    f32, bf16 = jnp.float32, jnp.bfloat16
    unused, pull_outer = jax.vjp(act_norm, as_f32(after(features, grad_active)), outer_gain)
    grad_branch, grad_gain_outer = pull_outer(grad_active.reshape(features.shape))
    grad_features = as_bf16(as_f32(cotangent) + grad_branch)
    gains = jnp.concatenate([grad_gain_outer, grad_gain_inner]) * factor
    recv_b = after(recv_b, grad_features, gains)
    message_b, kept_b = fold(
        (kept_b, recv_b),
        (
            (bf16, 1, 2, (((0, 1), (0, 1), (2, 2), 0, 0),)),
            (f32, 1, 2, (((0, 1), (0, 1), (0, 2), 0, 0),)),
        ),
    )
    recv_b = send(message_b, Z_FAR)
    recv_a = send(after(message_a, message_b), Z_NEAR)
    gains = after(gains, message_b)
    gains = gains + send(gains, CORE)

    recv_a = after(recv_a, gains)
    message, message_l, message_a, message_p, kept, kept_l, kept_a, kept_b = fold(
        (kept, recv, kept_a, recv_a, kept_b, recv_b),
        (
            (bf16, 2, 4, (((0, 1), (0, 2), (4, 4), 0, 0),)),
            (bf16, 1, 4, (((0, 1), (2, 1), (4, 4), 0, 0),)),
            (bf16, 1, 2, (((2, 3), (0, 1), (2, 2), 0, 0),)),
            (bf16, 1, 2, (((4, 5), (0, 1), (0, 2), 0, 0),)),
            (f32, 2, 4, (((0, 1), (0, 2), (0, 4), 0, 0),)),
            (f32, 1, 4, (((0, 1), (2, 1), (0, 4), 0, 0),)),
            (f32, 1, 2, (((2, 3), (0, 1), (0, 2), 0, 0),)),
            (f32, 1, 2, (((4, 5), (0, 1), (0, 2), 0, 0),)),
        ),
    )
    recv, recv_l, recv_a = send(message, FIRST), send(message_l, Z_NEAR), send(message_a, Z_FAR)
    gains = after(gains, message)
    gains = gains + send(gains, links(lambda i: i ^ 2))
    block_out = project_back(
        after(hidden, message), flat, (proj_a, proj_b, proj_a_other, proj_b_other)
    ).reshape(features.shape)
    gains = after(gains, block_out)
    gains = gains + send(gains, links(lambda i: i ^ 4))

    recv = after(recv, gains)
    message, message_l, kept, kept_l, kept_p = fold(
        (kept, recv, kept_l, recv_l, kept_a, recv_a),
        (
            (bf16, 2, 2, (((0, 1), (0, 2), (2, 2), 0, 0),)),
            (bf16, 1, 2, (((2, 3), (0, 1), (2, 2), 0, 0),)),
            (f32, 2, 2, (((0, 1), (0, 2), (0, 2), 0, 0),)),
            (f32, 1, 2, (((2, 3), (0, 1), (0, 2), 0, 0),)),
            (f32, 1, 2, (((4, 5), (0, 1), (0, 2), 0, 0),)),
        ),
    )
    message_p = after(message_p, message)
    recv, recv_l, recv_p = send(message, Z_NEAR), send(message_l, Z_FAR), send(message_p, SECOND)
    gains = after(gains, message)
    gains = gains + send(gains, Z_NEAR)

    recv = after(recv, gains)
    message, message_r, kept, kept_r = fold(
        (kept, recv, kept_l, recv_l, kept_p, recv_p),
        (
            (bf16, 2, 1, (((0, 1), (0, 2), (1, 1), 0, 0),)),
            (bf16, 2, 1, (((2, 3), (0, 1), (1, 1), 0, 0), ((4, 5), (0, 1), (1, 1), 1, 0))),
            (f32, 2, 1, (((0, 1), (0, 2), (0, 1), 0, 0),)),
            (f32, 2, 1, (((2, 3), (0, 1), (0, 1), 0, 0), ((4, 5), (0, 1), (0, 1), 1, 0))),
        ),
    )
    recv, recv_r = send(message, Z_FAR), send(message_r, FIRST)
    gains = after(gains, message)
    gains = gains + send(gains, Z_FAR)

    sums = kept + as_f32(recv)
    sums_r = kept_r + as_f32(recv_r)
    grad_project = sums_r[1, 0] * factor
    grad_dilated = jnp.stack([sums[0, 0], sums[1, 0], sums_r[0, 0]], axis=1) * factor

    device = lax.axis_index("seq")
    grad_outer_gain = lax.dynamic_slice(gains, (device * rows,), (rows,))
    part = inner // TORUS_DEVICES
    grad_inner_gain = lax.dynamic_slice(gains, (channels + device * part,), (part,))
    return (block_out, grad_features, grad_dilated, grad_project, grad_outer_gain, grad_inner_gain)


def body(*operands):
    if lax.axis_size("seq") == TORUS_DEVICES:
        return body_torus(*operands)
    return body_any(*operands)


def solution(mesh):
    return jax.shard_map(
        body,
        mesh=mesh,
        in_specs=(
            P("groups", "seq", None),
            P("groups", "seq", None),
            P("seq", None, None),
            P("seq", None),
            P(),
            P(),
        ),
        out_specs=(
            P("groups", "seq", None),
            P("groups", "seq", None),
            P(("groups", "seq"), None, None),
            P(("groups", "seq"), None),
            P(("groups", "seq")),
            P(("groups", "seq")),
        ),
        check_vma=False,
    )
```

```python
import math

import jax
import jax.numpy as jnp
from jax import lax
from jax.experimental import pallas as pl
from jax.experimental.pallas import tpu as pltpu
from jax.sharding import PartitionSpec as P

KERNEL_TAPS = 3
DILATION_STEP = 32
TORUS_DEVICES = 32


eps = 1e-06


def padded(block, sides, width):
    for axis, dim in sides:
        count = lax.axis_size(axis)
        forward = [(i, i + 1) for i in range(count - 1)]
        backward = [(target, source) for source, target in forward]
        low = lax.ppermute(
            lax.slice_in_dim(block, block.shape[dim] - width, None, axis=dim), axis, forward
        )
        high = lax.ppermute(lax.slice_in_dim(block, 0, width, axis=dim), axis, backward)
        block = jnp.concatenate([low, block, high], axis=dim)
    return block


def act_norm(values, gain):
    meansq = jnp.mean(values * values, axis=-1, keepdims=True)
    return jax.nn.gelu(values * lax.rsqrt(meansq + eps) * gain, approximate=True)


def reduce_dilated(padded_input, conv_output_gradient, factor):
    bin_count = conv_output_gradient.shape[1]
    tap_slices = [
        jnp.einsum(
            "btc,bti->ci",
            padded_input[:, tap_index * DILATION_STEP : tap_index * DILATION_STEP + bin_count],
            conv_output_gradient,
            preferred_element_type=jnp.float32,
        )
        for tap_index in range(KERNEL_TAPS)
    ]
    return lax.psum_scatter(
        jnp.stack(tap_slices, axis=1) * factor, "seq", scatter_dimension=0, tiled=True
    )


def body_any(features, cotangent, dilated_kernel_weight, project_weight, outer_gain, inner_gain):
    bin_count = features.shape[1]
    factor = 1.0 / math.sqrt(features.shape[0] * bin_count * lax.axis_size("seq"))
    full_dilated = lax.all_gather(dilated_kernel_weight, "seq", axis=0, tiled=True)
    full_project = lax.all_gather(project_weight, "seq", axis=0, tiled=True)
    as_float = features.astype(jnp.float32)
    active_features = act_norm(as_float, outer_gain).astype(jnp.bfloat16)
    padded_input = padded(active_features, (("seq", 1),), DILATION_STEP)
    conv_output = jnp.einsum(
        "btc,ci->bti",
        padded_input[:, 0:bin_count],
        full_dilated[:, 0, :],
        preferred_element_type=jnp.float32,
    )
    for tap_index in range(1, KERNEL_TAPS):
        conv_output = conv_output + jnp.einsum(
            "btc,ci->bti",
            padded_input[:, tap_index * DILATION_STEP : tap_index * DILATION_STEP + bin_count],
            full_dilated[:, tap_index, :],
            preferred_element_type=jnp.float32,
        )
    hidden = act_norm(conv_output, inner_gain).astype(jnp.bfloat16)
    block_out = (
        as_float
        + jnp.einsum("bti,ci->btc", hidden, full_project, preferred_element_type=jnp.float32)
    ).astype(jnp.bfloat16)
    grad_hidden = jnp.einsum(
        "btc,ci->bti", cotangent, full_project, preferred_element_type=jnp.float32
    )
    unused, pull_inner = jax.vjp(act_norm, conv_output, inner_gain)
    conv_output_gradient, grad_gain_inner = pull_inner(grad_hidden)
    conv_output_gradient = conv_output_gradient.astype(jnp.bfloat16)
    padded_input_gradient = padded(conv_output_gradient, (("seq", 1),), DILATION_STEP)
    grad_active = jnp.zeros(features.shape, jnp.float32)
    for tap_index in range(KERNEL_TAPS):
        tap_shift = (KERNEL_TAPS - 1 - tap_index) * DILATION_STEP
        grad_active = grad_active + jnp.einsum(
            "bti,ci->btc",
            padded_input_gradient[:, tap_shift : tap_shift + bin_count],
            full_dilated[:, tap_index, :],
            preferred_element_type=jnp.float32,
        )
    unused_two, pull_outer = jax.vjp(act_norm, as_float, outer_gain)
    grad_branch, grad_gain_outer = pull_outer(grad_active)
    grad_features = (cotangent.astype(jnp.float32) + grad_branch).astype(jnp.bfloat16)
    grad_dilated = reduce_dilated(padded_input, conv_output_gradient, factor)
    grad_project = lax.psum_scatter(
        jnp.einsum("btc,bti->ci", cotangent, hidden, preferred_element_type=jnp.float32) * factor,
        "seq",
        scatter_dimension=0,
        tiled=True,
    )
    grad_outer_gain, grad_inner_gain = (
        lax.psum_scatter(grad_gain_outer * factor, "seq", scatter_dimension=0, tiled=True),
        lax.psum_scatter(grad_gain_inner * factor, "seq", scatter_dimension=0, tiled=True),
    )
    return (block_out, grad_features, grad_dilated, grad_project, grad_outer_gain, grad_inner_gain)


def links(move):
    return [(i, move(i)) for i in range(TORUS_DEVICES)]


CORE = links(lambda i: i ^ 1)
FIRST = links(lambda i: i ^ (4 if i & 1 else 2))
SECOND = links(lambda i: i ^ (2 if i & 1 else 4))
Z_NEAR = links(lambda i: i ^ 8)
Z_FAR = links(lambda i: i ^ 16)

BITS = (0, 1)
PAIR_ORDER = [(r2, r1, low, high) for r2 in BITS for r1 in BITS for low in BITS for high in BITS]
LAST_ORDER = [(r2, r1, low, high) for r2 in BITS for low in BITS for high in BITS for r1 in BITS]
TAP_ORDERS = [PAIR_ORDER, PAIR_ORDER, LAST_ORDER]
PROJECT_ORDER = LAST_ORDER
BLOCKS = 16
HALF = 8

OUTER = [
    (i, j)
    for odd in range(1, TORUS_DEVICES - 1, 2)
    for i, j in ((odd, odd + 1), (odd + 1, odd))
]

VMEM = pl.BlockSpec(memory_space=pltpu.VMEM)
SMEM = pl.BlockSpec(memory_space=pltpu.SMEM)


def send(block, pairs):
    return lax.ppermute(block, "seq", pairs)


def after(value, *events):
    return lax.optimization_barrier((value,) + events)[0]


def device_index():
    return lax.axis_index("seq").astype(jnp.int32).reshape(1)


def block_of(device, place, other):
    r2, r1, low, high = place
    owner = device ^ other
    parity = owner & 1
    dx = r1 + parity * (r2 - r1)
    dy = r2 + parity * (r1 - r2)
    return owner ^ (16 * high + 8 * low + 4 * dy + 2 * dx)


def edge_swaps(block, parity):
    width = DILATION_STEP
    last = block.shape[1] - width
    inside = lax.dynamic_slice_in_dim(block, (1 - parity) * last, width, axis=1)
    outside = lax.dynamic_slice_in_dim(block, parity * last, width, axis=1)
    return send(inside, CORE), send(outside, OUTER)


def fold(inputs, outputs):
    def kernel(*refs):
        sources, targets = refs[: len(inputs)], refs[len(inputs) :]
        for target, (dtype, _, _, pieces) in zip(targets, outputs):
            for added, (m, m_count), (n, n_count), to_m, to_n in pieces:
                total = None
                for source in added:
                    value = sources[source][m : m + m_count, n : n + n_count]
                    value = value.astype(jnp.float32)
                    total = value if total is None else total + value
                target[to_m : to_m + m_count, to_n : to_n + n_count] = total.astype(dtype)

    tail = inputs[0].shape[2:]
    return pl.pallas_call(
        kernel,
        out_shape=[
            jax.ShapeDtypeStruct((m, n) + tail, dtype) for dtype, m, n, pieces in outputs
        ],
        in_specs=[VMEM] * len(inputs),
        out_specs=[VMEM] * len(outputs),
        compiler_params=pltpu.CompilerParams(vmem_limit_bytes=12 << 20),
        name="fold",
    )(*inputs)


def assemble(inputs, outputs):
    def kernel(*refs):
        sources, targets = refs[: len(inputs)], refs[len(inputs) :]
        for target, (_, _, pieces) in zip(targets, outputs):
            for source, start, count, to_m, to_n in pieces:
                n = sources[source].shape[1]
                target[to_m : to_m + count, to_n : to_n + n] = sources[source][
                    start : start + count
                ]

    tail = inputs[0].shape[2:]
    return pl.pallas_call(
        kernel,
        out_shape=[
            jax.ShapeDtypeStruct((m, n) + tail, inputs[0].dtype) for m, n, pieces in outputs
        ],
        in_specs=[VMEM] * len(inputs),
        out_specs=[VMEM] * len(outputs),
        compiler_params=pltpu.CompilerParams(vmem_limit_bytes=8 << 20),
        name="assemble",
    )(*inputs)


GELU_SCALE = math.sqrt(2.0 / math.pi)
GELU_CUBE = 0.044715


def edge_places(device, bins):
    parity = device & 1
    beyond = bins + DILATION_STEP
    core_at = pl.multiple_of((1 - parity) * beyond, DILATION_STEP)
    outer_at = pl.multiple_of(parity * beyond, DILATION_STEP)
    return core_at, outer_at


def prepare_kernel(
    index_ref,
    features_ref,
    cotangent_ref,
    gain_ref,
    *refs,
):
    device = index_ref[0]
    batch, bins, channels = features_ref.shape
    core_refs, outer_refs = refs[:batch], refs[batch : 2 * batch]
    taps_ref, project_ref, active, turned = refs[2 * batch :]
    rows = taps_ref.shape[4]
    width = DILATION_STEP
    gain = gain_ref[...]
    core_at, outer_at = edge_places(device, bins)

    def activate(x):
        x = x.astype(jnp.float32)
        inverse = lax.rsqrt(jnp.sum(x * x, axis=-1, keepdims=True) * (1.0 / channels) + eps)
        v = x * inverse * gain
        t = jnp.tanh(GELU_SCALE * (v + GELU_CUBE * (v * v * v)))
        return (0.5 * v * (1.0 + t)).astype(jnp.bfloat16)

    for b in range(batch):

        def some_rows(i, carry):
            at = pl.multiple_of(i * width, width)
            rows_of = activate(features_ref[b, pl.ds(at, width), :])
            active[b, pl.ds(pl.multiple_of(at + width, width), width), :] = rows_of
            return carry

        lax.fori_loop(0, bins // width, some_rows, 0)
        active[b, pl.ds(core_at, width), :] = activate(core_refs[b][0])
        active[b, pl.ds(outer_at, width), :] = activate(outer_refs[b][0])

    def blocks(order):
        for other in BITS:
            for at, where in enumerate(order):
                start = pl.multiple_of(block_of(device, where, other) * rows, 16)
                yield other, at, turned[pl.ds(start, rows), :]

    for tap in range(KERNEL_TAPS):
        for b in range(batch):
            turned[:, b * bins : (b + 1) * bins] = active[
                b, tap * DILATION_STEP : tap * DILATION_STEP + bins, :
            ].T
        for other, at, block in blocks(TAP_ORDERS[tap]):
            taps_ref[other, at // HALF, tap, at % HALF] = block
    turned[...] = cotangent_ref[...].T
    for other, at, block in blocks(PROJECT_ORDER):
        project_ref[other, at // HALF, 0, at % HALF] = block


def prepare(features, edges_of, cotangent, gain, rows):
    tokens, channels = cotangent.shape
    batch, bins, _ = features.shape
    shape = lambda count: jax.ShapeDtypeStruct((2, 2, count, HALF, rows, tokens), cotangent.dtype)
    return pl.pallas_call(
        prepare_kernel,
        out_shape=[shape(KERNEL_TAPS), shape(1)],
        in_specs=[SMEM] + [VMEM] * (3 + 2 * batch),
        out_specs=[VMEM] * 2,
        scratch_shapes=[
            pltpu.VMEM((batch, bins + 2 * DILATION_STEP, channels), jnp.bfloat16),
            pltpu.VMEM((channels, tokens), jnp.bfloat16),
        ],
        compiler_params=pltpu.CompilerParams(vmem_limit_bytes=16 << 20),
        name="prepare",
    )(device_index(), features, cotangent, gain.reshape(1, channels), *edges_of)


def place_products(device, parts, turned, orders, placed):
    rows, inner = parts[0].shape[2:]
    for other in BITS:
        for which in BITS:
            part = parts[2 * other + which]
            for matrix, right in enumerate(turned):
                product = jnp.dot(
                    part[matrix].reshape(HALF * rows, inner),
                    right,
                    preferred_element_type=jnp.float32,
                )
                for at in range(HALF):
                    block = block_of(device, orders[matrix][which * HALF + at], other)
                    target = pl.ds(pl.multiple_of(block * rows, 16), rows)
                    rows_of = product[at * rows : (at + 1) * rows]
                    if matrix == 0:
                        placed[target, :] = rows_of
                    else:
                        placed[target, :] += rows_of


def project_back_kernel(index_ref, hidden_ref, features_ref, *refs):
    parts, out_ref, placed = refs[:4], refs[4], refs[5]
    place_products(index_ref[0], parts, [hidden_ref[...].T], [PROJECT_ORDER], placed)
    out_ref[...] = (features_ref[...].astype(jnp.float32) + placed[...].T).astype(jnp.bfloat16)


def project_back(hidden, features, parts):
    return pl.pallas_call(
        project_back_kernel,
        out_shape=jax.ShapeDtypeStruct(features.shape, features.dtype),
        in_specs=[SMEM] + [VMEM] * 6,
        out_specs=VMEM,
        scratch_shapes=[pltpu.VMEM(features.shape[::-1], jnp.float32)],
        compiler_params=pltpu.CompilerParams(vmem_limit_bytes=16 << 20),
        name="project_back",
    )(device_index(), hidden, features, *parts)


def grad_active_kernel(index_ref, grad_ref, core_ref, outer_ref, *refs):
    parts, (out_ref, padded_ref, placed) = refs[:4], refs[4:]
    batch, padded_bins, _ = padded_ref.shape
    bins = padded_bins - 2 * DILATION_STEP
    core_at, outer_at = edge_places(index_ref[0], bins)
    for b in range(batch):
        padded_ref[b, DILATION_STEP : DILATION_STEP + bins] = grad_ref[b * bins : (b + 1) * bins]
        padded_ref[b, pl.ds(core_at, DILATION_STEP), :] = core_ref[b]
        padded_ref[b, pl.ds(outer_at, DILATION_STEP), :] = outer_ref[b]
    turned = []
    for tap in range(KERNEL_TAPS):
        shift = (KERNEL_TAPS - 1 - tap) * DILATION_STEP
        turned.append(
            jnp.concatenate([padded_ref[b, shift : shift + bins] for b in range(batch)], axis=0).T
        )
    place_products(index_ref[0], parts, turned, TAP_ORDERS, placed)
    out_ref[...] = placed[...].T


def grad_of_active(grad, edges_of, parts):
    tokens, inner = grad.shape
    batch = edges_of[0].shape[0]
    channels = 2 * BLOCKS * parts[0].shape[2]
    return pl.pallas_call(
        grad_active_kernel,
        out_shape=jax.ShapeDtypeStruct((tokens, channels), jnp.float32),
        in_specs=[SMEM] + [VMEM] * 7,
        out_specs=VMEM,
        scratch_shapes=[
            pltpu.VMEM((batch, tokens // batch + 2 * DILATION_STEP, inner), grad.dtype),
            pltpu.VMEM((channels, tokens), jnp.float32),
        ],
        compiler_params=pltpu.CompilerParams(vmem_limit_bytes=24 << 20),
        name="grad_active",
    )(device_index(), grad, *edges_of, *parts)


def rows_dot(left, right):
    return jnp.einsum("mnrt,ti->mnri", left, right, preferred_element_type=jnp.float32)


def contract(left, right):
    return jnp.einsum(
        "ct,ci->ti",
        left.reshape(-1, left.shape[-1]),
        right.reshape(-1, right.shape[-1]),
        preferred_element_type=jnp.float32,
    )


def body_torus(features, cotangent, dilated_kernel_weight, project_weight, outer_gain, inner_gain):
    batch, bin_count, channels = features.shape
    inner = project_weight.shape[1]
    rows = project_weight.shape[0]
    tokens = batch * bin_count
    factor = 1.0 / math.sqrt(tokens * TORUS_DEVICES)
    as_bf16 = lambda value: value.astype(jnp.bfloat16)
    as_f32 = lambda value: value.astype(jnp.float32)

    taps = jnp.moveaxis(dilated_kernel_weight, 1, 0)[:, None]
    pair = taps[:2]
    rest = jnp.concatenate([taps[2:], project_weight[None, None]])
    pair_in, rest_in = send(pair, Z_FAR), send(rest, FIRST)
    pair, last, proj = assemble(
        (pair, pair_in, rest, rest_in),
        (
            (2, 2, ((0, 0, 2, 0, 0), (1, 0, 2, 0, 1))),
            (1, 2, ((2, 0, 1, 0, 0), (3, 0, 1, 0, 1))),
            (1, 2, ((2, 1, 1, 0, 0), (3, 1, 1, 0, 1))),
        ),
    )
    pair_in, last_in, proj_b = send(pair, Z_NEAR), send(last, Z_FAR), send(proj, SECOND)
    parity = lax.axis_index("seq") & 1
    feature_edges = list(
        zip(*(edge_swaps(after(features, pair)[b : b + 1], parity) for b in range(batch)))
    )
    feature_edges = [array for side in feature_edges for array in side]
    grow = lambda m, n, a: (m, 2 * n, ((a, 0, m, 0, 0), (a + 1, 0, m, 0, n)))
    pair_in = after(pair_in, proj_b, *feature_edges)
    pair, last = assemble((pair, pair_in, last, last_in), (grow(2, 2, 0), grow(1, 2, 2)))
    pair_in, last_in, proj_in = send(pair, FIRST), send(last, Z_NEAR), send(proj, Z_FAR)
    (proj_a,) = assemble((proj, proj_in), (grow(1, 2, 0),))
    (near,) = assemble(
        after((pair, pair_in, last, last_in), proj_a),
        ((3, 8, ((0, 0, 2, 0, 0), (1, 0, 2, 0, 4), (2, 0, 1, 2, 0), (3, 0, 1, 2, 4))),),
    )
    far, near_other = send(near, SECOND), send(near, CORE)
    proj_in, proj_b_in = send(proj_a, Z_NEAR), send(proj_b, Z_FAR)
    flat_cotangent = cotangent.reshape(tokens, channels)
    act, act_p = prepare(
        after(features, near), feature_edges, flat_cotangent, outer_gain, rows
    )
    (proj_b,) = assemble((proj_b, after(proj_b_in, act)), (grow(1, 2, 0),))
    proj_b_in = send(proj_b, Z_NEAR)
    conv_output = contract(act[0, 0], after(near, proj_b))
    (proj_a,) = assemble((proj_a, after(proj_in, conv_output)), (grow(1, 4, 0),))
    proj_a_other = send(proj_a, CORE)
    (proj_b,) = assemble((proj_b, after(proj_b_in, proj_a)), (grow(1, 4, 0),))
    proj_b_other = send(proj_b, CORE)
    far = after(far, proj_b_other, proj_a_other)
    far_other = send(far, CORE)
    conv_output = conv_output + contract(act[1, 0], after(near_other, far))
    proj_a_late, proj_b_late = after((proj_a, proj_b), far)
    grad_hidden = (
        contract(act_p[0, 0], proj_a_late)
        + contract(act_p[1, 0], proj_a_other)
        + contract(act_p[0, 1], proj_b_late)
        + contract(act_p[1, 1], proj_b_other)
    )
    conv_output = conv_output + contract(act[0, 1], far) + contract(act[1, 1], far_other)
    hidden32, pull_inner = jax.vjp(act_norm, conv_output, inner_gain)
    hidden = as_bf16(hidden32)
    grad_conv, grad_gain_inner = pull_inner(grad_hidden)
    grad_conv = as_bf16(grad_conv)

    give = as_bf16(rows_dot(act[1, 1], grad_conv))
    recv_far = send(give, CORE)
    give = as_bf16(rows_dot(act[1, 0], after(grad_conv, give)))
    recv_near = send(give, CORE)
    give = as_bf16(
        rows_dot(act_p[1].reshape(2, HALF, rows, tokens), after(hidden, give))
    )
    recv_p = send(give, CORE)
    grad_edges = edge_swaps(after(grad_conv, give).reshape(batch, bin_count, inner), parity)
    message = as_bf16(rows_dot(act[0, 1], after(grad_conv, give)) + as_f32(recv_far))
    recv = send(message, SECOND)
    grad_p = after(hidden, message)
    split = lambda which: act_p[0, which].reshape(2, HALF // 2, rows, tokens)
    parts_of = lambda array, which: array[which].reshape(2, HALF // 2, rows, inner)
    message_b = as_bf16(
        rows_dot(split(1)[1:], grad_p) + as_f32(parts_of(recv_p, 1)[1:])
    )
    recv_b = send(message_b, Z_NEAR)
    message_a = as_bf16(
        rows_dot(split(0)[1:], grad_p) + as_f32(parts_of(recv_p, 0)[1:])
    )
    grad_p = after(hidden, message_a, message_b)
    kept_b = rows_dot(split(1)[:1], grad_p) + as_f32(parts_of(recv_p, 1)[:1])
    kept_a = rows_dot(split(0)[:1], grad_p) + as_f32(parts_of(recv_p, 0)[:1])
    kept = rows_dot(act[0, 0], after(grad_conv, kept_a, kept_b)) + as_f32(recv_near)

    flat = features.reshape(tokens, channels)
    grad_active = grad_of_active(
        after(grad_conv, kept), grad_edges, (near, far, near_other, far_other)
    )
    f32, bf16 = jnp.float32, jnp.bfloat16
    unused, pull_outer = jax.vjp(act_norm, as_f32(after(features, grad_active)), outer_gain)
    grad_branch, grad_gain_outer = pull_outer(grad_active.reshape(features.shape))
    grad_features = as_bf16(as_f32(cotangent) + grad_branch)
    gains = jnp.concatenate([grad_gain_outer, grad_gain_inner]) * factor
    recv_b = after(recv_b, grad_features, gains)
    message_b, kept_b = fold(
        (kept_b, recv_b),
        (
            (bf16, 1, 2, (((0, 1), (0, 1), (2, 2), 0, 0),)),
            (f32, 1, 2, (((0, 1), (0, 1), (0, 2), 0, 0),)),
        ),
    )
    recv_b = send(message_b, Z_FAR)
    recv_a = send(after(message_a, message_b), Z_NEAR)
    gains = after(gains, message_b)
    gains = gains + send(gains, CORE)
    gains = gains + send(gains, links(lambda i: i ^ 2))

    recv_a = after(recv_a, gains)
    message, message_l, message_a, message_p, kept, kept_l, kept_a, kept_b = fold(
        (kept, recv, kept_a, recv_a, kept_b, recv_b),
        (
            (bf16, 2, 4, (((0, 1), (0, 2), (4, 4), 0, 0),)),
            (bf16, 1, 4, (((0, 1), (2, 1), (4, 4), 0, 0),)),
            (bf16, 1, 2, (((2, 3), (0, 1), (2, 2), 0, 0),)),
            (bf16, 1, 2, (((4, 5), (0, 1), (0, 2), 0, 0),)),
            (f32, 2, 4, (((0, 1), (0, 2), (0, 4), 0, 0),)),
            (f32, 1, 4, (((0, 1), (2, 1), (0, 4), 0, 0),)),
            (f32, 1, 2, (((2, 3), (0, 1), (0, 2), 0, 0),)),
            (f32, 1, 2, (((4, 5), (0, 1), (0, 2), 0, 0),)),
        ),
    )
    recv, recv_l, recv_a = send(message, FIRST), send(message_l, Z_NEAR), send(message_a, Z_FAR)
    gains = after(gains, message)
    gains = gains + send(gains, links(lambda i: i ^ 4))
    block_out = project_back(
        after(hidden, message), flat, (proj_a, proj_b, proj_a_other, proj_b_other)
    ).reshape(features.shape)
    gains = after(gains, block_out)

    recv = after(recv, gains)
    message, message_l, kept, kept_l, kept_p = fold(
        (kept, recv, kept_l, recv_l, kept_a, recv_a),
        (
            (bf16, 2, 2, (((0, 1), (0, 2), (2, 2), 0, 0),)),
            (bf16, 1, 2, (((2, 3), (0, 1), (2, 2), 0, 0),)),
            (f32, 2, 2, (((0, 1), (0, 2), (0, 2), 0, 0),)),
            (f32, 1, 2, (((2, 3), (0, 1), (0, 2), 0, 0),)),
            (f32, 1, 2, (((4, 5), (0, 1), (0, 2), 0, 0),)),
        ),
    )
    message_p = after(message_p, message)
    recv, recv_l, recv_p = send(message, Z_NEAR), send(message_l, Z_FAR), send(message_p, SECOND)
    gains = after(gains, message)
    gains = gains + send(gains, Z_NEAR)

    recv = after(recv, gains)
    message, message_r, kept, kept_r = fold(
        (kept, recv, kept_l, recv_l, kept_p, recv_p),
        (
            (bf16, 2, 1, (((0, 1), (0, 2), (1, 1), 0, 0),)),
            (bf16, 2, 1, (((2, 3), (0, 1), (1, 1), 0, 0), ((4, 5), (0, 1), (1, 1), 1, 0))),
            (f32, 2, 1, (((0, 1), (0, 2), (0, 1), 0, 0),)),
            (f32, 2, 1, (((2, 3), (0, 1), (0, 1), 0, 0), ((4, 5), (0, 1), (0, 1), 1, 0))),
        ),
    )
    recv, recv_r = send(message, Z_FAR), send(message_r, FIRST)
    gains = after(gains, message)
    gains = gains + send(gains, Z_FAR)

    sums = kept + as_f32(recv)
    sums_r = kept_r + as_f32(recv_r)
    grad_project = sums_r[1, 0] * factor
    grad_dilated = jnp.stack([sums[0, 0], sums[1, 0], sums_r[0, 0]], axis=1) * factor

    device = lax.axis_index("seq")
    grad_outer_gain = lax.dynamic_slice(gains, (device * rows,), (rows,))
    part = inner // TORUS_DEVICES
    grad_inner_gain = lax.dynamic_slice(gains, (channels + device * part,), (part,))
    return (block_out, grad_features, grad_dilated, grad_project, grad_outer_gain, grad_inner_gain)


def body(*operands):
    if lax.axis_size("seq") == TORUS_DEVICES:
        return body_torus(*operands)
    return body_any(*operands)


def solution(mesh):
    return jax.shard_map(
        body,
        mesh=mesh,
        in_specs=(
            P("groups", "seq", None),
            P("groups", "seq", None),
            P("seq", None, None),
            P("seq", None),
            P(),
            P(),
        ),
        out_specs=(
            P("groups", "seq", None),
            P("groups", "seq", None),
            P(("groups", "seq"), None, None),
            P(("groups", "seq"), None),
            P(("groups", "seq")),
            P(("groups", "seq")),
        ),
        check_vma=False,
    )
```

```python
import math

import jax
import jax.numpy as jnp
from jax import lax
from jax.experimental import pallas as pl
from jax.experimental.pallas import tpu as pltpu
from jax.sharding import PartitionSpec as P

KERNEL_TAPS = 3
DILATION_STEP = 32
TORUS_DEVICES = 32


eps = 1e-06


def padded(block, sides, width):
    for axis, dim in sides:
        count = lax.axis_size(axis)
        forward = [(i, i + 1) for i in range(count - 1)]
        backward = [(target, source) for source, target in forward]
        low = lax.ppermute(
            lax.slice_in_dim(block, block.shape[dim] - width, None, axis=dim), axis, forward
        )
        high = lax.ppermute(lax.slice_in_dim(block, 0, width, axis=dim), axis, backward)
        block = jnp.concatenate([low, block, high], axis=dim)
    return block


def act_norm(values, gain):
    meansq = jnp.mean(values * values, axis=-1, keepdims=True)
    return jax.nn.gelu(values * lax.rsqrt(meansq + eps) * gain, approximate=True)


def reduce_dilated(padded_input, conv_output_gradient, factor):
    bin_count = conv_output_gradient.shape[1]
    tap_slices = [
        jnp.einsum(
            "btc,bti->ci",
            padded_input[:, tap_index * DILATION_STEP : tap_index * DILATION_STEP + bin_count],
            conv_output_gradient,
            preferred_element_type=jnp.float32,
        )
        for tap_index in range(KERNEL_TAPS)
    ]
    return lax.psum_scatter(
        jnp.stack(tap_slices, axis=1) * factor, "seq", scatter_dimension=0, tiled=True
    )


def body_any(features, cotangent, dilated_kernel_weight, project_weight, outer_gain, inner_gain):
    bin_count = features.shape[1]
    factor = 1.0 / math.sqrt(features.shape[0] * bin_count * lax.axis_size("seq"))
    full_dilated = lax.all_gather(dilated_kernel_weight, "seq", axis=0, tiled=True)
    full_project = lax.all_gather(project_weight, "seq", axis=0, tiled=True)
    as_float = features.astype(jnp.float32)
    active_features = act_norm(as_float, outer_gain).astype(jnp.bfloat16)
    padded_input = padded(active_features, (("seq", 1),), DILATION_STEP)
    conv_output = jnp.einsum(
        "btc,ci->bti",
        padded_input[:, 0:bin_count],
        full_dilated[:, 0, :],
        preferred_element_type=jnp.float32,
    )
    for tap_index in range(1, KERNEL_TAPS):
        conv_output = conv_output + jnp.einsum(
            "btc,ci->bti",
            padded_input[:, tap_index * DILATION_STEP : tap_index * DILATION_STEP + bin_count],
            full_dilated[:, tap_index, :],
            preferred_element_type=jnp.float32,
        )
    hidden = act_norm(conv_output, inner_gain).astype(jnp.bfloat16)
    block_out = (
        as_float
        + jnp.einsum("bti,ci->btc", hidden, full_project, preferred_element_type=jnp.float32)
    ).astype(jnp.bfloat16)
    grad_hidden = jnp.einsum(
        "btc,ci->bti", cotangent, full_project, preferred_element_type=jnp.float32
    )
    unused, pull_inner = jax.vjp(act_norm, conv_output, inner_gain)
    conv_output_gradient, grad_gain_inner = pull_inner(grad_hidden)
    conv_output_gradient = conv_output_gradient.astype(jnp.bfloat16)
    padded_input_gradient = padded(conv_output_gradient, (("seq", 1),), DILATION_STEP)
    grad_active = jnp.zeros(features.shape, jnp.float32)
    for tap_index in range(KERNEL_TAPS):
        tap_shift = (KERNEL_TAPS - 1 - tap_index) * DILATION_STEP
        grad_active = grad_active + jnp.einsum(
            "bti,ci->btc",
            padded_input_gradient[:, tap_shift : tap_shift + bin_count],
            full_dilated[:, tap_index, :],
            preferred_element_type=jnp.float32,
        )
    unused_two, pull_outer = jax.vjp(act_norm, as_float, outer_gain)
    grad_branch, grad_gain_outer = pull_outer(grad_active)
    grad_features = (cotangent.astype(jnp.float32) + grad_branch).astype(jnp.bfloat16)
    grad_dilated = reduce_dilated(padded_input, conv_output_gradient, factor)
    grad_project = lax.psum_scatter(
        jnp.einsum("btc,bti->ci", cotangent, hidden, preferred_element_type=jnp.float32) * factor,
        "seq",
        scatter_dimension=0,
        tiled=True,
    )
    grad_outer_gain, grad_inner_gain = (
        lax.psum_scatter(grad_gain_outer * factor, "seq", scatter_dimension=0, tiled=True),
        lax.psum_scatter(grad_gain_inner * factor, "seq", scatter_dimension=0, tiled=True),
    )
    return (block_out, grad_features, grad_dilated, grad_project, grad_outer_gain, grad_inner_gain)


def links(move):
    return [(i, move(i)) for i in range(TORUS_DEVICES)]


CORE = links(lambda i: i ^ 1)
FIRST = links(lambda i: i ^ (4 if i & 1 else 2))
SECOND = links(lambda i: i ^ (2 if i & 1 else 4))
Z_NEAR = links(lambda i: i ^ 8)
Z_FAR = links(lambda i: i ^ 16)

BITS = (0, 1)
PAIR_ORDER = [(r2, r1, low, high) for r2 in BITS for r1 in BITS for low in BITS for high in BITS]
LAST_ORDER = [(r2, r1, low, high) for r2 in BITS for low in BITS for high in BITS for r1 in BITS]
TAP_ORDERS = [PAIR_ORDER, PAIR_ORDER, LAST_ORDER]
PROJECT_ORDER = LAST_ORDER
BLOCKS = 16
HALF = 8

OUTER = [
    (i, j)
    for odd in range(1, TORUS_DEVICES - 1, 2)
    for i, j in ((odd, odd + 1), (odd + 1, odd))
]

VMEM = pl.BlockSpec(memory_space=pltpu.VMEM)
SMEM = pl.BlockSpec(memory_space=pltpu.SMEM)


def send(block, pairs):
    return lax.ppermute(block, "seq", pairs)


def after(value, *events):
    return lax.optimization_barrier((value,) + events)[0]


def device_index():
    return lax.axis_index("seq").astype(jnp.int32).reshape(1)


def block_of(device, place, other):
    r2, r1, low, high = place
    owner = device ^ other
    parity = owner & 1
    dx = r1 + parity * (r2 - r1)
    dy = r2 + parity * (r1 - r2)
    return owner ^ (16 * high + 8 * low + 4 * dy + 2 * dx)


def edge_swaps(block, parity):
    width = DILATION_STEP
    last = block.shape[1] - width
    inside = lax.dynamic_slice_in_dim(block, (1 - parity) * last, width, axis=1)
    outside = lax.dynamic_slice_in_dim(block, parity * last, width, axis=1)
    return send(inside, CORE), send(outside, OUTER)


def fold(inputs, outputs):
    def kernel(*refs):
        sources, targets = refs[: len(inputs)], refs[len(inputs) :]
        for target, (dtype, _, _, pieces) in zip(targets, outputs):
            for added, (m, m_count), (n, n_count), to_m, to_n in pieces:
                total = None
                for source in added:
                    value = sources[source][m : m + m_count, n : n + n_count]
                    value = value.astype(jnp.float32)
                    total = value if total is None else total + value
                target[to_m : to_m + m_count, to_n : to_n + n_count] = total.astype(dtype)

    tail = inputs[0].shape[2:]
    return pl.pallas_call(
        kernel,
        out_shape=[
            jax.ShapeDtypeStruct((m, n) + tail, dtype) for dtype, m, n, pieces in outputs
        ],
        in_specs=[VMEM] * len(inputs),
        out_specs=[VMEM] * len(outputs),
        compiler_params=pltpu.CompilerParams(vmem_limit_bytes=12 << 20),
        name="fold",
    )(*inputs)


def assemble(inputs, outputs):
    def kernel(*refs):
        sources, targets = refs[: len(inputs)], refs[len(inputs) :]
        for target, (_, _, pieces) in zip(targets, outputs):
            for source, start, count, to_m, to_n in pieces:
                n = sources[source].shape[1]
                target[to_m : to_m + count, to_n : to_n + n] = sources[source][
                    start : start + count
                ]

    tail = inputs[0].shape[2:]
    return pl.pallas_call(
        kernel,
        out_shape=[
            jax.ShapeDtypeStruct((m, n) + tail, inputs[0].dtype) for m, n, pieces in outputs
        ],
        in_specs=[VMEM] * len(inputs),
        out_specs=[VMEM] * len(outputs),
        compiler_params=pltpu.CompilerParams(vmem_limit_bytes=8 << 20),
        name="assemble",
    )(*inputs)


GELU_SCALE = math.sqrt(2.0 / math.pi)
GELU_CUBE = 0.044715


def edge_places(device, bins):
    parity = device & 1
    beyond = bins + DILATION_STEP
    core_at = pl.multiple_of((1 - parity) * beyond, DILATION_STEP)
    outer_at = pl.multiple_of(parity * beyond, DILATION_STEP)
    return core_at, outer_at


def prepare_kernel(
    index_ref,
    features_ref,
    cotangent_ref,
    gain_ref,
    *refs,
):
    device = index_ref[0]
    batch, bins, channels = features_ref.shape
    core_refs, outer_refs = refs[:batch], refs[batch : 2 * batch]
    taps_ref, project_ref, active, turned = refs[2 * batch :]
    rows = taps_ref.shape[4]
    width = DILATION_STEP
    gain = gain_ref[...]
    core_at, outer_at = edge_places(device, bins)

    def activate(x):
        x = x.astype(jnp.float32)
        inverse = lax.rsqrt(jnp.sum(x * x, axis=-1, keepdims=True) * (1.0 / channels) + eps)
        v = x * inverse * gain
        t = jnp.tanh(GELU_SCALE * (v + GELU_CUBE * (v * v * v)))
        return (0.5 * v * (1.0 + t)).astype(jnp.bfloat16)

    for b in range(batch):

        def some_rows(i, carry):
            at = pl.multiple_of(i * width, width)
            rows_of = activate(features_ref[b, pl.ds(at, width), :])
            active[b, pl.ds(pl.multiple_of(at + width, width), width), :] = rows_of
            return carry

        lax.fori_loop(0, bins // width, some_rows, 0)
        active[b, pl.ds(core_at, width), :] = activate(core_refs[b][0])
        active[b, pl.ds(outer_at, width), :] = activate(outer_refs[b][0])

    def blocks(order):
        for other in BITS:
            for at, where in enumerate(order):
                start = pl.multiple_of(block_of(device, where, other) * rows, 16)
                yield other, at, turned[pl.ds(start, rows), :]

    for tap in range(KERNEL_TAPS):
        for b in range(batch):
            turned[:, b * bins : (b + 1) * bins] = active[
                b, tap * DILATION_STEP : tap * DILATION_STEP + bins, :
            ].T
        for other, at, block in blocks(TAP_ORDERS[tap]):
            taps_ref[other, at // HALF, tap, at % HALF] = block
    turned[...] = cotangent_ref[...].T
    for other, at, block in blocks(PROJECT_ORDER):
        project_ref[other, at // HALF, 0, at % HALF] = block


def prepare(features, edges_of, cotangent, gain, rows):
    tokens, channels = cotangent.shape
    batch, bins, _ = features.shape
    shape = lambda count: jax.ShapeDtypeStruct((2, 2, count, HALF, rows, tokens), cotangent.dtype)
    return pl.pallas_call(
        prepare_kernel,
        out_shape=[shape(KERNEL_TAPS), shape(1)],
        in_specs=[SMEM] + [VMEM] * (3 + 2 * batch),
        out_specs=[VMEM] * 2,
        scratch_shapes=[
            pltpu.VMEM((batch, bins + 2 * DILATION_STEP, channels), jnp.bfloat16),
            pltpu.VMEM((channels, tokens), jnp.bfloat16),
        ],
        compiler_params=pltpu.CompilerParams(vmem_limit_bytes=16 << 20),
        name="prepare",
    )(device_index(), features, cotangent, gain.reshape(1, channels), *edges_of)


def place_products(device, parts, turned, orders, placed):
    rows, inner = parts[0].shape[2:]
    for other in BITS:
        for which in BITS:
            part = parts[2 * other + which]
            for matrix, right in enumerate(turned):
                product = jnp.dot(
                    part[matrix].reshape(HALF * rows, inner),
                    right,
                    preferred_element_type=jnp.float32,
                )
                for at in range(HALF):
                    block = block_of(device, orders[matrix][which * HALF + at], other)
                    target = pl.ds(pl.multiple_of(block * rows, 16), rows)
                    rows_of = product[at * rows : (at + 1) * rows]
                    if matrix == 0:
                        placed[target, :] = rows_of
                    else:
                        placed[target, :] += rows_of


def project_back_kernel(index_ref, hidden_ref, features_ref, *refs):
    parts, out_ref, placed = refs[:4], refs[4], refs[5]
    place_products(index_ref[0], parts, [hidden_ref[...].T], [PROJECT_ORDER], placed)
    out_ref[...] = (features_ref[...].astype(jnp.float32) + placed[...].T).astype(jnp.bfloat16)


def project_back(hidden, features, parts):
    return pl.pallas_call(
        project_back_kernel,
        out_shape=jax.ShapeDtypeStruct(features.shape, features.dtype),
        in_specs=[SMEM] + [VMEM] * 6,
        out_specs=VMEM,
        scratch_shapes=[pltpu.VMEM(features.shape[::-1], jnp.float32)],
        compiler_params=pltpu.CompilerParams(vmem_limit_bytes=16 << 20),
        name="project_back",
    )(device_index(), hidden, features, *parts)


def grad_active_kernel(index_ref, grad_ref, core_ref, outer_ref, *refs):
    parts, (out_ref, padded_ref, placed) = refs[:4], refs[4:]
    batch, padded_bins, _ = padded_ref.shape
    bins = padded_bins - 2 * DILATION_STEP
    core_at, outer_at = edge_places(index_ref[0], bins)
    for b in range(batch):
        padded_ref[b, DILATION_STEP : DILATION_STEP + bins] = grad_ref[b * bins : (b + 1) * bins]
        padded_ref[b, pl.ds(core_at, DILATION_STEP), :] = core_ref[b]
        padded_ref[b, pl.ds(outer_at, DILATION_STEP), :] = outer_ref[b]
    turned = []
    for tap in range(KERNEL_TAPS):
        shift = (KERNEL_TAPS - 1 - tap) * DILATION_STEP
        turned.append(
            jnp.concatenate([padded_ref[b, shift : shift + bins] for b in range(batch)], axis=0).T
        )
    place_products(index_ref[0], parts, turned, TAP_ORDERS, placed)
    out_ref[...] = placed[...].T


def grad_of_active(grad, edges_of, parts):
    tokens, inner = grad.shape
    batch = edges_of[0].shape[0]
    channels = 2 * BLOCKS * parts[0].shape[2]
    return pl.pallas_call(
        grad_active_kernel,
        out_shape=jax.ShapeDtypeStruct((tokens, channels), jnp.float32),
        in_specs=[SMEM] + [VMEM] * 7,
        out_specs=VMEM,
        scratch_shapes=[
            pltpu.VMEM((batch, tokens // batch + 2 * DILATION_STEP, inner), grad.dtype),
            pltpu.VMEM((channels, tokens), jnp.float32),
        ],
        compiler_params=pltpu.CompilerParams(vmem_limit_bytes=24 << 20),
        name="grad_active",
    )(device_index(), grad, *edges_of, *parts)


def rows_dot(left, right):
    return jnp.einsum("mnrt,ti->mnri", left, right, preferred_element_type=jnp.float32)


def contract(left, right):
    return jnp.einsum(
        "ct,ci->ti",
        left.reshape(-1, left.shape[-1]),
        right.reshape(-1, right.shape[-1]),
        preferred_element_type=jnp.float32,
    )


def body_torus(features, cotangent, dilated_kernel_weight, project_weight, outer_gain, inner_gain):
    batch, bin_count, channels = features.shape
    inner = project_weight.shape[1]
    rows = project_weight.shape[0]
    tokens = batch * bin_count
    factor = 1.0 / math.sqrt(tokens * TORUS_DEVICES)
    as_bf16 = lambda value: value.astype(jnp.bfloat16)
    as_f32 = lambda value: value.astype(jnp.float32)

    taps = jnp.moveaxis(dilated_kernel_weight, 1, 0)[:, None]
    pair = taps[:2]
    rest = jnp.concatenate([taps[2:], project_weight[None, None]])
    pair_in, rest_in = send(pair, Z_FAR), send(rest, FIRST)
    pair, last, proj = assemble(
        (pair, pair_in, rest, rest_in),
        (
            (2, 2, ((0, 0, 2, 0, 0), (1, 0, 2, 0, 1))),
            (1, 2, ((2, 0, 1, 0, 0), (3, 0, 1, 0, 1))),
            (1, 2, ((2, 1, 1, 0, 0), (3, 1, 1, 0, 1))),
        ),
    )
    pair_in, last_in, proj_b = send(pair, Z_NEAR), send(last, Z_FAR), send(proj, SECOND)
    parity = lax.axis_index("seq") & 1
    feature_edges = list(
        zip(*(edge_swaps(after(features, pair)[b : b + 1], parity) for b in range(batch)))
    )
    feature_edges = [array for side in feature_edges for array in side]
    grow = lambda m, n, a: (m, 2 * n, ((a, 0, m, 0, 0), (a + 1, 0, m, 0, n)))
    pair_in = after(pair_in, proj_b, *feature_edges)
    pair, last = assemble((pair, pair_in, last, last_in), (grow(2, 2, 0), grow(1, 2, 2)))
    pair_in, last_in, proj_in = send(pair, FIRST), send(last, Z_NEAR), send(proj, Z_FAR)
    (proj_a,) = assemble((proj, proj_in), (grow(1, 2, 0),))
    (near,) = assemble(
        after((pair, pair_in, last, last_in), proj_a),
        ((3, 8, ((0, 0, 2, 0, 0), (1, 0, 2, 0, 4), (2, 0, 1, 2, 0), (3, 0, 1, 2, 4))),),
    )
    far, near_other = send(near, SECOND), send(near, CORE)
    proj_in, proj_b_in = send(proj_a, Z_NEAR), send(proj_b, Z_FAR)
    flat_cotangent = cotangent.reshape(tokens, channels)
    act, act_p = prepare(
        after(features, near), feature_edges, flat_cotangent, outer_gain, rows
    )
    (proj_b,) = assemble((proj_b, after(proj_b_in, act)), (grow(1, 2, 0),))
    proj_b_in = send(proj_b, Z_NEAR)
    conv_output = contract(act[0, 0], after(near, proj_b))
    (proj_a,) = assemble((proj_a, after(proj_in, conv_output)), (grow(1, 4, 0),))
    proj_a_other = send(proj_a, CORE)
    (proj_b,) = assemble((proj_b, after(proj_b_in, proj_a)), (grow(1, 4, 0),))
    proj_b_other = send(proj_b, CORE)
    far = after(far, proj_b_other, proj_a_other)
    far_other = send(far, CORE)
    conv_output = conv_output + contract(act[1, 0], after(near_other, far))
    proj_a_late, proj_b_late = after((proj_a, proj_b), far)
    grad_hidden = (
        contract(act_p[0, 0], proj_a_late)
        + contract(act_p[1, 0], proj_a_other)
        + contract(act_p[0, 1], proj_b_late)
        + contract(act_p[1, 1], proj_b_other)
    )
    conv_output = conv_output + contract(act[0, 1], far) + contract(act[1, 1], far_other)
    hidden32, pull_inner = jax.vjp(act_norm, conv_output, inner_gain)
    hidden = as_bf16(hidden32)
    grad_conv, grad_gain_inner = pull_inner(grad_hidden)
    grad_conv = as_bf16(grad_conv)

    give = as_bf16(rows_dot(act[1, 1], grad_conv))
    recv_far = send(give, CORE)
    give = as_bf16(rows_dot(act[1, 0], after(grad_conv, give)))
    recv_near = send(give, CORE)
    give = as_bf16(
        rows_dot(act_p[1].reshape(2, HALF, rows, tokens), after(hidden, give))
    )
    recv_p = send(give, CORE)
    grad_edges = edge_swaps(after(grad_conv, give).reshape(batch, bin_count, inner), parity)
    message = as_bf16(rows_dot(act[0, 1], after(grad_conv, give)) + as_f32(recv_far))
    recv = send(message, SECOND)
    grad_p = after(hidden, message)
    split = lambda which: act_p[0, which].reshape(2, HALF // 2, rows, tokens)
    parts_of = lambda array, which: array[which].reshape(2, HALF // 2, rows, inner)
    message_b = as_bf16(
        rows_dot(split(1)[1:], grad_p) + as_f32(parts_of(recv_p, 1)[1:])
    )
    recv_b = send(message_b, Z_NEAR)
    message_a = as_bf16(
        rows_dot(split(0)[1:], grad_p) + as_f32(parts_of(recv_p, 0)[1:])
    )
    grad_p = after(hidden, message_a, message_b)
    kept_b = rows_dot(split(1)[:1], grad_p) + as_f32(parts_of(recv_p, 1)[:1])
    kept_a = rows_dot(split(0)[:1], grad_p) + as_f32(parts_of(recv_p, 0)[:1])
    kept = rows_dot(act[0, 0], after(grad_conv, kept_a, kept_b)) + as_f32(recv_near)

    flat = features.reshape(tokens, channels)
    grad_active = grad_of_active(
        after(grad_conv, kept), grad_edges, (near, far, near_other, far_other)
    )
    f32, bf16 = jnp.float32, jnp.bfloat16
    unused, pull_outer = jax.vjp(act_norm, as_f32(after(features, grad_active)), outer_gain)
    grad_branch, grad_gain_outer = pull_outer(grad_active.reshape(features.shape))
    grad_features = as_bf16(as_f32(cotangent) + grad_branch)
    gains = jnp.concatenate([grad_gain_outer, grad_gain_inner]) * factor
    recv_b = after(recv_b, grad_features, gains)
    message_b, kept_b = fold(
        (kept_b, recv_b),
        (
            (bf16, 1, 2, (((0, 1), (0, 1), (2, 2), 0, 0),)),
            (f32, 1, 2, (((0, 1), (0, 1), (0, 2), 0, 0),)),
        ),
    )
    recv_b = send(message_b, Z_FAR)
    recv_a = send(after(message_a, message_b), Z_NEAR)
    gains = after(gains, message_b)
    gains = gains + send(gains, CORE)
    gains = gains + send(gains, Z_NEAR)

    recv_a = after(recv_a, gains)
    message, message_l, message_a, message_p, kept, kept_l, kept_a, kept_b = fold(
        (kept, recv, kept_a, recv_a, kept_b, recv_b),
        (
            (bf16, 2, 4, (((0, 1), (0, 2), (4, 4), 0, 0),)),
            (bf16, 1, 4, (((0, 1), (2, 1), (4, 4), 0, 0),)),
            (bf16, 1, 2, (((2, 3), (0, 1), (2, 2), 0, 0),)),
            (bf16, 1, 2, (((4, 5), (0, 1), (0, 2), 0, 0),)),
            (f32, 2, 4, (((0, 1), (0, 2), (0, 4), 0, 0),)),
            (f32, 1, 4, (((0, 1), (2, 1), (0, 4), 0, 0),)),
            (f32, 1, 2, (((2, 3), (0, 1), (0, 2), 0, 0),)),
            (f32, 1, 2, (((4, 5), (0, 1), (0, 2), 0, 0),)),
        ),
    )
    recv, recv_l, recv_a = send(message, FIRST), send(message_l, Z_NEAR), send(message_a, Z_FAR)
    gains = after(gains, message)
    gains = gains + send(gains, Z_FAR)
    block_out = project_back(
        after(hidden, message), flat, (proj_a, proj_b, proj_a_other, proj_b_other)
    ).reshape(features.shape)
    gains = after(gains, block_out)

    recv = after(recv, gains)
    message, message_l, kept, kept_l, kept_p = fold(
        (kept, recv, kept_l, recv_l, kept_a, recv_a),
        (
            (bf16, 2, 2, (((0, 1), (0, 2), (2, 2), 0, 0),)),
            (bf16, 1, 2, (((2, 3), (0, 1), (2, 2), 0, 0),)),
            (f32, 2, 2, (((0, 1), (0, 2), (0, 2), 0, 0),)),
            (f32, 1, 2, (((2, 3), (0, 1), (0, 2), 0, 0),)),
            (f32, 1, 2, (((4, 5), (0, 1), (0, 2), 0, 0),)),
        ),
    )
    message_p = after(message_p, message)
    recv, recv_l, recv_p = send(message, Z_NEAR), send(message_l, Z_FAR), send(message_p, SECOND)
    gains = after(gains, message)
    gains = gains + send(gains, links(lambda i: i ^ 2))
    gains = gains + send(gains, links(lambda i: i ^ 4))

    recv = after(recv, gains)
    message, message_r, kept, kept_r = fold(
        (kept, recv, kept_l, recv_l, kept_p, recv_p),
        (
            (bf16, 2, 1, (((0, 1), (0, 2), (1, 1), 0, 0),)),
            (bf16, 2, 1, (((2, 3), (0, 1), (1, 1), 0, 0), ((4, 5), (0, 1), (1, 1), 1, 0))),
            (f32, 2, 1, (((0, 1), (0, 2), (0, 1), 0, 0),)),
            (f32, 2, 1, (((2, 3), (0, 1), (0, 1), 0, 0), ((4, 5), (0, 1), (0, 1), 1, 0))),
        ),
    )
    recv, recv_r = send(message, Z_FAR), send(message_r, FIRST)

    sums = kept + as_f32(recv)
    sums_r = kept_r + as_f32(recv_r)
    grad_project = sums_r[1, 0] * factor
    grad_dilated = jnp.stack([sums[0, 0], sums[1, 0], sums_r[0, 0]], axis=1) * factor

    device = lax.axis_index("seq")
    grad_outer_gain = lax.dynamic_slice(gains, (device * rows,), (rows,))
    part = inner // TORUS_DEVICES
    grad_inner_gain = lax.dynamic_slice(gains, (channels + device * part,), (part,))
    return (block_out, grad_features, grad_dilated, grad_project, grad_outer_gain, grad_inner_gain)


def body(*operands):
    if lax.axis_size("seq") == TORUS_DEVICES:
        return body_torus(*operands)
    return body_any(*operands)


def solution(mesh):
    return jax.shard_map(
        body,
        mesh=mesh,
        in_specs=(
            P("groups", "seq", None),
            P("groups", "seq", None),
            P("seq", None, None),
            P("seq", None),
            P(),
            P(),
        ),
        out_specs=(
            P("groups", "seq", None),
            P("groups", "seq", None),
            P(("groups", "seq"), None, None),
            P(("groups", "seq"), None),
            P(("groups", "seq")),
            P(("groups", "seq")),
        ),
        check_vma=False,
    )
```

```python
import math

import jax
import jax.numpy as jnp
from jax import lax
from jax.experimental import pallas as pl
from jax.experimental.pallas import tpu as pltpu
from jax.sharding import PartitionSpec as P

KERNEL_TAPS = 3
DILATION_STEP = 32
TORUS_DEVICES = 32


eps = 1e-06


def padded(block, sides, width):
    for axis, dim in sides:
        count = lax.axis_size(axis)
        forward = [(i, i + 1) for i in range(count - 1)]
        backward = [(target, source) for source, target in forward]
        low = lax.ppermute(
            lax.slice_in_dim(block, block.shape[dim] - width, None, axis=dim), axis, forward
        )
        high = lax.ppermute(lax.slice_in_dim(block, 0, width, axis=dim), axis, backward)
        block = jnp.concatenate([low, block, high], axis=dim)
    return block


def act_norm(values, gain):
    meansq = jnp.mean(values * values, axis=-1, keepdims=True)
    return jax.nn.gelu(values * lax.rsqrt(meansq + eps) * gain, approximate=True)


def reduce_dilated(padded_input, conv_output_gradient, factor):
    bin_count = conv_output_gradient.shape[1]
    tap_slices = [
        jnp.einsum(
            "btc,bti->ci",
            padded_input[:, tap_index * DILATION_STEP : tap_index * DILATION_STEP + bin_count],
            conv_output_gradient,
            preferred_element_type=jnp.float32,
        )
        for tap_index in range(KERNEL_TAPS)
    ]
    return lax.psum_scatter(
        jnp.stack(tap_slices, axis=1) * factor, "seq", scatter_dimension=0, tiled=True
    )


def body_any(features, cotangent, dilated_kernel_weight, project_weight, outer_gain, inner_gain):
    bin_count = features.shape[1]
    factor = 1.0 / math.sqrt(features.shape[0] * bin_count * lax.axis_size("seq"))
    full_dilated = lax.all_gather(dilated_kernel_weight, "seq", axis=0, tiled=True)
    full_project = lax.all_gather(project_weight, "seq", axis=0, tiled=True)
    as_float = features.astype(jnp.float32)
    active_features = act_norm(as_float, outer_gain).astype(jnp.bfloat16)
    padded_input = padded(active_features, (("seq", 1),), DILATION_STEP)
    conv_output = jnp.einsum(
        "btc,ci->bti",
        padded_input[:, 0:bin_count],
        full_dilated[:, 0, :],
        preferred_element_type=jnp.float32,
    )
    for tap_index in range(1, KERNEL_TAPS):
        conv_output = conv_output + jnp.einsum(
            "btc,ci->bti",
            padded_input[:, tap_index * DILATION_STEP : tap_index * DILATION_STEP + bin_count],
            full_dilated[:, tap_index, :],
            preferred_element_type=jnp.float32,
        )
    hidden = act_norm(conv_output, inner_gain).astype(jnp.bfloat16)
    block_out = (
        as_float
        + jnp.einsum("bti,ci->btc", hidden, full_project, preferred_element_type=jnp.float32)
    ).astype(jnp.bfloat16)
    grad_hidden = jnp.einsum(
        "btc,ci->bti", cotangent, full_project, preferred_element_type=jnp.float32
    )
    unused, pull_inner = jax.vjp(act_norm, conv_output, inner_gain)
    conv_output_gradient, grad_gain_inner = pull_inner(grad_hidden)
    conv_output_gradient = conv_output_gradient.astype(jnp.bfloat16)
    padded_input_gradient = padded(conv_output_gradient, (("seq", 1),), DILATION_STEP)
    grad_active = jnp.zeros(features.shape, jnp.float32)
    for tap_index in range(KERNEL_TAPS):
        tap_shift = (KERNEL_TAPS - 1 - tap_index) * DILATION_STEP
        grad_active = grad_active + jnp.einsum(
            "bti,ci->btc",
            padded_input_gradient[:, tap_shift : tap_shift + bin_count],
            full_dilated[:, tap_index, :],
            preferred_element_type=jnp.float32,
        )
    unused_two, pull_outer = jax.vjp(act_norm, as_float, outer_gain)
    grad_branch, grad_gain_outer = pull_outer(grad_active)
    grad_features = (cotangent.astype(jnp.float32) + grad_branch).astype(jnp.bfloat16)
    grad_dilated = reduce_dilated(padded_input, conv_output_gradient, factor)
    grad_project = lax.psum_scatter(
        jnp.einsum("btc,bti->ci", cotangent, hidden, preferred_element_type=jnp.float32) * factor,
        "seq",
        scatter_dimension=0,
        tiled=True,
    )
    grad_outer_gain, grad_inner_gain = (
        lax.psum_scatter(grad_gain_outer * factor, "seq", scatter_dimension=0, tiled=True),
        lax.psum_scatter(grad_gain_inner * factor, "seq", scatter_dimension=0, tiled=True),
    )
    return (block_out, grad_features, grad_dilated, grad_project, grad_outer_gain, grad_inner_gain)


def links(move):
    return [(i, move(i)) for i in range(TORUS_DEVICES)]


CORE = links(lambda i: i ^ 1)
FIRST = links(lambda i: i ^ (4 if i & 1 else 2))
SECOND = links(lambda i: i ^ (2 if i & 1 else 4))
Z_NEAR = links(lambda i: i ^ 8)
Z_FAR = links(lambda i: i ^ 16)

BITS = (0, 1)
PAIR_ORDER = [(r2, r1, low, high) for r2 in BITS for r1 in BITS for low in BITS for high in BITS]
LAST_ORDER = [(r2, r1, low, high) for r2 in BITS for low in BITS for high in BITS for r1 in BITS]
TAP_ORDERS = [PAIR_ORDER, PAIR_ORDER, LAST_ORDER]
PROJECT_ORDER = LAST_ORDER
BLOCKS = 16
HALF = 8

OUTER = [
    (i, j)
    for odd in range(1, TORUS_DEVICES - 1, 2)
    for i, j in ((odd, odd + 1), (odd + 1, odd))
]

VMEM = pl.BlockSpec(memory_space=pltpu.VMEM)
SMEM = pl.BlockSpec(memory_space=pltpu.SMEM)


def send(block, pairs):
    return lax.ppermute(block, "seq", pairs)


def after(value, *events):
    return lax.optimization_barrier((value,) + events)[0]


def device_index():
    return lax.axis_index("seq").astype(jnp.int32).reshape(1)


def block_of(device, place, other):
    r2, r1, low, high = place
    owner = device ^ other
    parity = owner & 1
    dx = r1 + parity * (r2 - r1)
    dy = r2 + parity * (r1 - r2)
    return owner ^ (16 * high + 8 * low + 4 * dy + 2 * dx)


def edge_swaps(block, parity):
    width = DILATION_STEP
    last = block.shape[1] - width
    inside = lax.dynamic_slice_in_dim(block, (1 - parity) * last, width, axis=1)
    outside = lax.dynamic_slice_in_dim(block, parity * last, width, axis=1)
    return send(inside, CORE), send(outside, OUTER)


def fold(inputs, outputs):
    def kernel(*refs):
        sources, targets = refs[: len(inputs)], refs[len(inputs) :]
        for target, (dtype, _, _, pieces) in zip(targets, outputs):
            for added, (m, m_count), (n, n_count), to_m, to_n in pieces:
                total = None
                for source in added:
                    value = sources[source][m : m + m_count, n : n + n_count]
                    value = value.astype(jnp.float32)
                    total = value if total is None else total + value
                target[to_m : to_m + m_count, to_n : to_n + n_count] = total.astype(dtype)

    tail = inputs[0].shape[2:]
    return pl.pallas_call(
        kernel,
        out_shape=[
            jax.ShapeDtypeStruct((m, n) + tail, dtype) for dtype, m, n, pieces in outputs
        ],
        in_specs=[VMEM] * len(inputs),
        out_specs=[VMEM] * len(outputs),
        compiler_params=pltpu.CompilerParams(vmem_limit_bytes=12 << 20),
        name="fold",
    )(*inputs)


def assemble(inputs, outputs):
    def kernel(*refs):
        sources, targets = refs[: len(inputs)], refs[len(inputs) :]
        for target, (_, _, pieces) in zip(targets, outputs):
            for source, start, count, to_m, to_n in pieces:
                n = sources[source].shape[1]
                target[to_m : to_m + count, to_n : to_n + n] = sources[source][
                    start : start + count
                ]

    tail = inputs[0].shape[2:]
    return pl.pallas_call(
        kernel,
        out_shape=[
            jax.ShapeDtypeStruct((m, n) + tail, inputs[0].dtype) for m, n, pieces in outputs
        ],
        in_specs=[VMEM] * len(inputs),
        out_specs=[VMEM] * len(outputs),
        compiler_params=pltpu.CompilerParams(vmem_limit_bytes=8 << 20),
        name="assemble",
    )(*inputs)


GELU_SCALE = math.sqrt(2.0 / math.pi)
GELU_CUBE = 0.044715


def edge_places(device, bins):
    parity = device & 1
    beyond = bins + DILATION_STEP
    core_at = pl.multiple_of((1 - parity) * beyond, DILATION_STEP)
    outer_at = pl.multiple_of(parity * beyond, DILATION_STEP)
    return core_at, outer_at


def prepare_kernel(
    index_ref,
    features_ref,
    cotangent_ref,
    gain_ref,
    *refs,
):
    device = index_ref[0]
    batch, bins, channels = features_ref.shape
    core_refs, outer_refs = refs[:batch], refs[batch : 2 * batch]
    taps_ref, project_ref, active, turned = refs[2 * batch :]
    rows = taps_ref.shape[4]
    width = DILATION_STEP
    gain = gain_ref[...]
    core_at, outer_at = edge_places(device, bins)

    def activate(x):
        x = x.astype(jnp.float32)
        inverse = lax.rsqrt(jnp.sum(x * x, axis=-1, keepdims=True) * (1.0 / channels) + eps)
        v = x * inverse * gain
        t = jnp.tanh(GELU_SCALE * (v + GELU_CUBE * (v * v * v)))
        return (0.5 * v * (1.0 + t)).astype(jnp.bfloat16)

    for b in range(batch):

        def some_rows(i, carry):
            at = pl.multiple_of(i * width, width)
            rows_of = activate(features_ref[b, pl.ds(at, width), :])
            active[b, pl.ds(pl.multiple_of(at + width, width), width), :] = rows_of
            return carry

        lax.fori_loop(0, bins // width, some_rows, 0)
        active[b, pl.ds(core_at, width), :] = activate(core_refs[b][0])
        active[b, pl.ds(outer_at, width), :] = activate(outer_refs[b][0])

    def blocks(order):
        for other in BITS:
            for at, where in enumerate(order):
                start = pl.multiple_of(block_of(device, where, other) * rows, 16)
                yield other, at, turned[pl.ds(start, rows), :]

    for tap in range(KERNEL_TAPS):
        for b in range(batch):
            turned[:, b * bins : (b + 1) * bins] = active[
                b, tap * DILATION_STEP : tap * DILATION_STEP + bins, :
            ].T
        for other, at, block in blocks(TAP_ORDERS[tap]):
            taps_ref[other, at // HALF, tap, at % HALF] = block
    turned[...] = cotangent_ref[...].T
    for other, at, block in blocks(PROJECT_ORDER):
        project_ref[other, at // HALF, 0, at % HALF] = block


def prepare(features, edges_of, cotangent, gain, rows):
    tokens, channels = cotangent.shape
    batch, bins, _ = features.shape
    shape = lambda count: jax.ShapeDtypeStruct((2, 2, count, HALF, rows, tokens), cotangent.dtype)
    return pl.pallas_call(
        prepare_kernel,
        out_shape=[shape(KERNEL_TAPS), shape(1)],
        in_specs=[SMEM] + [VMEM] * (3 + 2 * batch),
        out_specs=[VMEM] * 2,
        scratch_shapes=[
            pltpu.VMEM((batch, bins + 2 * DILATION_STEP, channels), jnp.bfloat16),
            pltpu.VMEM((channels, tokens), jnp.bfloat16),
        ],
        compiler_params=pltpu.CompilerParams(vmem_limit_bytes=16 << 20),
        name="prepare",
    )(device_index(), features, cotangent, gain.reshape(1, channels), *edges_of)


def place_products(device, parts, turned, orders, placed):
    rows, inner = parts[0].shape[2:]
    for other in BITS:
        for which in BITS:
            part = parts[2 * other + which]
            for matrix, right in enumerate(turned):
                product = jnp.dot(
                    part[matrix].reshape(HALF * rows, inner),
                    right,
                    preferred_element_type=jnp.float32,
                )
                for at in range(HALF):
                    block = block_of(device, orders[matrix][which * HALF + at], other)
                    target = pl.ds(pl.multiple_of(block * rows, 16), rows)
                    rows_of = product[at * rows : (at + 1) * rows]
                    if matrix == 0:
                        placed[target, :] = rows_of
                    else:
                        placed[target, :] += rows_of


def project_back_kernel(index_ref, hidden_ref, features_ref, *refs):
    parts, out_ref, placed = refs[:4], refs[4], refs[5]
    place_products(index_ref[0], parts, [hidden_ref[...].T], [PROJECT_ORDER], placed)
    out_ref[...] = (features_ref[...].astype(jnp.float32) + placed[...].T).astype(jnp.bfloat16)


def project_back(hidden, features, parts):
    return pl.pallas_call(
        project_back_kernel,
        out_shape=jax.ShapeDtypeStruct(features.shape, features.dtype),
        in_specs=[SMEM] + [VMEM] * 6,
        out_specs=VMEM,
        scratch_shapes=[pltpu.VMEM(features.shape[::-1], jnp.float32)],
        compiler_params=pltpu.CompilerParams(vmem_limit_bytes=16 << 20),
        name="project_back",
    )(device_index(), hidden, features, *parts)


def grad_active_kernel(index_ref, grad_ref, core_ref, outer_ref, *refs):
    parts, (out_ref, padded_ref, placed) = refs[:4], refs[4:]
    batch, padded_bins, _ = padded_ref.shape
    bins = padded_bins - 2 * DILATION_STEP
    core_at, outer_at = edge_places(index_ref[0], bins)
    for b in range(batch):
        padded_ref[b, DILATION_STEP : DILATION_STEP + bins] = grad_ref[b * bins : (b + 1) * bins]
        padded_ref[b, pl.ds(core_at, DILATION_STEP), :] = core_ref[b]
        padded_ref[b, pl.ds(outer_at, DILATION_STEP), :] = outer_ref[b]
    turned = []
    for tap in range(KERNEL_TAPS):
        shift = (KERNEL_TAPS - 1 - tap) * DILATION_STEP
        turned.append(
            jnp.concatenate([padded_ref[b, shift : shift + bins] for b in range(batch)], axis=0).T
        )
    place_products(index_ref[0], parts, turned, TAP_ORDERS, placed)
    out_ref[...] = placed[...].T


def grad_of_active(grad, edges_of, parts):
    tokens, inner = grad.shape
    batch = edges_of[0].shape[0]
    channels = 2 * BLOCKS * parts[0].shape[2]
    return pl.pallas_call(
        grad_active_kernel,
        out_shape=jax.ShapeDtypeStruct((tokens, channels), jnp.float32),
        in_specs=[SMEM] + [VMEM] * 7,
        out_specs=VMEM,
        scratch_shapes=[
            pltpu.VMEM((batch, tokens // batch + 2 * DILATION_STEP, inner), grad.dtype),
            pltpu.VMEM((channels, tokens), jnp.float32),
        ],
        compiler_params=pltpu.CompilerParams(vmem_limit_bytes=24 << 20),
        name="grad_active",
    )(device_index(), grad, *edges_of, *parts)


def rows_dot(left, right):
    return jnp.einsum("mnrt,ti->mnri", left, right, preferred_element_type=jnp.float32)


def contract(left, right):
    return jnp.einsum(
        "ct,ci->ti",
        left.reshape(-1, left.shape[-1]),
        right.reshape(-1, right.shape[-1]),
        preferred_element_type=jnp.float32,
    )


def body_torus(features, cotangent, dilated_kernel_weight, project_weight, outer_gain, inner_gain):
    batch, bin_count, channels = features.shape
    inner = project_weight.shape[1]
    rows = project_weight.shape[0]
    tokens = batch * bin_count
    factor = 1.0 / math.sqrt(tokens * TORUS_DEVICES)
    as_bf16 = lambda value: value.astype(jnp.bfloat16)
    as_f32 = lambda value: value.astype(jnp.float32)

    taps = jnp.moveaxis(dilated_kernel_weight, 1, 0)[:, None]
    pair = taps[:2]
    rest = jnp.concatenate([taps[2:], project_weight[None, None]])
    pair_in, rest_in = send(pair, Z_FAR), send(rest, FIRST)
    pair, last, proj = assemble(
        (pair, pair_in, rest, rest_in),
        (
            (2, 2, ((0, 0, 2, 0, 0), (1, 0, 2, 0, 1))),
            (1, 2, ((2, 0, 1, 0, 0), (3, 0, 1, 0, 1))),
            (1, 2, ((2, 1, 1, 0, 0), (3, 1, 1, 0, 1))),
        ),
    )
    pair_in, last_in, proj_b = send(pair, Z_NEAR), send(last, Z_FAR), send(proj, SECOND)
    parity = lax.axis_index("seq") & 1
    feature_edges = list(
        zip(*(edge_swaps(after(features, pair)[b : b + 1], parity) for b in range(batch)))
    )
    feature_edges = [array for side in feature_edges for array in side]
    grow = lambda m, n, a: (m, 2 * n, ((a, 0, m, 0, 0), (a + 1, 0, m, 0, n)))
    pair_in = after(pair_in, proj_b, *feature_edges)
    pair, last = assemble((pair, pair_in, last, last_in), (grow(2, 2, 0), grow(1, 2, 2)))
    pair_in, last_in, proj_in = send(pair, FIRST), send(last, Z_NEAR), send(proj, Z_FAR)
    (proj_a,) = assemble((proj, proj_in), (grow(1, 2, 0),))
    (near,) = assemble(
        after((pair, pair_in, last, last_in), proj_a),
        ((3, 8, ((0, 0, 2, 0, 0), (1, 0, 2, 0, 4), (2, 0, 1, 2, 0), (3, 0, 1, 2, 4))),),
    )
    far, near_other = send(near, SECOND), send(near, CORE)
    proj_in, proj_b_in = send(proj_a, Z_NEAR), send(proj_b, Z_FAR)
    flat_cotangent = cotangent.reshape(tokens, channels)
    act, act_p = prepare(
        after(features, near), feature_edges, flat_cotangent, outer_gain, rows
    )
    (proj_b,) = assemble((proj_b, after(proj_b_in, act)), (grow(1, 2, 0),))
    proj_b_in = send(proj_b, Z_NEAR)
    conv_output = contract(act[0, 0], after(near, proj_b))
    (proj_a,) = assemble((proj_a, after(proj_in, conv_output)), (grow(1, 4, 0),))
    proj_a_other = send(proj_a, CORE)
    (proj_b,) = assemble((proj_b, after(proj_b_in, proj_a)), (grow(1, 4, 0),))
    proj_b_other = send(proj_b, CORE)
    far = after(far, proj_b_other, proj_a_other)
    far_other = send(far, CORE)
    conv_output = conv_output + contract(act[1, 0], after(near_other, far))
    proj_a_late, proj_b_late = after((proj_a, proj_b), far)
    grad_hidden = (
        contract(act_p[0, 0], proj_a_late)
        + contract(act_p[1, 0], proj_a_other)
        + contract(act_p[0, 1], proj_b_late)
        + contract(act_p[1, 1], proj_b_other)
    )
    conv_output = conv_output + contract(act[0, 1], far) + contract(act[1, 1], far_other)
    hidden32, pull_inner = jax.vjp(act_norm, conv_output, inner_gain)
    hidden = as_bf16(hidden32)
    grad_conv, grad_gain_inner = pull_inner(grad_hidden)
    grad_conv = as_bf16(grad_conv)

    give = as_bf16(rows_dot(act[1, 1], grad_conv))
    recv_far = send(give, CORE)
    give = as_bf16(rows_dot(act[1, 0], after(grad_conv, give)))
    recv_near = send(give, CORE)
    give = as_bf16(
        rows_dot(act_p[1].reshape(2, HALF, rows, tokens), after(hidden, give))
    )
    recv_p = send(give, CORE)
    grad_edges = edge_swaps(after(grad_conv, give).reshape(batch, bin_count, inner), parity)
    message = as_bf16(rows_dot(act[0, 1], after(grad_conv, give)) + as_f32(recv_far))
    recv = send(message, SECOND)
    grad_p = after(hidden, message)
    split = lambda which: act_p[0, which].reshape(2, HALF // 2, rows, tokens)
    parts_of = lambda array, which: array[which].reshape(2, HALF // 2, rows, inner)
    message_b = as_bf16(
        rows_dot(split(1)[1:], grad_p) + as_f32(parts_of(recv_p, 1)[1:])
    )
    recv_b = send(message_b, Z_NEAR)
    message_a = as_bf16(
        rows_dot(split(0)[1:], grad_p) + as_f32(parts_of(recv_p, 0)[1:])
    )
    grad_p = after(hidden, message_a, message_b)
    kept_b = rows_dot(split(1)[:1], grad_p) + as_f32(parts_of(recv_p, 1)[:1])
    kept_a = rows_dot(split(0)[:1], grad_p) + as_f32(parts_of(recv_p, 0)[:1])
    kept = rows_dot(act[0, 0], after(grad_conv, kept_a, kept_b)) + as_f32(recv_near)

    flat = features.reshape(tokens, channels)
    grad_active = grad_of_active(
        after(grad_conv, kept), grad_edges, (near, far, near_other, far_other)
    )
    f32, bf16 = jnp.float32, jnp.bfloat16
    unused, pull_outer = jax.vjp(act_norm, as_f32(after(features, grad_active)), outer_gain)
    grad_branch, grad_gain_outer = pull_outer(grad_active.reshape(features.shape))
    grad_features = as_bf16(as_f32(cotangent) + grad_branch)
    part = inner // TORUS_DEVICES
    gains = factor * jnp.concatenate(
        [grad_gain_outer.reshape(-1, rows), grad_gain_inner.reshape(-1, part)], axis=1
    )
    recv_b = after(recv_b, grad_features, gains)
    message_b, kept_b = fold(
        (kept_b, recv_b),
        (
            (bf16, 1, 2, (((0, 1), (0, 1), (2, 2), 0, 0),)),
            (f32, 1, 2, (((0, 1), (0, 1), (0, 2), 0, 0),)),
        ),
    )
    recv_b = send(message_b, Z_FAR)
    recv_a = send(after(message_a, message_b), Z_NEAR)
    gains = after(gains, message_b)
    gains = gains + send(gains, CORE)
    gains = gains + send(gains, Z_NEAR)

    recv_a = after(recv_a, gains)
    message, message_l, message_a, message_p, kept, kept_l, kept_a, kept_b = fold(
        (kept, recv, kept_a, recv_a, kept_b, recv_b),
        (
            (bf16, 2, 4, (((0, 1), (0, 2), (4, 4), 0, 0),)),
            (bf16, 1, 4, (((0, 1), (2, 1), (4, 4), 0, 0),)),
            (bf16, 1, 2, (((2, 3), (0, 1), (2, 2), 0, 0),)),
            (bf16, 1, 2, (((4, 5), (0, 1), (0, 2), 0, 0),)),
            (f32, 2, 4, (((0, 1), (0, 2), (0, 4), 0, 0),)),
            (f32, 1, 4, (((0, 1), (2, 1), (0, 4), 0, 0),)),
            (f32, 1, 2, (((2, 3), (0, 1), (0, 2), 0, 0),)),
            (f32, 1, 2, (((4, 5), (0, 1), (0, 2), 0, 0),)),
        ),
    )
    recv, recv_l, recv_a = send(message, FIRST), send(message_l, Z_NEAR), send(message_a, Z_FAR)
    gains = after(gains, message)
    gains = gains + send(gains, Z_FAR)
    block_out = project_back(
        after(hidden, message), flat, (proj_a, proj_b, proj_a_other, proj_b_other)
    ).reshape(features.shape)
    gains = after(gains, block_out)

    recv = after(recv, gains)
    message, message_l, kept, kept_l, kept_p = fold(
        (kept, recv, kept_l, recv_l, kept_a, recv_a),
        (
            (bf16, 2, 2, (((0, 1), (0, 2), (2, 2), 0, 0),)),
            (bf16, 1, 2, (((2, 3), (0, 1), (2, 2), 0, 0),)),
            (f32, 2, 2, (((0, 1), (0, 2), (0, 2), 0, 0),)),
            (f32, 1, 2, (((2, 3), (0, 1), (0, 2), 0, 0),)),
            (f32, 1, 2, (((4, 5), (0, 1), (0, 2), 0, 0),)),
        ),
    )
    message_p = after(message_p, message)
    recv, recv_l, recv_p = send(message, Z_NEAR), send(message_l, Z_FAR), send(message_p, SECOND)
    gains = after(gains, message)
    gains = gains + send(gains, links(lambda i: i ^ 2))
    gains = gains + send(gains, links(lambda i: i ^ 4))

    recv = after(recv, gains)
    message, message_r, kept, kept_r = fold(
        (kept, recv, kept_l, recv_l, kept_p, recv_p),
        (
            (bf16, 2, 1, (((0, 1), (0, 2), (1, 1), 0, 0),)),
            (bf16, 2, 1, (((2, 3), (0, 1), (1, 1), 0, 0), ((4, 5), (0, 1), (1, 1), 1, 0))),
            (f32, 2, 1, (((0, 1), (0, 2), (0, 1), 0, 0),)),
            (f32, 2, 1, (((2, 3), (0, 1), (0, 1), 0, 0), ((4, 5), (0, 1), (0, 1), 1, 0))),
        ),
    )
    recv, recv_r = send(message, Z_FAR), send(message_r, FIRST)

    sums = kept + as_f32(recv)
    sums_r = kept_r + as_f32(recv_r)
    grad_project = sums_r[1, 0] * factor
    grad_dilated = jnp.stack([sums[0, 0], sums[1, 0], sums_r[0, 0]], axis=1) * factor

    device = lax.axis_index("seq")
    mine = lax.dynamic_index_in_dim(gains, device, axis=0, keepdims=False)
    grad_outer_gain, grad_inner_gain = mine[:rows], mine[rows:]
    return (block_out, grad_features, grad_dilated, grad_project, grad_outer_gain, grad_inner_gain)


def body(*operands):
    if lax.axis_size("seq") == TORUS_DEVICES:
        return body_torus(*operands)
    return body_any(*operands)


def solution(mesh):
    return jax.shard_map(
        body,
        mesh=mesh,
        in_specs=(
            P("groups", "seq", None),
            P("groups", "seq", None),
            P("seq", None, None),
            P("seq", None),
            P(),
            P(),
        ),
        out_specs=(
            P("groups", "seq", None),
            P("groups", "seq", None),
            P(("groups", "seq"), None, None),
            P(("groups", "seq"), None),
            P(("groups", "seq")),
            P(("groups", "seq")),
        ),
        check_vma=False,
    )
```
